32 devices in a mesh: tower: 4 (over y, x), member: 8 (over z, core).
Axes of the slice: x: 2, y: 2, z: 4, core: 2. Of those that a mesh axis runs over, the one named last changes fastest.
Arguments:
- bag_ids: int32 [8, 8, 4, 512], P('tower', 'member'), may hold values from 0 to 511
- touch_ids: int32 [8, 8, 128], P('tower', 'member'), may hold values from 0 to 511, as said below
- elapsed: int32 [8, 8, 128], P('tower', 'member'), may hold values from 0 to 39
- tables: float32 [8, 8, 512, 64], P('tower', 'member'), may hold values from -3 to 3
- accumulator: float32 [8, 8, 512], P('tower', 'member'), may hold values from 0.001 to 0.1
- first_weight: float32 [512, 8, 1024], P(None, 'tower'), may hold values from -0.25 to 0.25
- second_weight: float32 [1024, 8, 256], P(None, 'tower'), may hold values from -0.1875 to 0.1875
- lift_weight: float32 [2048, 128], replicated, may hold values from -0.5 to 0.5
- press_weight: float32 [2048, 128], replicated, may hold values from -0.125 to 0.125
- head_weight: float32 [2048], replicated, may hold values from -0.125 to 0.125
- labels: int32 [8, 64], P('member'), may hold values 0 or 1
Outputs:
- new_tables: float32 [8, 8, 512, 64], P('tower', 'member')
- new_accumulator: float32 [8, 8, 512], P('tower', 'member')
- grad_first: float32 [512, 8, 1024], P('member', 'tower')
- grad_second: float32 [1024, 8, 256], P('member', 'tower')
- grad_lift: float32 [2048, 128], P(('tower', 'member'))
- grad_press: float32 [2048, 128], P(('tower', 'member'))
- logits: float32 [8, 64], P('member', 'tower')
The draws below stay inside these ranges and needn't reach their ends.
Inputs may be any that keep to these rules, and one draw needn't show every extreme that they name: `touch_ids`: distinct within each table.
All inputs are finite; a program needn't handle non-finite values. No bound on the sum of `labels` on one device may be relied on, other than what follows from the above.
Results may differ from the reference program's by a relative error of at most 0.0003.
Values sent between devices are 32-bit elements; how exact they have to be, the bound alone decides.
A program may use at most 128 MiB of HBM per device.

```python
import math
import jax
import jax.numpy as jnp
import numpy as np
from jax import lax

W = 64
HID = 1024
TOUT = 256
RANK = 128
BAG = 4
ROWS = 512
TOUCH = 128
TOWERS = 8
TTAB = 8
FIN = 512
CROSS = 2048
SAMP = 64
SAMPLES = 512
N_MEMBER = 8


def draw_touch_ids(key, part):
    keys = jax.random.split(jax.random.fold_in(key, 7), TOWERS * TTAB)

    def one_table(table_key):
        perm_key, shift_key = jax.random.split(table_key)
        others = (jax.random.permutation(perm_key, ROWS - 2)[:TOUCH - 2] + 1).astype(jnp.int32)
        listed = jnp.concatenate([jnp.full((1,), ROWS - 1, jnp.int32), jnp.zeros((1,), jnp.int32), others])
        shift = jax.random.randint(shift_key, (), 0, TOUCH)
        return jnp.roll(listed, shift)
    return jax.vmap(one_table)(keys).reshape(TOWERS, TTAB, TOUCH).astype(jnp.int32)


def place_ends(values, own_key, least, top_value):
    spot = [jax.random.randint(jax.random.fold_in(own_key, axis), (), 0, length) for axis, length in enumerate(values.shape)]
    longest = values.shape.index(max(values.shape))
    neighbour = spot[:longest] + [(spot[longest] + 1) % values.shape[longest]] + spot[longest + 1:]
    return values.at[tuple(spot)].set(least).at[tuple(neighbour)].set(top_value)


def level_of(key, extent, pieces, smallest, top_value):
    level = 1.0
    for dim, blocks in pieces:
        draws = jax.random.uniform(jax.random.fold_in(jax.random.fold_in(key, 6), dim), (blocks,), jnp.float32, smallest / len(pieces), top_value / len(pieces))
        level = level * jnp.repeat(jnp.exp(draws), extent[dim] // blocks).reshape((-1,) + (1,) * (len(extent) - 1 - dim))
    return level


def cumulative_ranks(count, slope):
    loads = [(1 << 20) // math.isqrt(standing ** slope) + 1 for standing in range(1, count + 1)]
    width = 1 + sum(loads) // (1 << 30)
    return np.cumsum(np.array([max(1, weight // width) for weight in loads]))


def ranked_ids(stream_key, shape, number_of, lean):
    table = cumulative_ranks(number_of, lean)
    pick = jax.random.randint(jax.random.fold_in(stream_key, 1), shape, 0, int(table[number_of - 1]))
    grade = jnp.searchsorted(jnp.asarray(table, jnp.int32), pick, side="right")
    return jax.random.permutation(jax.random.fold_in(stream_key, 2), number_of)[grade].astype(jnp.int32)


def normal_values(key, dims, deviation, most, cuts=(), kind=jnp.bfloat16):
    array = jax.random.normal(key, dims, jnp.float32) * deviation
    if len(cuts) > 0:
        array = level_of(key, dims, cuts, -0.22, 0.18) * array
    return jnp.clip(array, min=-most, max=most).astype(kind)


def setup_inputs(seed: int = 0) -> dict:
    key_of = jax.random.split(jax.random.key(seed), 12)
    bag_ids = place_ends(ranked_ids(key_of[0], (TOWERS, TTAB, BAG, SAMPLES), ROWS, 2), jax.random.fold_in(key_of[0], 3), 0, ROWS - 1).astype(jnp.int32)
    touch_ids = draw_touch_ids(jax.random.fold_in(key_of[11], 71), 0)
    elapsed = place_ends(jax.random.randint(key_of[2], (TOWERS, TTAB, TOUCH), 0, 40), jax.random.fold_in(key_of[2], 1), 0, 39).astype(jnp.int32)
    tables = normal_values(key_of[3], (TOWERS, TTAB, ROWS, W), 0.5, 3.0, ((0, 4), (1, 8)), jnp.float32)
    accumulator = jnp.clip(jnp.exp(math.log(0.1) - 4.6051702 * jax.random.uniform(key_of[4], (TOWERS, TTAB, ROWS), jnp.float32) ** level_of(key_of[4], (TOWERS, TTAB, ROWS), ((0, 4), (1, 8)), -0.2, 0.2)), 0.001, 0.1)
    first_weight = normal_values(key_of[5], (FIN, TOWERS, HID), FIN ** -0.5, 0.25, ((1, 4),), jnp.float32)
    second_weight = normal_values(key_of[6], (HID, TOWERS, TOUT), HID ** -0.5, 0.1875, ((1, 4),), jnp.float32)
    lift_weight = normal_values(key_of[7], (CROSS, RANK), RANK ** -0.5, 0.5, (), jnp.float32)
    press_weight = normal_values(key_of[8], (CROSS, RANK), CROSS ** -0.5, 0.125, (), jnp.float32)
    head_weight = normal_values(key_of[9], (CROSS,), CROSS ** -0.5, 0.125, (), jnp.float32)
    labels = place_ends((jax.random.randint(key_of[10], (N_MEMBER, SAMP), 0, 2) < 1).astype(jnp.int32), jax.random.fold_in(key_of[10], 1), 0, 1)
    return dict(bag_ids=bag_ids, touch_ids=touch_ids, elapsed=elapsed, tables=tables, accumulator=accumulator, first_weight=first_weight, second_weight=second_weight, lift_weight=lift_weight, press_weight=press_weight, head_weight=head_weight, labels=labels)


PRECISE = lax.Precision.HIGHEST
DECAY_RATE = 0.98
LEARN_RATE = 1.0
EPSILON = 1e-08

def decay_factors(touch_ids, elapsed, table_rows):
    rates = jnp.exp(elapsed.astype(jnp.float32) * math.log(DECAY_RATE))
    matches = touch_ids[..., None] == jnp.arange(table_rows, dtype=jnp.int32)
    hits = lax.optimization_barrier(jnp.sum(matches.astype(jnp.float32), axis=-2))
    chosen = lax.optimization_barrier(jnp.sum(jnp.where(matches, rates[..., None], jnp.float32(0.0)), axis=-2))
    return jnp.where(hits > 0.0, chosen, jnp.float32(1.0))

def pool_table(decayed_table, bag_table):
    return lax.optimization_barrier(jnp.sum(decayed_table[bag_table], axis=0))

def reference(bag_ids, touch_ids, elapsed, tables, accumulator, first_weight, second_weight, lift_weight, press_weight, head_weight, labels):
    factors = lax.map(lambda inputs: decay_factors(inputs[0], inputs[1], ROWS), (touch_ids, elapsed))
    decayed = tables * factors[..., None]

    def forward(decayed_tables, weight_one, weight_two, lift, press):
        pooled = lax.map(lambda inputs: jax.vmap(pool_table)(inputs[0], inputs[1]), (decayed_tables, bag_ids))
        features = jnp.transpose(pooled, (2, 0, 1, 3)).reshape(SAMPLES, TOWERS, FIN)
        hidden = jnp.einsum('sti,ith->sth', features, weight_one, precision=PRECISE)
        tower_out = jnp.einsum('sth,hto->sto', jax.nn.silu(hidden), weight_two, precision=PRECISE)
        start_rows = tower_out.reshape(SAMPLES, CROSS)
        projected = jnp.dot(start_rows, press, precision=PRECISE)
        scaling = jnp.dot(projected, lift.T, precision=PRECISE)
        crossed = start_rows * scaling + start_rows
        return jnp.dot(crossed, head_weight, precision=PRECISE)
    logit_values, pullback = jax.vjp(forward, decayed, first_weight, second_weight, lift_weight, press_weight)
    errors = jax.nn.sigmoid(logit_values) - labels.reshape(SAMPLES).astype(jnp.float32)
    grad_tables, grad_one, grad_two, grad_lift, grad_press = pullback(errors)
    mean_square = lax.optimization_barrier(jnp.mean(grad_tables * grad_tables, axis=-1))
    new_accumulator = accumulator + mean_square
    new_tables = decayed - LEARN_RATE * grad_tables / (jnp.sqrt(new_accumulator)[..., None] + EPSILON)
    return (new_tables, new_accumulator, grad_one, grad_two, grad_lift, grad_press, logit_values.reshape(N_MEMBER, SAMP))
```

```python
import functools
import math

import jax
import jax.numpy as jnp
from jax import lax
from jax.experimental import pallas as pl
from jax.experimental.pallas import tpu as pltpu
from jax.sharding import PartitionSpec as P

MESH = pl.DeviceIdType.MESH
DECAY_RATE = 0.98
LEARN_RATE = 1.0
EPSILON = 1e-08
F32 = jnp.float32
BF16 = jnp.bfloat16
NN = (((1,), (0,)), ((), ()))
NT = (((1,), (1,)), ((), ()))


def split(x):
    hi = x.astype(BF16)
    return hi, (x - hi.astype(F32)).astype(BF16)


def dot1(a, b, dims=NN):
    return lax.dot_general(a, b, dims, preferred_element_type=F32)


def few3(a, b, dims=NN):
    (ah, al), (bh, bl) = a, b
    both = dot1(jnp.concatenate([ah, al], axis=0), bh, dims)
    m = ah.shape[0]
    return both[:m] + (both[m:] + dot1(ah, bl, dims))


def deep3(a, b, dims=NN):
    (ah, al), (bh, bl) = a, b
    return dot1(
        jnp.concatenate([ah, al, ah], axis=1),
        jnp.concatenate([bh, bh, bl], axis=dims[0][1][0]),
        dims,
    )


def sigmoid(x):
    return 1.0 / (1.0 + jnp.exp(-x))


def main_kernel(
    dims,
    bag_ref,
    touch_ref,
    elapsed_ref,
    tables_ref,
    first_hbm,
    second_hbm,
    lift_hbm,
    press_hbm,
    head_ref,
    label_ref,
    logits_out,
    decayed_out,
    gt_out,
    gf_out,
    gsec_out,
    glp_out,
    stage,
    w1h,
    w1l,
    w2f,
    w2h,
    w2l,
    lift,
    press,
    mixh,
    mixl,
    cols,
    counts_ref,
    decayed,
    pool,
    feats,
    tout_send,
    tout_recv,
    stats,
    rs_buf,
    gath,
    act,
    acth,
    actl,
    pth,
    ptl,
    gf,
    gf_in,
    gsec,
    gsec_in,
    gpool,
    gpool_in,
    glp,
    glp_in,
    gt,
    logits,
    load_sem,
    store_sem,
    crit_send,
    crit_recv,
    bulk_send,
    bulk_recv,
    relay_send,
    mate_sem,
    rs_send,
    rs_recv,
    to_send,
    to_recv,
    gm_send,
    gm_recv,
    gt_send,
    gt_recv,
    back_send,
    back_recv,
):
    n, nt = dims
    me = lax.axis_index("member")
    tpos = lax.axis_index("tower")
    towers, bags, total = bag_ref.shape
    width, rows = tables_ref.shape[1:]
    touches = touch_ref.shape[2]
    hid, outs = w2h.shape[1:]
    fin = w1h.shape[1]
    rank = lift.shape[1]
    flat = towers * outs
    chips = n // 2
    own = total // n
    half = own * chips
    piece = own // nt
    chunk = min(256, half)
    tile = min(256, hid)
    pair_hid = 2 * (hid // n)
    block_hid = hid // n
    pair_flat = flat // chips
    chip, core = me // 2, lax.rem(me, 2)
    mate = me + 1 - 2 * core

    loads = []

    def load(source, target):
        loads.append(pltpu.make_async_copy(source, target, load_sem.at[len(loads)]))
        loads[-1].start()

    for t in range(towers):
        load(first_hbm.at[:, t, :], stage.at[t, :fin])
    for t in range(towers):
        load(second_hbm.at[:, t, :], w2f.at[t])
    load(lift_hbm.at[pl.ds(tpos * flat, flat)], lift)
    load(press_hbm.at[pl.ds(tpos * flat, flat)], press)

    barrier = pltpu.get_barrier_semaphore()
    for d in range(1, n):
        pl.semaphore_signal(
            barrier, inc=1, device_id={"member": lax.rem(me + d, n)}, device_id_type=MESH
        )
    for d in range(1, nt):
        pl.semaphore_signal(
            barrier, inc=1, device_id={"tower": lax.rem(tpos + d, nt)}, device_id_type=MESH
        )

    stores = []

    def store(source, target):
        stores.append(pltpu.make_async_copy(source, target, store_sem.at[len(stores)]))
        stores[-1].start()

    def slice_at(index):
        return pl.ds(pl.multiple_of(index * own, own), own)

    stack = [bag_ref[t].astype(F32) for t in range(towers)]
    stack.append(jnp.zeros((128 - towers * bags, total), F32))
    cols[...] = jnp.concatenate(stack, axis=0).T
    stack = []
    for t in range(towers):
        stack.append(touch_ref[t].astype(F32))
        stack.append(jnp.exp(elapsed_ref[t].astype(F32) * math.log(DECAY_RATE)))
    stack.append(jnp.zeros((128 - 2 * towers, touches), F32))
    owed = jnp.concatenate(stack, axis=0).T
    pairs = []
    place = lax.broadcasted_iota(jnp.int32, (touches, rows), 1).astype(F32)
    for t in range(towers):
        ids, rates = owed[:, 2 * t : 2 * t + 1], owed[:, 2 * t + 1 : 2 * t + 2]
        chosen = jnp.sum(jnp.where(place == ids, rates, 0.0), axis=0, keepdims=True)
        value = tables_ref[t] * jnp.where(chosen > 0.0, chosen, 1.0)
        decayed[t] = value
        pairs.append(jnp.concatenate(split(value), axis=0))
    place = lax.broadcasted_iota(jnp.int32, (own, rows), 1).astype(F32)
    for parity in (1 - core, core):
        pooled = []
        for t in range(towers):
            pieces = []
            for c in range(chips):
                span = slice_at(2 * c + parity)
                counts = jnp.zeros((own, rows), F32)
                for b in range(bags):
                    k = t * bags + b
                    counts = counts + jnp.where(place == cols[span, k : k + 1], 1.0, 0.0)
                pieces.append(counts.astype(BF16))
            counts = jnp.concatenate(pieces, axis=0)
            counts_ref[t, parity] = counts
            both = dot1(counts, pairs[t], NT)
            pooled.append(both[:, :width] + both[:, width:])
        pool[parity] = jnp.concatenate(pooled, axis=1)
    feats[me] = pool[core]

    pl.semaphore_wait(barrier, n - 1 + nt - 1)

    def crit_copy(i, k):
        there = lax.rem(chip + i, chips)
        return pltpu.make_async_remote_copy(
            src_ref=pool.at[k, slice_at(there)],
            dst_ref=feats.at[me, slice_at(there)],
            send_sem=crit_send.at[i, k],
            recv_sem=crit_recv.at[i, core],
            device_id={"member": 2 * there + k},
            device_id_type=MESH,
        )

    def crit_wait(i, k):
        there = lax.rem(chip + chips - i, chips)
        pltpu.make_async_remote_copy(
            src_ref=feats.at[2 * there + k, slice_at(chip)],
            dst_ref=feats.at[2 * there + k, slice_at(chip)],
            send_sem=crit_send.at[i, k],
            recv_sem=crit_recv.at[i, k],
            device_id={"member": 2 * there + k},
            device_id_type=MESH,
        ).wait_recv()

    def bulk_copy(i, k, j):
        there = lax.rem(chip + i, chips)
        at = slice_at(lax.rem(there + j, chips))
        return pltpu.make_async_remote_copy(
            src_ref=pool.at[k, at],
            dst_ref=feats.at[me, at],
            send_sem=bulk_send.at[i, k, j],
            recv_sem=bulk_recv.at[i, core, j],
            device_id={"member": 2 * there + k},
            device_id_type=MESH,
        )

    def bulk_wait(i):
        there = lax.rem(chip + chips - i, chips)
        for k in range(2):
            for j in range(1, chips):
                at = slice_at(lax.rem(chip + j, chips))
                pltpu.make_async_remote_copy(
                    src_ref=feats.at[2 * there + k, at],
                    dst_ref=feats.at[2 * there + k, at],
                    send_sem=bulk_send.at[i, k, j],
                    recv_sem=bulk_recv.at[i, k, j],
                    device_id={"member": 2 * there + k},
                    device_id_type=MESH,
                ).wait_recv()

    def mate_copy():
        return pltpu.make_async_remote_copy(
            src_ref=pool.at[1 - core],
            dst_ref=feats.at[me],
            send_sem=mate_sem.at[0],
            recv_sem=mate_sem.at[1],
            device_id={"member": mate},
            device_id_type=MESH,
        )

    order = sorted(range(1, chips), key=lambda i: -min(i, chips - i))

    def bulk_each(i, act_on):
        def both():
            for k in range(2):
                for j in range(1, chips):
                    act_on(bulk_copy(i, k, j))

        if i == 1:
            pl.when(chip != chips - 1)(both)
        elif i == chips - 1:
            pl.when(chip != 0)(both)
        else:
            both()

    def relay_each(act_on):
        def over(source, target, i):
            for k in range(2):
                for j in range(1, chips):
                    at = slice_at((target + j) % chips)
                    act_on(
                        pltpu.make_async_remote_copy(
                            src_ref=feats.at[2 * source + k, at],
                            dst_ref=feats.at[2 * source + k, at],
                            send_sem=relay_send.at[k, j],
                            recv_sem=bulk_recv.at[i, k, j],
                            device_id={"member": 2 * target + core},
                            device_id_type=MESH,
                        )
                    )

        pl.when(chip == chips - 2)(lambda: over(0, chips - 1, chips - 1))
        pl.when(chip == 1)(lambda: over(chips - 1, 0, 1))

    for i in order:
        for k in range(2):
            crit_copy(i, k).start()
    mate_copy().start()
    store(decayed, decayed_out)

    for copy in loads[:towers]:
        copy.wait()
    for t in range(towers):

        @pl.loop(0, fin // 64)
        def _(i):
            span = pl.ds(pl.multiple_of(i * 64, 64), 64)
            w1h[t, span, :], w1l[t, span, :] = split(stage[t, span, :])

    for i in order:
        bulk_each(i, lambda copy: copy.start())

    for copy in loads[towers:]:
        copy.wait()
    for t in range(towers):

        @pl.loop(0, hid // 128)
        def _(i):
            span = pl.ds(pl.multiple_of(i * 128, 128), 128)
            w2h[t, span, :], w2l[t, span, :] = split(w2f[t, span, :])

    head = head_ref[:, pl.ds(pl.multiple_of(tpos * flat, flat), flat)]
    mixh[...], mixl[...] = split(jnp.concatenate([lift[...].T * head, press[...].T], axis=0))

    mate_copy().wait_recv()
    for i in order:
        for k in range(2):
            crit_wait(i, k)
    flat_out = []
    for t in range(towers):
        part = slice(t * width, (t + 1) * width)
        x = jnp.concatenate([feats[b, slice_at(chip), part] for b in range(n)], axis=1)
        h = few3(split(x), (w1h[t], w1l[t]))
        flat_out.append(few3(split(h * sigmoid(h)), (w2h[t], w2l[t])))
    flat_out = jnp.concatenate(flat_out, axis=1)
    stats[:, : 2 * rank] = few3(split(flat_out), (mixh[...], mixl[...]), NT)
    stats[:, 2 * rank :] = jnp.broadcast_to(
        jnp.sum(flat_out * head, axis=1, keepdims=True), (own, rank)
    )

    def tower_copy(d):
        other = lax.rem(tpos + d, nt)
        return pltpu.make_async_remote_copy(
            src_ref=stats.at[pl.ds(pl.multiple_of(other * piece, piece), piece)],
            dst_ref=rs_buf.at[tpos],
            send_sem=rs_send.at[d],
            recv_sem=rs_recv.at[d],
            device_id={"tower": other},
            device_id_type=MESH,
        )

    for d in range(1, nt):
        tower_copy(d).start()

    for c in range(chips):
        tout_send[c] = flat_out[:, c * pair_flat : (c + 1) * pair_flat]
    tout_recv[chip] = tout_send[chip]

    def tout_copy(i):
        there = lax.rem(chip + i, chips)
        return pltpu.make_async_remote_copy(
            src_ref=tout_send.at[there],
            dst_ref=tout_recv.at[chip],
            send_sem=to_send.at[i],
            recv_sem=to_recv.at[i],
            device_id={"member": 2 * there + core},
            device_id_type=MESH,
        )

    def member_copy(i):
        return pltpu.make_async_remote_copy(
            src_ref=gath.at[chip, tpos],
            dst_ref=gath.at[chip, tpos],
            send_sem=gm_send.at[i],
            recv_sem=gm_recv.at[i],
            device_id={"member": 2 * lax.rem(chip + i, chips) + core},
            device_id_type=MESH,
        )

    def column_copy(d):
        return pltpu.make_async_remote_copy(
            src_ref=gath.at[:, tpos],
            dst_ref=gath.at[:, tpos],
            send_sem=gt_send.at[d],
            recv_sem=gt_recv.at[d],
            device_id={"tower": lax.rem(tpos + d, nt)},
            device_id_type=MESH,
        )

    for d in range(1, nt):
        tower_copy(d).wait_recv()
    summed = stats[pl.ds(pl.multiple_of(tpos * piece, piece), piece), :]
    for d in range(1, nt):
        summed = summed + rs_buf[lax.rem(tpos + d, nt)]
    scaled, projected = summed[:, :rank], summed[:, rank : 2 * rank]
    logit = jnp.sum(projected * scaled, axis=1, keepdims=True) + summed[:, 2 * rank :]
    logits[...] = logit
    seat = lax.broadcasted_iota(jnp.int32, (piece, own), 1)
    wanted = lax.broadcasted_iota(jnp.int32, (piece, own), 0) + tpos * piece
    clicks = jnp.where(seat == wanted, label_ref[...].astype(F32), 0.0)
    error = sigmoid(logit) - jnp.sum(clicks, axis=1, keepdims=True)
    gath[chip, tpos, :, :rank] = error * projected
    gath[chip, tpos, :, rank : 2 * rank] = error * scaled
    gath[chip, tpos, :, 2 * rank :] = error
    for i in order:
        member_copy(i).start()
    store(logits, logits_out)

    via = sorted({2, chips - 2})
    for i in via:
        bulk_wait(i)
    relay_each(lambda copy: copy.start())
    for i in order:
        tout_copy(i).start()
    for i in order:
        if i not in via:
            bulk_wait(i)

    start = pl.multiple_of(chip * pair_hid, pair_hid)

    def hidden_chunk(t, c):
        part = slice(t * width, (t + 1) * width)
        span = slice(c * chunk, (c + 1) * chunk)
        x = split(jnp.concatenate([feats[b, span, part] for b in range(n)], axis=1))
        for k in range(hid // tile):
            lanes = slice(k * tile, (k + 1) * tile)
            h = deep3(x, (w1h[t, :, lanes], w1l[t, :, lanes]))
            sig = sigmoid(h)
            a = h * sig
            act[span, lanes] = a
            stage[t, span, lanes] = sig + a * (1.0 - sig)
        both = jnp.concatenate([feats[2 * chip + k, span, part] for k in range(2)], axis=1)
        pth[t, :, span], ptl[t, :, span] = split(both.T)
        acth[t, :, span], actl[t, :, span] = split(act[span, pl.ds(start, pair_hid)].T)

    for t in range(towers):
        for c in range(half // chunk):
            hidden_chunk(t, c)
        if t == 0:
            for i in order:
                member_copy(i).wait_recv()
            for d in range(1, nt):
                column_copy(d).start()

    for i in order:
        tout_copy(i).wait_recv()
    for d in range(1, nt):
        column_copy(d).wait_recv()

    def back_copy(slot, source, target):
        return pltpu.make_async_remote_copy(
            src_ref=source,
            dst_ref=target,
            send_sem=back_send.at[slot],
            recv_sem=back_recv.at[slot],
            device_id={"member": mate},
            device_id_type=MESH,
        )

    def rows_of(which, size):
        return pl.ds(pl.multiple_of(which * size, size), size)

    def back_copies(t):
        return [
            back_copy(3 * t, gpool.at[t, rows_of(1 - core, width)], gpool_in.at[t]),
            back_copy(3 * t + 1, gf.at[t, rows_of(1 - core, width)], gf_in.at[t]),
            back_copy(3 * t + 2, gsec.at[t, rows_of(1 - core, block_hid)], gsec_in.at[t]),
        ]

    def lift_copy():
        return back_copy(3 * towers, glp.at[rows_of(1 - core, pair_flat // 2)], glp_in)

    def put(ref, index, value, fresh):
        if fresh:
            ref[index] = value
        else:
            ref[index] += value

    pair_rows = pl.ds(pl.multiple_of(chip * 2 * width, 2 * width), 2 * width)
    for t in range(towers):
        part = slice(t * outs, (t + 1) * outs)
        for c in range(half // chunk):
            span = slice(c * chunk, (c + 1) * chunk)
            here = slice(c * (chunk // own), (c + 1) * (chunk // own))
            block = gath[here].reshape(chunk, 3 * rank)
            go = split(
                block[:, 2 * rank : 2 * rank + 1] * head[:, part]
                + deep3(split(block[:, : 2 * rank]), (mixh[:, part], mixl[:, part]))
            )
            grad_pooled = jnp.zeros((2 * width, chunk), F32)
            for k in range(hid // tile):
                lanes = slice(k * tile, (k + 1) * tile)
                grad_act = deep3(go, (w2h[t, lanes, :], w2l[t, lanes, :]), NT)
                grad_hidden = split(grad_act * stage[t, span, lanes])
                value = deep3((pth[t, :, span], ptl[t, :, span]), grad_hidden)
                put(gf, (t, slice(None), lanes), value, c == 0)
                first = (w1h[t, pair_rows, lanes], w1l[t, pair_rows, lanes])
                grad_pooled = grad_pooled + deep3(first, grad_hidden, NT)
            gpool[t, :, span] = grad_pooled
            put(gsec, (t,), deep3((acth[t, :, span], actl[t, :, span]), go), c == 0)
        for copy in back_copies(t):
            copy.start()

    outputs = jnp.concatenate([tout_recv[c] for c in range(chips)], axis=0)
    block = gath[...].reshape(half, 3 * rank)
    value = deep3(split(outputs.T), split(block[:, : 2 * rank]))
    seat = lax.broadcasted_iota(jnp.int32, (pair_flat, flat), 1)
    wanted = lax.broadcasted_iota(jnp.int32, (pair_flat, flat), 0) + chip * pair_flat
    weights = jnp.sum(jnp.where(seat == wanted, head, 0.0), axis=1, keepdims=True)
    glp[:, :rank] = weights * value[:, :rank]
    glp[:, rank:] = value[:, rank:]
    lift_copy().start()

    for t in range(towers):
        from_mate = back_copies(t)
        mine = jnp.concatenate(split(gpool[t, rows_of(core, width), :]), axis=0)
        both = dot1(mine, counts_ref[t, core])
        from_mate[0].wait_recv()
        theirs = jnp.concatenate(split(gpool_in[t]), axis=0)
        both = both + dot1(theirs, counts_ref[t, 1 - core])
        gt[t] = both[:width] + both[width:]
        store(gt.at[t], gt_out.at[t])
        from_mate[1].wait_recv()
        gf_in[t] += gf[t, rows_of(core, width), :]
        store(gf_in.at[t], gf_out.at[t])
        from_mate[2].wait_recv()
        gsec_in[t] += gsec[t, rows_of(core, block_hid), :]
        store(gsec_in.at[t], gsec_out.at[t])
    lift_copy().wait_recv()
    glp_in[...] += glp[rows_of(core, pair_flat // 2), :]
    store(glp_in, glp_out)

    for i in order:
        for k in range(2):
            crit_copy(i, k).wait_send()
        bulk_each(i, lambda copy: copy.wait_send())
        tout_copy(i).wait_send()
        member_copy(i).wait_send()
    relay_each(lambda copy: copy.wait_send())
    mate_copy().wait_send()
    for d in range(1, nt):
        tower_copy(d).wait_send()
        column_copy(d).wait_send()
    for t in range(towers):
        for copy in back_copies(t):
            copy.wait_send()
    lift_copy().wait_send()
    for copy in stores:
        copy.wait()


def final_kernel(
    logits_ref,
    decayed_ref,
    gt_ref,
    gf_ref,
    gsec_ref,
    glp_ref,
    acc_ref,
    new_tables_ref,
    new_acc_ref,
    grad_first_ref,
    grad_second_ref,
    grad_lift_ref,
    grad_press_ref,
    logits_out_ref,
):
    rank = logits_ref.shape[1]
    for t in range(gt_ref.shape[0]):
        grad_second_ref[:, t, :] = gsec_ref[t]
        grad_first_ref[:, t, :] = gf_ref[t]
        g = gt_ref[t]
        value = acc_ref[t] + jnp.mean(g * g, axis=0, keepdims=True)
        new_acc_ref[t] = value
        new_tables_ref[t] = decayed_ref[t] - LEARN_RATE * g / (jnp.sqrt(value) + EPSILON)
    grad_lift_ref[...] = glp_ref[:, :rank]
    grad_press_ref[...] = glp_ref[:, rank:]
    piece = logits_ref.shape[0]
    place = lax.broadcasted_iota(jnp.int32, (piece, piece), 1)
    wanted = lax.broadcasted_iota(jnp.int32, (piece, piece), 0)
    values = jnp.where(place == wanted, logits_ref[:, :1], 0.0)
    logits_out_ref[...] = jnp.sum(values, axis=0, keepdims=True)


def per_device(n, nt, *args):
    bag_ids, touch_ids, elapsed, tables, accumulator, first, second, lift, press, head, labels = args
    towers, _, bags, total = bag_ids.shape
    rows, width = tables.shape[2:]
    fin, _, hid = first.shape
    outs = second.shape[2]
    rank = lift.shape[1]
    flat = towers * outs
    chips = n // 2
    own = total // n
    half = own * chips
    piece = own // nt
    block_hid = hid // n
    pair_flat = flat // chips
    lanes = towers * width
    vmem = pl.BlockSpec(memory_space=pltpu.VMEM)
    anys = pl.BlockSpec(memory_space=pl.ANY)
    sem = pltpu.SemaphoreType.DMA
    shape = jax.ShapeDtypeStruct
    between = pl.pallas_call(
        functools.partial(main_kernel, (n, nt)),
        out_shape=(
            shape((piece, rank), F32),
            shape((towers, width, rows), F32),
            shape((towers, width, rows), F32),
            shape((towers, width, hid), F32),
            shape((towers, block_hid, outs), F32),
            shape((pair_flat // 2, 2 * rank), F32),
        ),
        in_specs=[vmem] * 4 + [anys] * 4 + [vmem] * 2,
        out_specs=[anys] * 6,
        scratch_shapes=[
            pltpu.VMEM((towers, max(half, fin), hid), F32),
            pltpu.VMEM((towers, fin, hid), BF16),
            pltpu.VMEM((towers, fin, hid), BF16),
            pltpu.VMEM((towers, hid, outs), F32),
            pltpu.VMEM((towers, hid, outs), BF16),
            pltpu.VMEM((towers, hid, outs), BF16),
            pltpu.VMEM((flat, rank), F32),
            pltpu.VMEM((flat, rank), F32),
            pltpu.VMEM((2 * rank, flat), BF16),
            pltpu.VMEM((2 * rank, flat), BF16),
            pltpu.VMEM((total, 128), F32),
            pltpu.VMEM((towers, 2, half, rows), BF16),
            pltpu.VMEM((towers, width, rows), F32),
            pltpu.VMEM((2, half, lanes), F32),
            pltpu.VMEM((n, half, lanes), F32),
            pltpu.VMEM((chips, own, pair_flat), F32),
            pltpu.VMEM((chips, own, pair_flat), F32),
            pltpu.VMEM((own, 3 * rank), F32),
            pltpu.VMEM((nt, piece, 3 * rank), F32),
            pltpu.VMEM((chips, nt, piece, 3 * rank), F32),
            pltpu.VMEM((half, hid), F32),
            pltpu.VMEM((towers, 2 * block_hid, half), BF16),
            pltpu.VMEM((towers, 2 * block_hid, half), BF16),
            pltpu.VMEM((towers, 2 * width, half), BF16),
            pltpu.VMEM((towers, 2 * width, half), BF16),
            pltpu.VMEM((towers, 2 * width, hid), F32),
            pltpu.VMEM((towers, width, hid), F32),
            pltpu.VMEM((towers, 2 * block_hid, outs), F32),
            pltpu.VMEM((towers, block_hid, outs), F32),
            pltpu.VMEM((towers, 2 * width, half), F32),
            pltpu.VMEM((towers, width, half), F32),
            pltpu.VMEM((pair_flat, 2 * rank), F32),
            pltpu.VMEM((pair_flat // 2, 2 * rank), F32),
            pltpu.VMEM((towers, width, rows), F32),
            pltpu.VMEM((piece, rank), F32),
            sem((2 * towers + 2,)),
            sem((3 + 3 * towers,)),
            sem((chips, 2)),
            sem((chips, 2)),
            sem((chips, 2, chips)),
            sem((chips, 2, chips)),
            sem((2, chips)),
            sem((2,)),
            sem((nt,)),
            sem((nt,)),
            sem((chips,)),
            sem((chips,)),
            sem((chips,)),
            sem((chips,)),
            sem((nt,)),
            sem((nt,)),
            sem((3 * towers + 1,)),
            sem((3 * towers + 1,)),
        ],
        compiler_params=pltpu.CompilerParams(
            collective_id=0, has_side_effects=True, vmem_limit_bytes=67043328
        ),
    )(
        bag_ids[:, 0],
        touch_ids,
        elapsed,
        jnp.transpose(tables[:, 0], (0, 2, 1)),
        first,
        second,
        lift,
        press,
        head[None, :],
        labels,
    )
    out = pl.pallas_call(
        final_kernel,
        out_shape=(
            shape((towers, width, rows), F32),
            shape((towers, 1, rows), F32),
            shape((width, towers, hid), F32),
            shape((block_hid, towers, outs), F32),
            shape((flat // n, rank), F32),
            shape((flat // n, rank), F32),
            shape((1, piece), F32),
        ),
        in_specs=[vmem] * 7,
        out_specs=[vmem] * 7,
    )(*between, accumulator)
    new_tables, new_acc, grad_first, grad_second, grad_lift, grad_press, logits = out
    return (
        jnp.transpose(new_tables, (0, 2, 1))[:, None],
        new_acc,
        grad_first,
        grad_second,
        grad_lift,
        grad_press,
        logits,
    )


def solution(mesh):
    placed = (
        P("tower", "member", None, None),
        P("tower", "member", None),
        P("tower", "member", None),
        P("tower", "member", None, None),
        P("tower", "member", None),
        P(None, "tower", None),
        P(None, "tower", None),
        P(),
        P(),
        P(),
        P("member", None),
    )
    return jax.shard_map(
        functools.partial(per_device, mesh.shape["member"], mesh.shape["tower"]),
        mesh=mesh,
        in_specs=placed,
        out_specs=(
            P("tower", "member", None, None),
            P("tower", "member", None),
            P("member", "tower", None),
            P("member", "tower", None),
            P(("tower", "member"), None),
            P(("tower", "member"), None),
            P("member", "tower"),
        ),
        check_vma=False,
    )
```

```python
import functools
import math

import jax
import jax.numpy as jnp
from jax import lax
from jax.experimental import pallas as pl
from jax.experimental.pallas import tpu as pltpu
from jax.sharding import PartitionSpec as P

MESH = pl.DeviceIdType.MESH
DECAY_RATE = 0.98
LEARN_RATE = 1.0
EPSILON = 1e-08
F32 = jnp.float32
BF16 = jnp.bfloat16
NN = (((1,), (0,)), ((), ()))
NT = (((1,), (1,)), ((), ()))


def split(x):
    hi = x.astype(BF16)
    return hi, (x - hi.astype(F32)).astype(BF16)


def dot1(a, b, dims=NN):
    return lax.dot_general(a, b, dims, preferred_element_type=F32)


def few3(a, b, dims=NN):
    (ah, al), (bh, bl) = a, b
    both = dot1(jnp.concatenate([ah, al], axis=0), bh, dims)
    m = ah.shape[0]
    return both[:m] + (both[m:] + dot1(ah, bl, dims))


def deep3(a, b, dims=NN):
    (ah, al), (bh, bl) = a, b
    return dot1(
        jnp.concatenate([ah, al, ah], axis=1),
        jnp.concatenate([bh, bh, bl], axis=dims[0][1][0]),
        dims,
    )


def sigmoid(x):
    return 1.0 / (1.0 + jnp.exp(-x))


def main_kernel(
    dims,
    bag_ref,
    touch_ref,
    elapsed_ref,
    tables_ref,
    first_hbm,
    second_hbm,
    lift_hbm,
    press_hbm,
    head_ref,
    label_ref,
    logits_out,
    decayed_out,
    gt_out,
    gf_out,
    gsec_out,
    glp_out,
    stage,
    w1h,
    w1l,
    w2f,
    w2h,
    w2l,
    lift,
    press,
    mixh,
    mixl,
    cols,
    counts_ref,
    decayed,
    pool,
    feats,
    tout_send,
    tout_recv,
    stats,
    rs_buf,
    gath,
    act,
    acth,
    actl,
    pth,
    ptl,
    gf,
    gf_in,
    gsec,
    gsec_in,
    gpool,
    gpool_in,
    glp,
    glp_in,
    gt,
    logits,
    load_sem,
    store_sem,
    own_send,
    mate_send,
    ag_send,
    ag_recv,
    rs_send,
    rs_recv,
    to_send,
    to_recv,
    gm_send,
    gm_recv,
    gt_send,
    gt_recv,
    back_send,
    back_recv,
):
    n, nt = dims
    me = lax.axis_index("member")
    tpos = lax.axis_index("tower")
    towers, bags, total = bag_ref.shape
    width, rows = tables_ref.shape[1:]
    touches = touch_ref.shape[2]
    hid, outs = w2h.shape[1:]
    fin = w1h.shape[1]
    rank = lift.shape[1]
    flat = towers * outs
    chips = n // 2
    own = total // n
    half = own * chips
    piece = own // nt
    chunk = min(256, half)
    tile = min(256, hid)
    pair_hid = 2 * (hid // n)
    block_hid = hid // n
    pair_flat = flat // chips
    chip, core = me // 2, lax.rem(me, 2)
    mate = me + 1 - 2 * core

    loads = []

    def load(source, target):
        loads.append(pltpu.make_async_copy(source, target, load_sem.at[len(loads)]))
        loads[-1].start()

    for t in range(towers):
        load(first_hbm.at[:, t, :], stage.at[t, :fin])
    for t in range(towers):
        load(second_hbm.at[:, t, :], w2f.at[t])
    load(lift_hbm.at[pl.ds(tpos * flat, flat)], lift)
    load(press_hbm.at[pl.ds(tpos * flat, flat)], press)

    barrier = pltpu.get_barrier_semaphore()
    for d in range(1, n):
        pl.semaphore_signal(
            barrier, inc=1, device_id={"member": lax.rem(me + d, n)}, device_id_type=MESH
        )
    for d in range(1, nt):
        pl.semaphore_signal(
            barrier, inc=1, device_id={"tower": lax.rem(tpos + d, nt)}, device_id_type=MESH
        )

    stores = []

    def store(source, target):
        stores.append(pltpu.make_async_copy(source, target, store_sem.at[len(stores)]))
        stores[-1].start()

    def slice_at(index):
        return pl.ds(pl.multiple_of(index * own, own), own)

    stack = [bag_ref[t].astype(F32) for t in range(towers)]
    stack.append(jnp.zeros((128 - towers * bags, total), F32))
    cols[...] = jnp.concatenate(stack, axis=0).T
    stack = []
    for t in range(towers):
        stack.append(touch_ref[t].astype(F32))
        stack.append(jnp.exp(elapsed_ref[t].astype(F32) * math.log(DECAY_RATE)))
    stack.append(jnp.zeros((128 - 2 * towers, touches), F32))
    owed = jnp.concatenate(stack, axis=0).T
    pairs = []
    place = lax.broadcasted_iota(jnp.int32, (touches, rows), 1).astype(F32)
    for t in range(towers):
        ids, rates = owed[:, 2 * t : 2 * t + 1], owed[:, 2 * t + 1 : 2 * t + 2]
        chosen = jnp.sum(jnp.where(place == ids, rates, 0.0), axis=0, keepdims=True)
        value = tables_ref[t] * jnp.where(chosen > 0.0, chosen, 1.0)
        decayed[t] = value
        pairs.append(jnp.concatenate(split(value), axis=0))
    def own_copy(sign, k, s):
        at = slice_at(s)
        return pltpu.make_async_remote_copy(
            src_ref=pool.at[k, at],
            dst_ref=feats.at[me, at],
            send_sem=own_send.at[(1 - sign) // 2, k, s],
            recv_sem=ag_recv.at[me, s],
            device_id={"member": 2 * (chip + sign) + k},
            device_id_type=MESH,
        )

    def mate_copy(s):
        at = slice_at(s)
        return pltpu.make_async_remote_copy(
            src_ref=pool.at[1 - core, at],
            dst_ref=feats.at[me, at],
            send_sem=mate_send.at[s],
            recv_sem=ag_recv.at[me, s],
            device_id={"member": mate},
            device_id_type=MESH,
        )

    def block_copy(sign, block, s):
        at = slice_at(s)
        return pltpu.make_async_remote_copy(
            src_ref=feats.at[block, at],
            dst_ref=feats.at[block, at],
            send_sem=ag_send.at[(1 - sign) // 2, block, s],
            recv_sem=ag_recv.at[block, s],
            device_id={"member": 2 * (chip + sign) + core},
            device_id_type=MESH,
        )

    def goes_on(sign):
        return chip < chips - 1 if sign > 0 else chip > 0

    def present(sign, d):
        return chip >= d if sign > 0 else chip + d < chips

    def ahead(sign, act_on):
        @pl.loop(0, chips - 1 - chip if sign > 0 else chip)
        def _(i):
            act_on(chips - 1 - i if sign > 0 else i)

    def behind(sign, act_on):
        @pl.loop(0, chip if sign > 0 else chips - 1 - chip)
        def _(i):
            act_on(chip - 1 - i if sign > 0 else chip + 1 + i)

    def pass_on(sign, d, over):
        def one(s):
            for k in range(2):
                block = 2 * (chip - sign * d) + k
                block_copy(sign, block, s).wait_recv()

                @pl.when(goes_on(sign))
                def _():
                    block_copy(sign, block, s).start()

        @pl.when(present(sign, d))
        def _():
            over(one)

    def own_rest(sign, over):
        def one(s):
            for k in range(2):
                own_copy(sign, k, s).start()

        @pl.when(goes_on(sign))
        def _():
            over(one)

    order = sorted(range(1, chips), key=lambda i: -min(i, chips - i))
    place = lax.broadcasted_iota(jnp.int32, (2 * own, rows), 1).astype(F32)
    for i in order + [0]:
        there = lax.rem(chip + i, chips)
        span = pl.ds(pl.multiple_of(there * 2 * own, 2 * own), 2 * own)
        pooled = []
        for t in range(towers):
            counts = jnp.zeros((2 * own, rows), F32)
            for b in range(bags):
                k = t * bags + b
                counts = counts + jnp.where(place == cols[span, k : k + 1], 1.0, 0.0)
            counts = counts.astype(BF16)
            for k in range(2):
                counts_ref[t, k, slice_at(there), :] = counts[k * own : (k + 1) * own]
            both = dot1(counts, pairs[t], NT)
            pooled.append(both[:, :width] + both[:, width:])
        pooled = jnp.concatenate(pooled, axis=1)
        for k in range(2):
            pool[k, slice_at(there), :] = pooled[k * own : (k + 1) * own]
        if i == order[0]:
            pl.semaphore_wait(barrier, n - 1 + nt - 1)
        if i:

            @pl.when(there > chip)
            def _():
                for k in range(2):
                    own_copy(1, k, there).start()

            @pl.when(there < chip)
            def _():
                for k in range(2):
                    own_copy(-1, k, there).start()

        mate_copy(there).start()
    feats[me] = pool[core]

    for copy in loads[:towers]:
        copy.wait()
    for t in range(towers):

        @pl.loop(0, fin // 64)
        def _(i):
            span = pl.ds(pl.multiple_of(i * 64, 64), 64)
            w1h[t, span, :], w1l[t, span, :] = split(stage[t, span, :])

    for sign in (1, -1):
        pass_on(sign, 1, functools.partial(ahead, sign))
    for sign in (1, -1):
        own_rest(sign, lambda act_on: act_on(chip))

    for copy in loads[towers:]:
        copy.wait()
    for t in range(towers):

        @pl.loop(0, hid // 128)
        def _(i):
            span = pl.ds(pl.multiple_of(i * 128, 128), 128)
            w2h[t, span, :], w2l[t, span, :] = split(w2f[t, span, :])

    head = head_ref[:, pl.ds(pl.multiple_of(tpos * flat, flat), flat)]
    mixh[...], mixl[...] = split(jnp.concatenate([lift[...].T * head, press[...].T], axis=0))

    for d in range(2, chips):
        for sign in (1, -1):
            pass_on(sign, d, functools.partial(ahead, sign))
    for sign in (1, -1):
        own_rest(sign, functools.partial(behind, sign))
    store(decayed, decayed_out)

    def mate_arrives(s):
        block_copy(1, mate, s).wait_recv()

    mate_arrives(chip)
    for d in range(1, chips):
        for sign in (1, -1):
            pass_on(sign, d, lambda act_on: act_on(chip))
    flat_out = []
    for t in range(towers):
        part = slice(t * width, (t + 1) * width)
        x = jnp.concatenate([feats[b, slice_at(chip), part] for b in range(n)], axis=1)
        h = few3(split(x), (w1h[t], w1l[t]))
        flat_out.append(few3(split(h * sigmoid(h)), (w2h[t], w2l[t])))
    flat_out = jnp.concatenate(flat_out, axis=1)
    stats[:, : 2 * rank] = few3(split(flat_out), (mixh[...], mixl[...]), NT)
    stats[:, 2 * rank :] = jnp.broadcast_to(
        jnp.sum(flat_out * head, axis=1, keepdims=True), (own, rank)
    )

    def tower_copy(d):
        other = lax.rem(tpos + d, nt)
        return pltpu.make_async_remote_copy(
            src_ref=stats.at[pl.ds(pl.multiple_of(other * piece, piece), piece)],
            dst_ref=rs_buf.at[tpos],
            send_sem=rs_send.at[d],
            recv_sem=rs_recv.at[d],
            device_id={"tower": other},
            device_id_type=MESH,
        )

    for d in range(1, nt):
        tower_copy(d).start()

    for c in range(chips):
        tout_send[c] = flat_out[:, c * pair_flat : (c + 1) * pair_flat]
    tout_recv[chip] = tout_send[chip]

    def tout_copy(i):
        there = lax.rem(chip + i, chips)
        return pltpu.make_async_remote_copy(
            src_ref=tout_send.at[there],
            dst_ref=tout_recv.at[chip],
            send_sem=to_send.at[i],
            recv_sem=to_recv.at[i],
            device_id={"member": 2 * there + core},
            device_id_type=MESH,
        )

    def member_copy(i):
        return pltpu.make_async_remote_copy(
            src_ref=gath.at[chip, tpos],
            dst_ref=gath.at[chip, tpos],
            send_sem=gm_send.at[i],
            recv_sem=gm_recv.at[i],
            device_id={"member": 2 * lax.rem(chip + i, chips) + core},
            device_id_type=MESH,
        )

    def column_copy(d):
        return pltpu.make_async_remote_copy(
            src_ref=gath.at[:, tpos],
            dst_ref=gath.at[:, tpos],
            send_sem=gt_send.at[d],
            recv_sem=gt_recv.at[d],
            device_id={"tower": lax.rem(tpos + d, nt)},
            device_id_type=MESH,
        )

    for sign in (1, -1):
        pass_on(sign, 1, functools.partial(behind, sign))
    for sign in (1, -1):
        behind(sign, mate_arrives)
    per = 4
    together = per * width

    def hidden_group(t, c, g):
        part = slice(t * width, (t + 1) * width)
        span = slice(c * chunk, (c + 1) * chunk)
        x = jnp.concatenate([feats[per * g + k, span, part] for k in range(per)], axis=1)
        x = split(x)
        ins = pl.ds(pl.multiple_of(g * together, together), together)
        for k in range(hid // tile):
            lanes = slice(k * tile, (k + 1) * tile)
            yield lanes, deep3(x, (w1h[t, ins, lanes], w1l[t, ins, lanes]))

    near = chip // 2
    for t in range(towers):
        for c in range(half // chunk):
            span = slice(c * chunk, (c + 1) * chunk)
            for lanes, value in hidden_group(t, c, near):
                stage[t, span, lanes] = value

    for d in range(1, nt):
        tower_copy(d).wait_recv()
    summed = stats[pl.ds(pl.multiple_of(tpos * piece, piece), piece), :]
    for d in range(1, nt):
        summed = summed + rs_buf[lax.rem(tpos + d, nt)]
    scaled, projected = summed[:, :rank], summed[:, rank : 2 * rank]
    logit = jnp.sum(projected * scaled, axis=1, keepdims=True) + summed[:, 2 * rank :]
    logits[...] = logit
    seat = lax.broadcasted_iota(jnp.int32, (piece, own), 1)
    wanted = lax.broadcasted_iota(jnp.int32, (piece, own), 0) + tpos * piece
    clicks = jnp.where(seat == wanted, label_ref[...].astype(F32), 0.0)
    error = sigmoid(logit) - jnp.sum(clicks, axis=1, keepdims=True)
    gath[chip, tpos, :, :rank] = error * projected
    gath[chip, tpos, :, rank : 2 * rank] = error * scaled
    gath[chip, tpos, :, 2 * rank :] = error
    for i in order:
        member_copy(i).start()
    store(logits, logits_out)

    def far(sign, d, wanted):
        @pl.when(wanted)
        def _():
            pass_on(sign, d, functools.partial(behind, sign))

    for d in range(2, chips):
        for sign in (1, -1):
            far(sign, d, goes_on(sign))
    for i in order:
        tout_copy(i).start()
    for i in order:
        member_copy(i).wait_recv()
    for d in range(1, nt):
        column_copy(d).start()
    for d in range(2, chips):
        for sign in (1, -1):
            far(sign, d, jnp.logical_not(goes_on(sign)))

    start = pl.multiple_of(chip * pair_hid, pair_hid)
    groups = n // per
    for t in range(towers):
        part = slice(t * width, (t + 1) * width)
        for c in range(half // chunk):
            span = slice(c * chunk, (c + 1) * chunk)
            for i in range(1, groups):
                for lanes, value in hidden_group(t, c, lax.rem(near + i, groups)):
                    h = stage[t, span, lanes] + value
                    if i < groups - 1:
                        stage[t, span, lanes] = h
                    else:
                        sig = sigmoid(h)
                        a = h * sig
                        act[span, lanes] = a
                        stage[t, span, lanes] = sig + a * (1.0 - sig)
            both = jnp.concatenate([feats[2 * chip + k, span, part] for k in range(2)], axis=1)
            pth[t, :, span], ptl[t, :, span] = split(both.T)
            acth[t, :, span], actl[t, :, span] = split(act[span, pl.ds(start, pair_hid)].T)

    for i in order:
        tout_copy(i).wait_recv()
    for d in range(1, nt):
        column_copy(d).wait_recv()

    def back_copy(slot, source, target):
        return pltpu.make_async_remote_copy(
            src_ref=source,
            dst_ref=target,
            send_sem=back_send.at[slot],
            recv_sem=back_recv.at[slot],
            device_id={"member": mate},
            device_id_type=MESH,
        )

    def rows_of(which, size):
        return pl.ds(pl.multiple_of(which * size, size), size)

    def back_copies(t):
        return [
            back_copy(3 * t, gpool.at[t, rows_of(1 - core, width)], gpool_in.at[t]),
            back_copy(3 * t + 1, gf.at[t, rows_of(1 - core, width)], gf_in.at[t]),
            back_copy(3 * t + 2, gsec.at[t, rows_of(1 - core, block_hid)], gsec_in.at[t]),
        ]

    def lift_copy():
        return back_copy(3 * towers, glp.at[rows_of(1 - core, pair_flat // 2)], glp_in)

    def put(ref, index, value, fresh):
        if fresh:
            ref[index] = value
        else:
            ref[index] += value

    pair_rows = pl.ds(pl.multiple_of(chip * 2 * width, 2 * width), 2 * width)
    for t in range(towers):
        part = slice(t * outs, (t + 1) * outs)
        for c in range(half // chunk):
            span = slice(c * chunk, (c + 1) * chunk)
            here = slice(c * (chunk // own), (c + 1) * (chunk // own))
            block = gath[here].reshape(chunk, 3 * rank)
            go = split(
                block[:, 2 * rank : 2 * rank + 1] * head[:, part]
                + deep3(split(block[:, : 2 * rank]), (mixh[:, part], mixl[:, part]))
            )
            grad_pooled = jnp.zeros((2 * width, chunk), F32)
            for k in range(hid // tile):
                lanes = slice(k * tile, (k + 1) * tile)
                grad_act = deep3(go, (w2h[t, lanes, :], w2l[t, lanes, :]), NT)
                grad_hidden = split(grad_act * stage[t, span, lanes])
                value = deep3((pth[t, :, span], ptl[t, :, span]), grad_hidden)
                put(gf, (t, slice(None), lanes), value, c == 0)
                first = (w1h[t, pair_rows, lanes], w1l[t, pair_rows, lanes])
                grad_pooled = grad_pooled + deep3(first, grad_hidden, NT)
            gpool[t, :, span] = grad_pooled
            put(gsec, (t,), deep3((acth[t, :, span], actl[t, :, span]), go), c == 0)
        for copy in back_copies(t):
            copy.start()

    outputs = jnp.concatenate([tout_recv[c] for c in range(chips)], axis=0)
    block = gath[...].reshape(half, 3 * rank)
    value = deep3(split(outputs.T), split(block[:, : 2 * rank]))
    seat = lax.broadcasted_iota(jnp.int32, (pair_flat, flat), 1)
    wanted = lax.broadcasted_iota(jnp.int32, (pair_flat, flat), 0) + chip * pair_flat
    weights = jnp.sum(jnp.where(seat == wanted, head, 0.0), axis=1, keepdims=True)
    glp[:, :rank] = weights * value[:, :rank]
    glp[:, rank:] = value[:, rank:]
    lift_copy().start()

    for t in range(towers):
        from_mate = back_copies(t)
        mine = jnp.concatenate(split(gpool[t, rows_of(core, width), :]), axis=0)
        both = dot1(mine, counts_ref[t, core])
        from_mate[0].wait_recv()
        theirs = jnp.concatenate(split(gpool_in[t]), axis=0)
        both = both + dot1(theirs, counts_ref[t, 1 - core])
        gt[t] = both[:width] + both[width:]
        store(gt.at[t], gt_out.at[t])
        from_mate[1].wait_recv()
        gf_in[t] += gf[t, rows_of(core, width), :]
        store(gf_in.at[t], gf_out.at[t])
        from_mate[2].wait_recv()
        gsec_in[t] += gsec[t, rows_of(core, block_hid), :]
        store(gsec_in.at[t], gsec_out.at[t])
    lift_copy().wait_recv()
    glp_in[...] += glp[rows_of(core, pair_flat // 2), :]
    store(glp_in, glp_out)

    for sign in (1, -1):

        @pl.when(goes_on(sign))
        def _():
            for s in range(chips):
                for k in range(2):
                    own_copy(sign, k, s).wait_send()
                for d in range(1, chips):

                    @pl.when(present(sign, d))
                    def _():
                        for k in range(2):
                            block_copy(sign, 2 * (chip - sign * d) + k, s).wait_send()

    for s in range(chips):
        mate_copy(s).wait_send()
    for i in order:
        tout_copy(i).wait_send()
        member_copy(i).wait_send()
    for d in range(1, nt):
        tower_copy(d).wait_send()
        column_copy(d).wait_send()
    for t in range(towers):
        for copy in back_copies(t):
            copy.wait_send()
    lift_copy().wait_send()
    for copy in stores:
        copy.wait()


def final_kernel(
    logits_ref,
    decayed_ref,
    gt_ref,
    gf_ref,
    gsec_ref,
    glp_ref,
    acc_ref,
    new_tables_ref,
    new_acc_ref,
    grad_first_ref,
    grad_second_ref,
    grad_lift_ref,
    grad_press_ref,
    logits_out_ref,
):
    rank = logits_ref.shape[1]
    for t in range(gt_ref.shape[0]):
        grad_second_ref[:, t, :] = gsec_ref[t]
        grad_first_ref[:, t, :] = gf_ref[t]
        g = gt_ref[t]
        value = acc_ref[t] + jnp.mean(g * g, axis=0, keepdims=True)
        new_acc_ref[t] = value
        new_tables_ref[t] = decayed_ref[t] - LEARN_RATE * g / (jnp.sqrt(value) + EPSILON)
    grad_lift_ref[...] = glp_ref[:, :rank]
    grad_press_ref[...] = glp_ref[:, rank:]
    piece = logits_ref.shape[0]
    place = lax.broadcasted_iota(jnp.int32, (piece, piece), 1)
    wanted = lax.broadcasted_iota(jnp.int32, (piece, piece), 0)
    values = jnp.where(place == wanted, logits_ref[:, :1], 0.0)
    logits_out_ref[...] = jnp.sum(values, axis=0, keepdims=True)


def per_device(n, nt, *args):
    bag_ids, touch_ids, elapsed, tables, accumulator, first, second, lift, press, head, labels = args
    towers, _, bags, total = bag_ids.shape
    rows, width = tables.shape[2:]
    fin, _, hid = first.shape
    outs = second.shape[2]
    rank = lift.shape[1]
    flat = towers * outs
    chips = n // 2
    own = total // n
    half = own * chips
    piece = own // nt
    block_hid = hid // n
    pair_flat = flat // chips
    lanes = towers * width
    vmem = pl.BlockSpec(memory_space=pltpu.VMEM)
    anys = pl.BlockSpec(memory_space=pl.ANY)
    sem = pltpu.SemaphoreType.DMA
    shape = jax.ShapeDtypeStruct
    between = pl.pallas_call(
        functools.partial(main_kernel, (n, nt)),
        out_shape=(
            shape((piece, rank), F32),
            shape((towers, width, rows), F32),
            shape((towers, width, rows), F32),
            shape((towers, width, hid), F32),
            shape((towers, block_hid, outs), F32),
            shape((pair_flat // 2, 2 * rank), F32),
        ),
        in_specs=[vmem] * 4 + [anys] * 4 + [vmem] * 2,
        out_specs=[anys] * 6,
        scratch_shapes=[
            pltpu.VMEM((towers, max(half, fin), hid), F32),
            pltpu.VMEM((towers, fin, hid), BF16),
            pltpu.VMEM((towers, fin, hid), BF16),
            pltpu.VMEM((towers, hid, outs), F32),
            pltpu.VMEM((towers, hid, outs), BF16),
            pltpu.VMEM((towers, hid, outs), BF16),
            pltpu.VMEM((flat, rank), F32),
            pltpu.VMEM((flat, rank), F32),
            pltpu.VMEM((2 * rank, flat), BF16),
            pltpu.VMEM((2 * rank, flat), BF16),
            pltpu.VMEM((total, 128), F32),
            pltpu.VMEM((towers, 2, half, rows), BF16),
            pltpu.VMEM((towers, width, rows), F32),
            pltpu.VMEM((2, half, lanes), F32),
            pltpu.VMEM((n, half, lanes), F32),
            pltpu.VMEM((chips, own, pair_flat), F32),
            pltpu.VMEM((chips, own, pair_flat), F32),
            pltpu.VMEM((own, 3 * rank), F32),
            pltpu.VMEM((nt, piece, 3 * rank), F32),
            pltpu.VMEM((chips, nt, piece, 3 * rank), F32),
            pltpu.VMEM((half, hid), F32),
            pltpu.VMEM((towers, 2 * block_hid, half), BF16),
            pltpu.VMEM((towers, 2 * block_hid, half), BF16),
            pltpu.VMEM((towers, 2 * width, half), BF16),
            pltpu.VMEM((towers, 2 * width, half), BF16),
            pltpu.VMEM((towers, 2 * width, hid), F32),
            pltpu.VMEM((towers, width, hid), F32),
            pltpu.VMEM((towers, 2 * block_hid, outs), F32),
            pltpu.VMEM((towers, block_hid, outs), F32),
            pltpu.VMEM((towers, 2 * width, half), F32),
            pltpu.VMEM((towers, width, half), F32),
            pltpu.VMEM((pair_flat, 2 * rank), F32),
            pltpu.VMEM((pair_flat // 2, 2 * rank), F32),
            pltpu.VMEM((towers, width, rows), F32),
            pltpu.VMEM((piece, rank), F32),
            sem((2 * towers + 2,)),
            sem((3 + 3 * towers,)),
            sem((2, 2, chips)),
            sem((chips,)),
            sem((2, n, chips)),
            sem((n, chips)),
            sem((nt,)),
            sem((nt,)),
            sem((chips,)),
            sem((chips,)),
            sem((chips,)),
            sem((chips,)),
            sem((nt,)),
            sem((nt,)),
            sem((3 * towers + 1,)),
            sem((3 * towers + 1,)),
        ],
        compiler_params=pltpu.CompilerParams(
            collective_id=0, has_side_effects=True, vmem_limit_bytes=67043328
        ),
    )(
        bag_ids[:, 0],
        touch_ids,
        elapsed,
        jnp.transpose(tables[:, 0], (0, 2, 1)),
        first,
        second,
        lift,
        press,
        head[None, :],
        labels,
    )
    out = pl.pallas_call(
        final_kernel,
        out_shape=(
            shape((towers, width, rows), F32),
            shape((towers, 1, rows), F32),
            shape((width, towers, hid), F32),
            shape((block_hid, towers, outs), F32),
            shape((flat // n, rank), F32),
            shape((flat // n, rank), F32),
            shape((1, piece), F32),
        ),
        in_specs=[vmem] * 7,
        out_specs=[vmem] * 7,
    )(*between, accumulator)
    new_tables, new_acc, grad_first, grad_second, grad_lift, grad_press, logits = out
    return (
        jnp.transpose(new_tables, (0, 2, 1))[:, None],
        new_acc,
        grad_first,
        grad_second,
        grad_lift,
        grad_press,
        logits,
    )


def solution(mesh):
    placed = (
        P("tower", "member", None, None),
        P("tower", "member", None),
        P("tower", "member", None),
        P("tower", "member", None, None),
        P("tower", "member", None),
        P(None, "tower", None),
        P(None, "tower", None),
        P(),
        P(),
        P(),
        P("member", None),
    )
    return jax.shard_map(
        functools.partial(per_device, mesh.shape["member"], mesh.shape["tower"]),
        mesh=mesh,
        in_specs=placed,
        out_specs=(
            P("tower", "member", None, None),
            P("tower", "member", None),
            P("member", "tower", None),
            P("member", "tower", None),
            P(("tower", "member"), None),
            P(("tower", "member"), None),
            P("member", "tower"),
        ),
        check_vma=False,
    )
```

```python
import functools
import math

import jax
import jax.numpy as jnp
from jax import lax
from jax.experimental import pallas as pl
from jax.experimental.pallas import tpu as pltpu
from jax.sharding import PartitionSpec as P

MESH = pl.DeviceIdType.MESH
DECAY_RATE = 0.98
LEARN_RATE = 1.0
EPSILON = 1e-08
F32 = jnp.float32
BF16 = jnp.bfloat16
NN = (((1,), (0,)), ((), ()))
NT = (((1,), (1,)), ((), ()))


def split(x):
    hi = x.astype(BF16)
    return hi, (x - hi.astype(F32)).astype(BF16)


def dot1(a, b, dims=NN):
    return lax.dot_general(a, b, dims, preferred_element_type=F32)


def few3(a, b, dims=NN):
    (ah, al), (bh, bl) = a, b
    both = dot1(jnp.concatenate([ah, al], axis=0), bh, dims)
    m = ah.shape[0]
    return both[:m] + (both[m:] + dot1(ah, bl, dims))


def deep3(a, b, dims=NN):
    (ah, al), (bh, bl) = a, b
    return dot1(
        jnp.concatenate([ah, al, ah], axis=1),
        jnp.concatenate([bh, bh, bl], axis=dims[0][1][0]),
        dims,
    )


def sigmoid(x):
    return 1.0 / (1.0 + jnp.exp(-x))


def main_kernel(
    dims,
    bag_ref,
    touch_ref,
    elapsed_ref,
    tables_ref,
    first_hbm,
    second_hbm,
    lift_hbm,
    press_hbm,
    head_ref,
    label_ref,
    logits_out,
    decayed_out,
    gt_out,
    gf_out,
    gsec_out,
    glp_out,
    stage,
    w1h,
    w1l,
    w2f,
    w2h,
    w2l,
    lift,
    press,
    mixh,
    mixl,
    cols,
    counts_ref,
    decayed,
    pool,
    feats,
    tout_send,
    tout_recv,
    stats,
    rs_buf,
    gath,
    errs,
    act,
    acth,
    actl,
    pth,
    ptl,
    gf,
    gf_in,
    gsec,
    gsec_in,
    gpool,
    gpool_in,
    glp,
    glp_in,
    gt,
    logits,
    load_sem,
    store_sem,
    own_send,
    mate_send,
    ag_send,
    ag_recv,
    rs_send,
    rs_recv,
    to_send,
    to_recv,
    gm_send,
    gm_recv,
    gt_send,
    gt_recv,
    back_send,
    back_recv,
):
    n, nt = dims
    me = lax.axis_index("member")
    tpos = lax.axis_index("tower")
    towers, bags, total = bag_ref.shape
    width, rows = tables_ref.shape[1:]
    touches = touch_ref.shape[2]
    hid, outs = w2h.shape[1:]
    fin = w1h.shape[1]
    rank = lift.shape[1]
    flat = towers * outs
    chips = n // 2
    own = total // n
    half = own * chips
    piece = own // nt
    chunk = min(256, half)
    tile = min(256, hid)
    pair_hid = 2 * (hid // n)
    block_hid = hid // n
    pair_flat = flat // chips
    chip, core = me // 2, lax.rem(me, 2)
    mate = me + 1 - 2 * core

    loads = []

    def load(source, target):
        loads.append(pltpu.make_async_copy(source, target, load_sem.at[len(loads)]))
        loads[-1].start()

    for t in range(towers):
        load(first_hbm.at[:, t, :], stage.at[t, :fin])
    for t in range(towers):
        load(second_hbm.at[:, t, :], w2f.at[t])
    load(lift_hbm.at[pl.ds(tpos * flat, flat)], lift)
    load(press_hbm.at[pl.ds(tpos * flat, flat)], press)

    barrier = pltpu.get_barrier_semaphore()
    for d in range(1, n):
        pl.semaphore_signal(
            barrier, inc=1, device_id={"member": lax.rem(me + d, n)}, device_id_type=MESH
        )
    for d in range(1, nt):
        pl.semaphore_signal(
            barrier, inc=1, device_id={"tower": lax.rem(tpos + d, nt)}, device_id_type=MESH
        )

    stores = []

    def store(source, target):
        stores.append(pltpu.make_async_copy(source, target, store_sem.at[len(stores)]))
        stores[-1].start()

    def slice_at(index):
        return pl.ds(pl.multiple_of(index * own, own), own)

    stack = [bag_ref[t].astype(F32) for t in range(towers)]
    stack.append(jnp.zeros((128 - towers * bags, total), F32))
    cols[...] = jnp.concatenate(stack, axis=0).T
    stack = []
    for t in range(towers):
        stack.append(touch_ref[t].astype(F32))
        stack.append(jnp.exp(elapsed_ref[t].astype(F32) * math.log(DECAY_RATE)))
    stack.append(jnp.zeros((128 - 2 * towers, touches), F32))
    owed = jnp.concatenate(stack, axis=0).T
    pairs = []
    place = lax.broadcasted_iota(jnp.int32, (touches, rows), 1).astype(F32)
    for t in range(towers):
        ids, rates = owed[:, 2 * t : 2 * t + 1], owed[:, 2 * t + 1 : 2 * t + 2]
        chosen = jnp.sum(jnp.where(place == ids, rates, 0.0), axis=0, keepdims=True)
        value = tables_ref[t] * jnp.where(chosen > 0.0, chosen, 1.0)
        decayed[t] = value
        pairs.append(jnp.concatenate(split(value), axis=0))
    def own_copy(sign, k, s):
        at = slice_at(s)
        return pltpu.make_async_remote_copy(
            src_ref=pool.at[k, at],
            dst_ref=feats.at[me, at],
            send_sem=own_send.at[(1 - sign) // 2, k, s],
            recv_sem=ag_recv.at[me, s],
            device_id={"member": 2 * (chip + sign) + k},
            device_id_type=MESH,
        )

    def mate_copy(s):
        at = slice_at(s)
        return pltpu.make_async_remote_copy(
            src_ref=pool.at[1 - core, at],
            dst_ref=feats.at[me, at],
            send_sem=mate_send.at[s],
            recv_sem=ag_recv.at[me, s],
            device_id={"member": mate},
            device_id_type=MESH,
        )

    def block_copy(sign, block, s):
        at = slice_at(s)
        return pltpu.make_async_remote_copy(
            src_ref=feats.at[block, at],
            dst_ref=feats.at[block, at],
            send_sem=ag_send.at[(1 - sign) // 2, block, s],
            recv_sem=ag_recv.at[block, s],
            device_id={"member": 2 * (chip + sign) + core},
            device_id_type=MESH,
        )

    def goes_on(sign):
        return chip < chips - 1 if sign > 0 else chip > 0

    def present(sign, d):
        return chip >= d if sign > 0 else chip + d < chips

    def ahead(sign, act_on):
        @pl.loop(0, chips - 1 - chip if sign > 0 else chip)
        def _(i):
            act_on(chips - 1 - i if sign > 0 else i)

    def behind(sign, act_on):
        @pl.loop(0, chip if sign > 0 else chips - 1 - chip)
        def _(i):
            act_on(chip - 1 - i if sign > 0 else chip + 1 + i)

    def pass_on(sign, d, over):
        def one(s):
            for k in range(2):
                block = 2 * (chip - sign * d) + k
                block_copy(sign, block, s).wait_recv()

                @pl.when(goes_on(sign))
                def _():
                    block_copy(sign, block, s).start()

        @pl.when(present(sign, d))
        def _():
            over(one)

    def at_once(sign):
        if sign > 0:
            return jnp.logical_or(chip == 0, chip == chips - 2)
        return jnp.logical_or(chip == chips - 1, chip == 1)

    def own_rest(sign):
        def one(s):
            for k in range(2):
                own_copy(sign, k, s).start()

        @pl.when(goes_on(sign) & jnp.logical_not(at_once(sign)))
        def _():
            one(chip)
            behind(sign, one)

    order = sorted(range(1, chips), key=lambda i: -min(i, chips - i))
    place = lax.broadcasted_iota(jnp.int32, (2 * own, rows), 1).astype(F32)
    for i in range(1, chips + 1):
        there = lax.rem(jnp.where(chip < chips // 2, chip + chips - i, chip + i), chips)
        span = pl.ds(pl.multiple_of(there * 2 * own, 2 * own), 2 * own)
        pooled = []
        for t in range(towers):
            counts = jnp.zeros((2 * own, rows), F32)
            for b in range(bags):
                k = t * bags + b
                counts = counts + jnp.where(place == cols[span, k : k + 1], 1.0, 0.0)
            counts = counts.astype(BF16)
            for k in range(2):
                counts_ref[t, k, slice_at(there), :] = counts[k * own : (k + 1) * own]
            both = dot1(counts, pairs[t], NT)
            pooled.append(both[:, :width] + both[:, width:])
        pooled = jnp.concatenate(pooled, axis=1)
        for k in range(2):
            pool[k, slice_at(there), :] = pooled[k * own : (k + 1) * own]
        if i == 1:
            pl.semaphore_wait(barrier, n - 1 + nt - 1)

        @pl.when(jnp.logical_or(there > chip, at_once(1)) & goes_on(1))
        def _():
            for k in range(2):
                own_copy(1, k, there).start()

        @pl.when(jnp.logical_or(there < chip, at_once(-1)) & goes_on(-1))
        def _():
            for k in range(2):
                own_copy(-1, k, there).start()

        mate_copy(there).start()
    feats[me] = pool[core]

    for copy in loads[:towers]:
        copy.wait()
    for t in range(towers):

        @pl.loop(0, fin // 64)
        def _(i):
            span = pl.ds(pl.multiple_of(i * 64, 64), 64)
            w1h[t, span, :], w1l[t, span, :] = split(stage[t, span, :])

    for sign in (1, -1):
        pass_on(sign, 1, functools.partial(ahead, sign))
    for sign in (1, -1):
        own_rest(sign)

    for copy in loads[towers:]:
        copy.wait()
    for t in range(towers):

        @pl.loop(0, hid // 128)
        def _(i):
            span = pl.ds(pl.multiple_of(i * 128, 128), 128)
            w2h[t, span, :], w2l[t, span, :] = split(w2f[t, span, :])

    head = head_ref[:, pl.ds(pl.multiple_of(tpos * flat, flat), flat)]
    mixh[...], mixl[...] = split(jnp.concatenate([lift[...].T * head, press[...].T], axis=0))

    for d in range(2, chips):
        for sign in (1, -1):
            pass_on(sign, d, functools.partial(ahead, sign))
    store(decayed, decayed_out)

    def mate_arrives(s):
        block_copy(1, mate, s).wait_recv()

    mate_arrives(chip)
    for d in range(1, chips):
        for sign in (1, -1):
            pass_on(sign, d, lambda act_on: act_on(chip))
    flat_out = []
    for t in range(towers):
        part = slice(t * width, (t + 1) * width)
        x = jnp.concatenate([feats[b, slice_at(chip), part] for b in range(n)], axis=1)
        h = few3(split(x), (w1h[t], w1l[t]))
        flat_out.append(few3(split(h * sigmoid(h)), (w2h[t], w2l[t])))
    flat_out = jnp.concatenate(flat_out, axis=1)
    stats[:, : 2 * rank] = few3(split(flat_out), (mixh[...], mixl[...]), NT)
    stats[:, 2 * rank :] = jnp.broadcast_to(
        jnp.sum(flat_out * head, axis=1, keepdims=True), (own, rank)
    )

    def tower_copy(d):
        other = lax.rem(tpos + d, nt)
        return pltpu.make_async_remote_copy(
            src_ref=stats.at[pl.ds(pl.multiple_of(other * piece, piece), piece)],
            dst_ref=rs_buf.at[tpos],
            send_sem=rs_send.at[d],
            recv_sem=rs_recv.at[d],
            device_id={"tower": other},
            device_id_type=MESH,
        )

    for d in range(1, nt):
        tower_copy(d).start()

    for c in range(chips):
        tout_send[c] = flat_out[:, c * pair_flat : (c + 1) * pair_flat]
    tout_recv[chip] = tout_send[chip]

    def tout_copy(i):
        there = lax.rem(chip + i, chips)
        return pltpu.make_async_remote_copy(
            src_ref=tout_send.at[there],
            dst_ref=tout_recv.at[chip],
            send_sem=to_send.at[i],
            recv_sem=to_recv.at[i],
            device_id={"member": 2 * there + core},
            device_id_type=MESH,
        )

    def member_copies(i):
        return [
            pltpu.make_async_remote_copy(
                src_ref=ref.at[chip, tpos],
                dst_ref=ref.at[chip, tpos],
                send_sem=gm_send.at[k, i],
                recv_sem=gm_recv.at[k, i],
                device_id={"member": 2 * lax.rem(chip + i, chips) + core},
                device_id_type=MESH,
            )
            for k, ref in enumerate((errs, gath))
        ]

    def column_copies(d):
        return [
            pltpu.make_async_remote_copy(
                src_ref=ref.at[:, tpos],
                dst_ref=ref.at[:, tpos],
                send_sem=gt_send.at[k, d],
                recv_sem=gt_recv.at[k, d],
                device_id={"tower": lax.rem(tpos + d, nt)},
                device_id_type=MESH,
            )
            for k, ref in enumerate((errs, gath))
        ]

    for sign in (1, -1):
        pass_on(sign, 1, functools.partial(behind, sign))
    for sign in (1, -1):
        behind(sign, mate_arrives)
    per = 4
    together = per * width

    def hidden_group(t, c, g):
        part = slice(t * width, (t + 1) * width)
        span = slice(c * chunk, (c + 1) * chunk)
        x = jnp.concatenate([feats[per * g + k, span, part] for k in range(per)], axis=1)
        x = split(x)
        ins = pl.ds(pl.multiple_of(g * together, together), together)
        for k in range(hid // tile):
            lanes = slice(k * tile, (k + 1) * tile)
            yield lanes, deep3(x, (w1h[t, ins, lanes], w1l[t, ins, lanes]))

    near = chip // 2
    for t in range(towers):
        for c in range(half // chunk):
            span = slice(c * chunk, (c + 1) * chunk)
            for lanes, value in hidden_group(t, c, near):
                stage[t, span, lanes] = value

    for d in range(1, nt):
        tower_copy(d).wait_recv()
    summed = stats[pl.ds(pl.multiple_of(tpos * piece, piece), piece), :]
    for d in range(1, nt):
        summed = summed + rs_buf[lax.rem(tpos + d, nt)]
    scaled, projected = summed[:, :rank], summed[:, rank : 2 * rank]
    logit = jnp.sum(projected * scaled, axis=1, keepdims=True) + summed[:, 2 * rank :]
    logits[...] = logit
    seat = lax.broadcasted_iota(jnp.int32, (piece, own), 1)
    wanted = lax.broadcasted_iota(jnp.int32, (piece, own), 0) + tpos * piece
    clicks = jnp.where(seat == wanted, label_ref[...].astype(F32), 0.0)
    error = sigmoid(logit) - jnp.sum(clicks, axis=1, keepdims=True)
    gath[chip, tpos, :, :rank] = error * projected
    gath[chip, tpos, :, rank:] = error * scaled
    seat = lax.broadcasted_iota(jnp.int32, (piece, rank), 1)
    wanted = lax.broadcasted_iota(jnp.int32, (piece, rank), 0)
    errs[chip, tpos] = jnp.sum(jnp.where(seat == wanted, error, 0.0), axis=0, keepdims=True)
    for i in order:
        for copy in member_copies(i):
            copy.start()
    store(logits, logits_out)

    def far(sign, d, wanted):
        @pl.when(wanted)
        def _():
            pass_on(sign, d, functools.partial(behind, sign))

    for d in range(2, chips):
        for sign in (1, -1):
            far(sign, d, goes_on(sign))
    for i in order:
        tout_copy(i).start()
    for i in order:
        for copy in member_copies(i):
            copy.wait_recv()
    for d in range(1, nt):
        for copy in column_copies(d):
            copy.start()
    for d in range(2, chips):
        for sign in (1, -1):
            far(sign, d, jnp.logical_not(goes_on(sign)))

    start = pl.multiple_of(chip * pair_hid, pair_hid)
    groups = n // per
    for t in range(towers):
        part = slice(t * width, (t + 1) * width)
        for c in range(half // chunk):
            span = slice(c * chunk, (c + 1) * chunk)
            for i in range(1, groups):
                for lanes, value in hidden_group(t, c, lax.rem(near + i, groups)):
                    h = stage[t, span, lanes] + value
                    if i < groups - 1:
                        stage[t, span, lanes] = h
                    else:
                        sig = sigmoid(h)
                        a = h * sig
                        act[span, lanes] = a
                        stage[t, span, lanes] = sig + a * (1.0 - sig)
            both = jnp.concatenate([feats[2 * chip + k, span, part] for k in range(2)], axis=1)
            pth[t, :, span], ptl[t, :, span] = split(both.T)
            acth[t, :, span], actl[t, :, span] = split(act[span, pl.ds(start, pair_hid)].T)

    for i in order:
        tout_copy(i).wait_recv()
    for d in range(1, nt):
        for copy in column_copies(d):
            copy.wait_recv()

    def back_copy(slot, source, target):
        return pltpu.make_async_remote_copy(
            src_ref=source,
            dst_ref=target,
            send_sem=back_send.at[slot],
            recv_sem=back_recv.at[slot],
            device_id={"member": mate},
            device_id_type=MESH,
        )

    def rows_of(which, size):
        return pl.ds(pl.multiple_of(which * size, size), size)

    def back_copies(t):
        return [
            back_copy(3 * t, gpool.at[t, rows_of(1 - core, width)], gpool_in.at[t]),
            back_copy(3 * t + 1, gf.at[t, rows_of(1 - core, width)], gf_in.at[t]),
            back_copy(3 * t + 2, gsec.at[t, rows_of(1 - core, block_hid)], gsec_in.at[t]),
        ]

    def lift_copy():
        return back_copy(3 * towers, glp.at[rows_of(1 - core, pair_flat // 2)], glp_in)

    def put(ref, index, value, fresh):
        if fresh:
            ref[index] = value
        else:
            ref[index] += value

    errors = jnp.concatenate(
        [
            jnp.broadcast_to(errs[c, t], (piece, rank))
            for c in range(chips)
            for t in range(nt)
        ],
        axis=0,
    )
    seat = lax.broadcasted_iota(jnp.int32, (half, rank), 1)
    wanted = lax.rem(lax.broadcasted_iota(jnp.int32, (half, rank), 0), piece)
    errors = jnp.sum(jnp.where(seat == wanted, errors, 0.0), axis=1, keepdims=True)
    pair_rows = pl.ds(pl.multiple_of(chip * 2 * width, 2 * width), 2 * width)
    for t in range(towers):
        part = slice(t * outs, (t + 1) * outs)
        for c in range(half // chunk):
            span = slice(c * chunk, (c + 1) * chunk)
            here = slice(c * (chunk // own), (c + 1) * (chunk // own))
            block = gath[here].reshape(chunk, 2 * rank)
            go = split(
                errors[span] * head[:, part]
                + deep3(split(block), (mixh[:, part], mixl[:, part]))
            )
            grad_pooled = jnp.zeros((2 * width, chunk), F32)
            for k in range(hid // tile):
                lanes = slice(k * tile, (k + 1) * tile)
                grad_act = deep3(go, (w2h[t, lanes, :], w2l[t, lanes, :]), NT)
                grad_hidden = split(grad_act * stage[t, span, lanes])
                value = deep3((pth[t, :, span], ptl[t, :, span]), grad_hidden)
                put(gf, (t, slice(None), lanes), value, c == 0)
                first = (w1h[t, pair_rows, lanes], w1l[t, pair_rows, lanes])
                grad_pooled = grad_pooled + deep3(first, grad_hidden, NT)
            gpool[t, :, span] = grad_pooled
            put(gsec, (t,), deep3((acth[t, :, span], actl[t, :, span]), go), c == 0)
        for copy in back_copies(t):
            copy.start()

    outputs = jnp.concatenate([tout_recv[c] for c in range(chips)], axis=0)
    block = gath[...].reshape(half, 2 * rank)
    value = deep3(split(outputs.T), split(block))
    seat = lax.broadcasted_iota(jnp.int32, (pair_flat, flat), 1)
    wanted = lax.broadcasted_iota(jnp.int32, (pair_flat, flat), 0) + chip * pair_flat
    weights = jnp.sum(jnp.where(seat == wanted, head, 0.0), axis=1, keepdims=True)
    glp[:, :rank] = weights * value[:, :rank]
    glp[:, rank:] = value[:, rank:]
    lift_copy().start()

    for t in range(towers):
        from_mate = back_copies(t)
        mine = jnp.concatenate(split(gpool[t, rows_of(core, width), :]), axis=0)
        both = dot1(mine, counts_ref[t, core])
        from_mate[0].wait_recv()
        theirs = jnp.concatenate(split(gpool_in[t]), axis=0)
        both = both + dot1(theirs, counts_ref[t, 1 - core])
        gt[t] = both[:width] + both[width:]
        store(gt.at[t], gt_out.at[t])
        from_mate[1].wait_recv()
        gf_in[t] += gf[t, rows_of(core, width), :]
        store(gf_in.at[t], gf_out.at[t])
        from_mate[2].wait_recv()
        gsec_in[t] += gsec[t, rows_of(core, block_hid), :]
        store(gsec_in.at[t], gsec_out.at[t])
    lift_copy().wait_recv()
    glp_in[...] += glp[rows_of(core, pair_flat // 2), :]
    store(glp_in, glp_out)

    for sign in (1, -1):

        @pl.when(goes_on(sign))
        def _():
            for s in range(chips):
                for k in range(2):
                    own_copy(sign, k, s).wait_send()
                for d in range(1, chips):

                    @pl.when(present(sign, d))
                    def _():
                        for k in range(2):
                            block_copy(sign, 2 * (chip - sign * d) + k, s).wait_send()

    for s in range(chips):
        mate_copy(s).wait_send()
    for i in order:
        tout_copy(i).wait_send()
        for copy in member_copies(i):
            copy.wait_send()
    for d in range(1, nt):
        tower_copy(d).wait_send()
        for copy in column_copies(d):
            copy.wait_send()
    for t in range(towers):
        for copy in back_copies(t):
            copy.wait_send()
    lift_copy().wait_send()
    for copy in stores:
        copy.wait()


def final_kernel(
    logits_ref,
    decayed_ref,
    gt_ref,
    gf_ref,
    gsec_ref,
    glp_ref,
    acc_ref,
    new_tables_ref,
    new_acc_ref,
    grad_first_ref,
    grad_second_ref,
    grad_lift_ref,
    grad_press_ref,
    logits_out_ref,
):
    rank = logits_ref.shape[1]
    for t in range(gt_ref.shape[0]):
        grad_second_ref[:, t, :] = gsec_ref[t]
        grad_first_ref[:, t, :] = gf_ref[t]
        g = gt_ref[t]
        value = acc_ref[t] + jnp.mean(g * g, axis=0, keepdims=True)
        new_acc_ref[t] = value
        new_tables_ref[t] = decayed_ref[t] - LEARN_RATE * g / (jnp.sqrt(value) + EPSILON)
    grad_lift_ref[...] = glp_ref[:, :rank]
    grad_press_ref[...] = glp_ref[:, rank:]
    piece = logits_ref.shape[0]
    place = lax.broadcasted_iota(jnp.int32, (piece, piece), 1)
    wanted = lax.broadcasted_iota(jnp.int32, (piece, piece), 0)
    values = jnp.where(place == wanted, logits_ref[:, :1], 0.0)
    logits_out_ref[...] = jnp.sum(values, axis=0, keepdims=True)


def per_device(n, nt, *args):
    bag_ids, touch_ids, elapsed, tables, accumulator, first, second, lift, press, head, labels = args
    towers, _, bags, total = bag_ids.shape
    rows, width = tables.shape[2:]
    fin, _, hid = first.shape
    outs = second.shape[2]
    rank = lift.shape[1]
    flat = towers * outs
    chips = n // 2
    own = total // n
    half = own * chips
    piece = own // nt
    block_hid = hid // n
    pair_flat = flat // chips
    lanes = towers * width
    vmem = pl.BlockSpec(memory_space=pltpu.VMEM)
    anys = pl.BlockSpec(memory_space=pl.ANY)
    sem = pltpu.SemaphoreType.DMA
    shape = jax.ShapeDtypeStruct
    between = pl.pallas_call(
        functools.partial(main_kernel, (n, nt)),
        out_shape=(
            shape((piece, rank), F32),
            shape((towers, width, rows), F32),
            shape((towers, width, rows), F32),
            shape((towers, width, hid), F32),
            shape((towers, block_hid, outs), F32),
            shape((pair_flat // 2, 2 * rank), F32),
        ),
        in_specs=[vmem] * 4 + [anys] * 4 + [vmem] * 2,
        out_specs=[anys] * 6,
        scratch_shapes=[
            pltpu.VMEM((towers, max(half, fin), hid), F32),
            pltpu.VMEM((towers, fin, hid), BF16),
            pltpu.VMEM((towers, fin, hid), BF16),
            pltpu.VMEM((towers, hid, outs), F32),
            pltpu.VMEM((towers, hid, outs), BF16),
            pltpu.VMEM((towers, hid, outs), BF16),
            pltpu.VMEM((flat, rank), F32),
            pltpu.VMEM((flat, rank), F32),
            pltpu.VMEM((2 * rank, flat), BF16),
            pltpu.VMEM((2 * rank, flat), BF16),
            pltpu.VMEM((total, 128), F32),
            pltpu.VMEM((towers, 2, half, rows), BF16),
            pltpu.VMEM((towers, width, rows), F32),
            pltpu.VMEM((2, half, lanes), F32),
            pltpu.VMEM((n, half, lanes), F32),
            pltpu.VMEM((chips, own, pair_flat), F32),
            pltpu.VMEM((chips, own, pair_flat), F32),
            pltpu.VMEM((own, 3 * rank), F32),
            pltpu.VMEM((nt, piece, 3 * rank), F32),
            pltpu.VMEM((chips, nt, piece, 2 * rank), F32),
            pltpu.VMEM((chips, nt, 1, rank), F32),
            pltpu.VMEM((half, hid), F32),
            pltpu.VMEM((towers, 2 * block_hid, half), BF16),
            pltpu.VMEM((towers, 2 * block_hid, half), BF16),
            pltpu.VMEM((towers, 2 * width, half), BF16),
            pltpu.VMEM((towers, 2 * width, half), BF16),
            pltpu.VMEM((towers, 2 * width, hid), F32),
            pltpu.VMEM((towers, width, hid), F32),
            pltpu.VMEM((towers, 2 * block_hid, outs), F32),
            pltpu.VMEM((towers, block_hid, outs), F32),
            pltpu.VMEM((towers, 2 * width, half), F32),
            pltpu.VMEM((towers, width, half), F32),
            pltpu.VMEM((pair_flat, 2 * rank), F32),
            pltpu.VMEM((pair_flat // 2, 2 * rank), F32),
            pltpu.VMEM((towers, width, rows), F32),
            pltpu.VMEM((piece, rank), F32),
            sem((2 * towers + 2,)),
            sem((3 + 3 * towers,)),
            sem((2, 2, chips)),
            sem((chips,)),
            sem((2, n, chips)),
            sem((n, chips)),
            sem((nt,)),
            sem((nt,)),
            sem((chips,)),
            sem((chips,)),
            sem((2, chips)),
            sem((2, chips)),
            sem((2, nt)),
            sem((2, nt)),
            sem((3 * towers + 1,)),
            sem((3 * towers + 1,)),
        ],
        compiler_params=pltpu.CompilerParams(
            collective_id=0, has_side_effects=True, vmem_limit_bytes=67043328
        ),
    )(
        bag_ids[:, 0],
        touch_ids,
        elapsed,
        jnp.transpose(tables[:, 0], (0, 2, 1)),
        first,
        second,
        lift,
        press,
        head[None, :],
        labels,
    )
    out = pl.pallas_call(
        final_kernel,
        out_shape=(
            shape((towers, width, rows), F32),
            shape((towers, 1, rows), F32),
            shape((width, towers, hid), F32),
            shape((block_hid, towers, outs), F32),
            shape((flat // n, rank), F32),
            shape((flat // n, rank), F32),
            shape((1, piece), F32),
        ),
        in_specs=[vmem] * 7,
        out_specs=[vmem] * 7,
    )(*between, accumulator)
    new_tables, new_acc, grad_first, grad_second, grad_lift, grad_press, logits = out
    return (
        jnp.transpose(new_tables, (0, 2, 1))[:, None],
        new_acc,
        grad_first,
        grad_second,
        grad_lift,
        grad_press,
        logits,
    )


def solution(mesh):
    placed = (
        P("tower", "member", None, None),
        P("tower", "member", None),
        P("tower", "member", None),
        P("tower", "member", None, None),
        P("tower", "member", None),
        P(None, "tower", None),
        P(None, "tower", None),
        P(),
        P(),
        P(),
        P("member", None),
    )
    return jax.shard_map(
        functools.partial(per_device, mesh.shape["member"], mesh.shape["tower"]),
        mesh=mesh,
        in_specs=placed,
        out_specs=(
            P("tower", "member", None, None),
            P("tower", "member", None),
            P("member", "tower", None),
            P("member", "tower", None),
            P(("tower", "member"), None),
            P(("tower", "member"), None),
            P("member", "tower"),
        ),
        check_vma=False,
    )
```

```python
import functools
import math

import jax
import jax.numpy as jnp
from jax import lax
from jax.experimental import pallas as pl
from jax.experimental.pallas import tpu as pltpu
from jax.sharding import PartitionSpec as P

MESH = pl.DeviceIdType.MESH
DECAY_RATE = 0.98
LEARN_RATE = 1.0
EPSILON = 1e-08
F32 = jnp.float32
BF16 = jnp.bfloat16
NN = (((1,), (0,)), ((), ()))
NT = (((1,), (1,)), ((), ()))


def split(x):
    hi = x.astype(BF16)
    return hi, (x - hi.astype(F32)).astype(BF16)


def dot1(a, b, dims=NN):
    return lax.dot_general(a, b, dims, preferred_element_type=F32)


def few3(a, b, dims=NN):
    (ah, al), (bh, bl) = a, b
    both = dot1(jnp.concatenate([ah, al], axis=0), bh, dims)
    m = ah.shape[0]
    return both[:m] + (both[m:] + dot1(ah, bl, dims))


def deep3(a, b, dims=NN):
    (ah, al), (bh, bl) = a, b
    return dot1(
        jnp.concatenate([ah, al, ah], axis=1),
        jnp.concatenate([bh, bh, bl], axis=dims[0][1][0]),
        dims,
    )


def sigmoid(x):
    return 1.0 / (1.0 + jnp.exp(-x))


def main_kernel(
    dims,
    bag_ref,
    touch_ref,
    elapsed_ref,
    tables_ref,
    first_hbm,
    second_hbm,
    lift_hbm,
    press_hbm,
    head_ref,
    label_ref,
    logits_out,
    decayed_out,
    gt_out,
    gf_out,
    gsec_out,
    glp_out,
    stage,
    w1h,
    w1l,
    w2f,
    w2h,
    w2l,
    lift,
    press,
    mixh,
    mixl,
    cols,
    counts_ref,
    decayed,
    pool,
    feats,
    tout_send,
    tout_recv,
    stats,
    rs_buf,
    line,
    line_buf,
    gath,
    errs,
    act,
    acth,
    actl,
    pth,
    ptl,
    gf,
    gf_in,
    gsec,
    gsec_in,
    gpool,
    gpool_in,
    glp,
    glp_in,
    gt,
    logits,
    load_sem,
    store_sem,
    crit_send,
    mate_send,
    ag_send,
    ag_recv,
    rs_send,
    rs_recv,
    to_send,
    to_recv,
    gm_send,
    gm_recv,
    gt_send,
    gt_recv,
    back_send,
    back_recv,
):
    n, nt = dims
    me = lax.axis_index("member")
    tpos = lax.axis_index("tower")
    towers, bags, total = bag_ref.shape
    width, rows = tables_ref.shape[1:]
    touches = touch_ref.shape[2]
    hid, outs = w2h.shape[1:]
    fin = w1h.shape[1]
    rank = lift.shape[1]
    flat = towers * outs
    chips = n // 2
    own = total // n
    half = own * chips
    piece = own // nt
    chunk = min(256, half)
    tile = min(256, hid)
    pair_hid = 2 * (hid // n)
    block_hid = hid // n
    pair_flat = flat // chips
    chip, core = me // 2, lax.rem(me, 2)
    mate = me + 1 - 2 * core

    loads = []

    def load(source, target):
        loads.append(pltpu.make_async_copy(source, target, load_sem.at[len(loads)]))
        loads[-1].start()

    for t in range(towers):
        load(first_hbm.at[:, t, :], stage.at[t, :fin])
    for t in range(towers):
        load(second_hbm.at[:, t, :], w2f.at[t])
    load(lift_hbm.at[pl.ds(tpos * flat, flat)], lift)
    load(press_hbm.at[pl.ds(tpos * flat, flat)], press)

    barrier = pltpu.get_barrier_semaphore()
    for d in range(1, n):
        pl.semaphore_signal(
            barrier, inc=1, device_id={"member": lax.rem(me + d, n)}, device_id_type=MESH
        )
    for d in range(1, nt):
        pl.semaphore_signal(
            barrier, inc=1, device_id={"tower": lax.rem(tpos + d, nt)}, device_id_type=MESH
        )

    stores = []

    def store(source, target):
        stores.append(pltpu.make_async_copy(source, target, store_sem.at[len(stores)]))
        stores[-1].start()

    def slice_at(index):
        return pl.ds(pl.multiple_of(index * own, own), own)

    stack = [bag_ref[t].astype(F32) for t in range(towers)]
    stack.append(jnp.zeros((128 - towers * bags, total), F32))
    cols[...] = jnp.concatenate(stack, axis=0).T
    stack = []
    for t in range(towers):
        stack.append(touch_ref[t].astype(F32))
        stack.append(jnp.exp(elapsed_ref[t].astype(F32) * math.log(DECAY_RATE)))
    stack.append(jnp.zeros((128 - 2 * towers, touches), F32))
    owed = jnp.concatenate(stack, axis=0).T
    pairs = []
    place = lax.broadcasted_iota(jnp.int32, (touches, rows), 1).astype(F32)
    for t in range(towers):
        ids, rates = owed[:, 2 * t : 2 * t + 1], owed[:, 2 * t + 1 : 2 * t + 2]
        chosen = jnp.sum(jnp.where(place == ids, rates, 0.0), axis=0, keepdims=True)
        value = tables_ref[t] * jnp.where(chosen > 0.0, chosen, 1.0)
        decayed[t] = value
        pairs.append(jnp.concatenate(split(value), axis=0))
    out = jnp.where(chip < chips // 2, -1, 1)
    inward = -out

    def way(sign):
        return jnp.where(sign > 0, 0, 1)

    def slice_from(sign, j):
        return lax.rem(chip + chips + sign * j, chips)

    def own_copy(there, k, s, semaphore):
        at = slice_at(s)
        return pltpu.make_async_remote_copy(
            src_ref=pool.at[k, at],
            dst_ref=feats.at[me, at],
            send_sem=semaphore,
            recv_sem=ag_recv.at[chip, s],
            device_id={"member": 2 * there + k},
            device_id_type=MESH,
        )

    def mate_copy():
        return pltpu.make_async_remote_copy(
            src_ref=pool.at[1 - core],
            dst_ref=feats.at[me],
            send_sem=mate_send.at[0],
            recv_sem=ag_recv.at[chip, 0],
            device_id={"member": mate},
            device_id_type=MESH,
        )

    def pair_copy(sign, d, s):
        source, at = chip - sign * d, slice_at(s)
        pair = pl.ds(2 * source, 2)
        return pltpu.make_async_remote_copy(
            src_ref=feats.at[pair, at],
            dst_ref=feats.at[pair, at],
            send_sem=ag_send.at[way(sign), d],
            recv_sem=ag_recv.at[source, s],
            device_id={"member": 2 * (chip + sign) + core},
            device_id_type=MESH,
        )

    def goes_on(sign):
        return (chip + sign >= 0) & (chip + sign < chips)

    def present(sign, d):
        return (chip - sign * d >= 0) & (chip - sign * d < chips)

    def own_rest(sign):
        @pl.when(goes_on(sign))
        def _():
            for j in (0, *range(chips - 1, 1, -1)):
                for k in range(2):
                    own_copy(chip + sign, k, slice_from(sign, j), ag_send.at[way(sign), 0]).start()

    def own_arrives(d):
        for sign in (1, -1):

            @pl.when(present(sign, d))
            def _():
                pair_copy(sign, d, chip).wait_recv()

    def pass_on(part, sign, d):
        @pl.when(goes_on(sign))
        def _():
            for j in part:
                copy = pair_copy(sign, d, slice_from(sign, j))
                if j:
                    copy.wait_recv()
                if j != 1:
                    copy.start()

    def arrives(sign, d):
        @pl.when(jnp.logical_not(goes_on(sign)))
        def _():
            for j in range(chips - 1, 0, -1):
                pair_copy(sign, d, slice_from(sign, j)).wait_recv()

    order = sorted(range(1, chips), key=lambda i: -min(i, chips - i))
    place = lax.broadcasted_iota(jnp.int32, (2 * own, rows), 1).astype(F32)
    for i in range(1, chips + 1):
        there = lax.rem(jnp.where(chip < chips // 2, chip + chips - i, chip + i), chips)
        span = pl.ds(pl.multiple_of(there * 2 * own, 2 * own), 2 * own)
        pooled = []
        for t in range(towers):
            counts = jnp.zeros((2 * own, rows), F32)
            for b in range(bags):
                k = t * bags + b
                counts = counts + jnp.where(place == cols[span, k : k + 1], 1.0, 0.0)
            counts = counts.astype(BF16)
            for k in range(2):
                counts_ref[t, k, slice_at(there), :] = counts[k * own : (k + 1) * own]
            both = dot1(counts, pairs[t], NT)
            pooled.append(both[:, :width] + both[:, width:])
        pooled = jnp.concatenate(pooled, axis=1)
        for k in range(2):
            pool[k, slice_at(there), :] = pooled[k * own : (k + 1) * own]
        if i == 1:
            pl.semaphore_wait(barrier, n - 1 + nt - 1)

        if i < chips:
            for k in range(2):
                own_copy(there, k, there, crit_send.at[0]).start()
    own_rest(out)
    mate_copy().start()
    feats[me] = pool[core]

    for copy in loads[:towers]:
        copy.wait()
    for t in range(towers):

        @pl.loop(0, fin // 64)
        def _(i):
            span = pl.ds(pl.multiple_of(i * 64, 64), 64)
            w1h[t, span, :], w1l[t, span, :] = split(stage[t, span, :])

    own_rest(inward)
    for copy in loads[towers:]:
        copy.wait()
    for t in range(towers):

        @pl.loop(0, hid // 128)
        def _(i):
            span = pl.ds(pl.multiple_of(i * 128, 128), 128)
            w2h[t, span, :], w2l[t, span, :] = split(w2f[t, span, :])

    head = head_ref[:, pl.ds(pl.multiple_of(tpos * flat, flat), flat)]
    mixh[...], mixl[...] = split(jnp.concatenate([lift[...].T * head, press[...].T], axis=0))
    store(decayed, decayed_out)

    def along(d, act_on):
        for sign in (out, inward):
            pl.when(present(sign, d))(functools.partial(act_on, sign, d))

    mate_copy().wait_recv()
    for d in range(1, chips):
        own_arrives(d)
    for d in range(1, chips):
        along(d, functools.partial(pass_on, [0]))
    along(1, functools.partial(pass_on, [chips - 1]))
    flat_out = []
    for t in range(towers):
        part = slice(t * width, (t + 1) * width)
        x = jnp.concatenate([feats[b, slice_at(chip), part] for b in range(n)], axis=1)
        h = few3(split(x), (w1h[t], w1l[t]))
        flat_out.append(few3(split(h * sigmoid(h)), (w2h[t], w2l[t])))
    flat_out = jnp.concatenate(flat_out, axis=1)
    stats[...] = few3(split(flat_out), (mixh[...], mixl[...]), NT).reshape(nt, piece, 2 * rank)
    linear = jnp.sum(flat_out * head, axis=1, keepdims=True)
    seat = lax.broadcasted_iota(jnp.int32, (piece, rank), 1)
    wanted = lax.broadcasted_iota(jnp.int32, (piece, rank), 0)
    for k in range(nt):
        row = jnp.where(seat == wanted, linear[k * piece : (k + 1) * piece], 0.0)
        line[k] = jnp.sum(row, axis=0, keepdims=True)

    def tower_copies(d):
        other = lax.rem(tpos + d, nt)
        return [
            pltpu.make_async_remote_copy(
                src_ref=ref.at[other],
                dst_ref=buf.at[tpos],
                send_sem=rs_send.at[k],
                recv_sem=rs_recv.at[k, d - 1],
                device_id={"tower": other},
                device_id_type=MESH,
            )
            for k, (ref, buf) in enumerate(((line, line_buf), (stats, rs_buf)))
        ]

    for d in range(1, nt):
        for copy in tower_copies(d):
            copy.start()

    for c in range(chips):
        tout_send[c] = flat_out[:, c * pair_flat : (c + 1) * pair_flat]
    tout_recv[chip] = tout_send[chip]

    def tout_copy(i):
        there = lax.rem(chip + i, chips)
        return pltpu.make_async_remote_copy(
            src_ref=tout_send.at[there],
            dst_ref=tout_recv.at[chip],
            send_sem=to_send.at[0],
            recv_sem=to_recv.at[i - 1],
            device_id={"member": 2 * there + core},
            device_id_type=MESH,
        )

    def member_copies(i, there):
        return [
            pltpu.make_async_remote_copy(
                src_ref=ref.at[chip, tpos],
                dst_ref=ref.at[chip, tpos],
                send_sem=gm_send.at[k],
                recv_sem=gm_recv.at[k, i - 1],
                device_id={"member": 2 * there + core},
                device_id_type=MESH,
            )
            for k, ref in enumerate((errs, gath))
        ]

    def column_copies(d, source, count):
        where = pl.ds(source, count)
        return [
            pltpu.make_async_remote_copy(
                src_ref=ref.at[where, tpos],
                dst_ref=ref.at[where, tpos],
                send_sem=gt_send.at[k],
                recv_sem=gt_recv.at[k, d - 1],
                device_id={"tower": lax.rem(tpos + d, nt)},
                device_id_type=MESH,
            )
            for k, ref in enumerate((errs, gath))
        ]

    def column_start(source):
        for d in range(1, nt):
            for copy in column_copies(d, source, 1):
                copy.start()

    along(1, functools.partial(pass_on, range(chips - 2, 0, -1)))
    along(1, arrives)
    per = 4
    together = per * width

    def hidden_group(t, c, g):
        part = slice(t * width, (t + 1) * width)
        span = slice(c * chunk, (c + 1) * chunk)
        x = jnp.concatenate([feats[per * g + k, span, part] for k in range(per)], axis=1)
        x = split(x)
        ins = pl.ds(pl.multiple_of(g * together, together), together)
        for k in range(hid // tile):
            lanes = slice(k * tile, (k + 1) * tile)
            yield lanes, deep3(x, (w1h[t, ins, lanes], w1l[t, ins, lanes]))

    near = chip // 2
    for t in range(towers):
        for c in range(half // chunk):
            span = slice(c * chunk, (c + 1) * chunk)
            for lanes, value in hidden_group(t, c, near):
                stage[t, span, lanes] = value

    for d in range(1, nt):
        for copy in tower_copies(d):
            copy.wait_recv()
    summed, linear = stats[tpos], line[tpos]
    for d in range(1, nt):
        summed = summed + rs_buf[lax.rem(tpos + d, nt)]
        linear = linear + line_buf[lax.rem(tpos + d, nt)]
    scaled, projected = summed[:, :rank], summed[:, rank:]
    linear = jnp.sum(jnp.where(seat == wanted, linear, 0.0), axis=1, keepdims=True)
    logit = jnp.sum(projected * scaled, axis=1, keepdims=True) + linear
    logit = jnp.broadcast_to(logit, (piece, rank))
    logits[...] = logit
    place = lax.broadcasted_iota(jnp.int32, (piece, own), 1)
    mine = lax.broadcasted_iota(jnp.int32, (piece, own), 0) + tpos * piece
    clicks = jnp.where(place == mine, label_ref[...].astype(F32), 0.0)
    error = sigmoid(logit) - jnp.sum(clicks, axis=1, keepdims=True)
    gath[chip, tpos, :, :rank] = error * projected
    gath[chip, tpos, :, rank:] = error * scaled
    errs[chip, tpos] = jnp.sum(jnp.where(seat == wanted, error, 0.0), axis=0, keepdims=True)
    for i in order:
        for copy in member_copies(i, lax.rem(chip + i, chips)):
            copy.start()
    column_start(chip)
    store(logits, logits_out)

    for d in range(2, chips):
        along(d, functools.partial(pass_on, [chips - 1]))
    for source in sorted(range(chips), key=lambda c: -min(c, chips - 1 - c)):

        @pl.when(chip != source)
        def _():
            for copy in member_copies(lax.rem(chip + chips - source, chips), source):
                copy.wait_recv()
            column_start(source)

    for d in range(2, chips):
        along(d, functools.partial(pass_on, range(chips - 2, 0, -1)))
    for i in order:
        tout_copy(i).start()
    for d in range(2, chips):
        along(d, arrives)

    start = pl.multiple_of(chip * pair_hid, pair_hid)
    groups = n // per
    for t in range(towers):
        part = slice(t * width, (t + 1) * width)
        for c in range(half // chunk):
            span = slice(c * chunk, (c + 1) * chunk)
            for i in range(1, groups):
                for lanes, value in hidden_group(t, c, lax.rem(near + i, groups)):
                    h = stage[t, span, lanes] + value
                    if i < groups - 1:
                        stage[t, span, lanes] = h
                    else:
                        sig = sigmoid(h)
                        a = h * sig
                        act[span, lanes] = a
                        stage[t, span, lanes] = sig + a * (1.0 - sig)
            both = jnp.concatenate([feats[2 * chip + k, span, part] for k in range(2)], axis=1)
            pth[t, :, span], ptl[t, :, span] = split(both.T)
            acth[t, :, span], actl[t, :, span] = split(act[span, pl.ds(start, pair_hid)].T)

    def sent(ref, semaphore):
        pltpu.make_async_remote_copy(
            src_ref=ref,
            dst_ref=ref,
            send_sem=semaphore,
            recv_sem=ag_recv.at[0, 0],
            device_id={"member": mate},
            device_id_type=MESH,
        ).wait_send()

    sent(pool.at[0], mate_send.at[0])
    for k, ref in enumerate((line, stats)):
        sent(ref.at[: nt - 1], rs_send.at[k])
    sent(feats.at[:2, : half - own], crit_send.at[0])
    for sign in (1, -1):

        @pl.when(goes_on(sign))
        def _():
            sent(pool.at[:, : half - own], ag_send.at[way(sign), 0])
            for d in range(1, chips):

                @pl.when(present(sign, d))
                def _():
                    sent(feats.at[:2, : half - own], ag_send.at[way(sign), d])

    for i in order:
        tout_copy(i).wait_recv()
    for d in range(1, nt):
        for copy in column_copies(d, 0, chips):
            copy.wait_recv()
    sent(tout_send.at[: chips - 1], to_send.at[0])
    for k, ref in enumerate((errs, gath)):
        sent(ref.at[: chips - 1, 0], gm_send.at[k])
        sent(ref.at[:, : nt - 1], gt_send.at[k])

    def back_copy(slot, source, target):
        return pltpu.make_async_remote_copy(
            src_ref=source,
            dst_ref=target,
            send_sem=back_send.at[slot],
            recv_sem=back_recv.at[slot],
            device_id={"member": mate},
            device_id_type=MESH,
        )

    def rows_of(which, size):
        return pl.ds(pl.multiple_of(which * size, size), size)

    def back_copies(t):
        return [
            back_copy(3 * t, gpool.at[t, rows_of(1 - core, width)], gpool_in.at[t]),
            back_copy(3 * t + 1, gf.at[t, rows_of(1 - core, width)], gf_in.at[t]),
            back_copy(3 * t + 2, gsec.at[t, rows_of(1 - core, block_hid)], gsec_in.at[t]),
        ]

    def lift_copy():
        return back_copy(3 * towers, glp.at[rows_of(1 - core, pair_flat // 2)], glp_in)

    def put(ref, index, value, fresh):
        if fresh:
            ref[index] = value
        else:
            ref[index] += value

    errors = jnp.concatenate(
        [
            jnp.broadcast_to(errs[c, t], (piece, rank))
            for c in range(chips)
            for t in range(nt)
        ],
        axis=0,
    )
    seat = lax.broadcasted_iota(jnp.int32, (half, rank), 1)
    wanted = lax.rem(lax.broadcasted_iota(jnp.int32, (half, rank), 0), piece)
    errors = jnp.sum(jnp.where(seat == wanted, errors, 0.0), axis=1, keepdims=True)
    pair_rows = pl.ds(pl.multiple_of(chip * 2 * width, 2 * width), 2 * width)
    for t in range(towers):
        part = slice(t * outs, (t + 1) * outs)
        for c in range(half // chunk):
            span = slice(c * chunk, (c + 1) * chunk)
            here = slice(c * (chunk // own), (c + 1) * (chunk // own))
            block = gath[here].reshape(chunk, 2 * rank)
            go = split(
                errors[span] * head[:, part]
                + deep3(split(block), (mixh[:, part], mixl[:, part]))
            )
            grad_pooled = jnp.zeros((2 * width, chunk), F32)
            for k in range(hid // tile):
                lanes = slice(k * tile, (k + 1) * tile)
                grad_act = deep3(go, (w2h[t, lanes, :], w2l[t, lanes, :]), NT)
                grad_hidden = split(grad_act * stage[t, span, lanes])
                value = deep3((pth[t, :, span], ptl[t, :, span]), grad_hidden)
                put(gf, (t, slice(None), lanes), value, c == 0)
                first = (w1h[t, pair_rows, lanes], w1l[t, pair_rows, lanes])
                grad_pooled = grad_pooled + deep3(first, grad_hidden, NT)
            gpool[t, :, span] = grad_pooled
            put(gsec, (t,), deep3((acth[t, :, span], actl[t, :, span]), go), c == 0)
        for copy in back_copies(t):
            copy.start()

    outputs = jnp.concatenate([tout_recv[c] for c in range(chips)], axis=0)
    block = gath[...].reshape(half, 2 * rank)
    value = deep3(split(outputs.T), split(block))
    seat = lax.broadcasted_iota(jnp.int32, (pair_flat, flat), 1)
    wanted = lax.broadcasted_iota(jnp.int32, (pair_flat, flat), 0) + chip * pair_flat
    weights = jnp.sum(jnp.where(seat == wanted, head, 0.0), axis=1, keepdims=True)
    glp[:, :rank] = weights * value[:, :rank]
    glp[:, rank:] = value[:, rank:]
    lift_copy().start()

    for t in range(towers):
        from_mate = back_copies(t)
        mine = jnp.concatenate(split(gpool[t, rows_of(core, width), :]), axis=0)
        both = dot1(mine, counts_ref[t, core])
        from_mate[0].wait_recv()
        theirs = jnp.concatenate(split(gpool_in[t]), axis=0)
        both = both + dot1(theirs, counts_ref[t, 1 - core])
        gt[t] = both[:width] + both[width:]
        store(gt.at[t], gt_out.at[t])
        from_mate[1].wait_recv()
        gf_in[t] += gf[t, rows_of(core, width), :]
        store(gf_in.at[t], gf_out.at[t])
        from_mate[2].wait_recv()
        gsec_in[t] += gsec[t, rows_of(core, block_hid), :]
        store(gsec_in.at[t], gsec_out.at[t])
    lift_copy().wait_recv()
    glp_in[...] += glp[rows_of(core, pair_flat // 2), :]
    store(glp_in, glp_out)

    for t in range(towers):
        for copy in back_copies(t):
            copy.wait_send()
    lift_copy().wait_send()
    for copy in stores:
        copy.wait()


def final_kernel(
    logits_ref,
    decayed_ref,
    gt_ref,
    gf_ref,
    gsec_ref,
    glp_ref,
    acc_ref,
    new_tables_ref,
    new_acc_ref,
    grad_first_ref,
    grad_second_ref,
    grad_lift_ref,
    grad_press_ref,
    logits_out_ref,
):
    rank = logits_ref.shape[1]
    for t in range(gt_ref.shape[0]):
        grad_second_ref[:, t, :] = gsec_ref[t]
        grad_first_ref[:, t, :] = gf_ref[t]
        g = gt_ref[t]
        value = acc_ref[t] + jnp.mean(g * g, axis=0, keepdims=True)
        new_acc_ref[t] = value
        new_tables_ref[t] = decayed_ref[t] - LEARN_RATE * g / (jnp.sqrt(value) + EPSILON)
    grad_lift_ref[...] = glp_ref[:, :rank]
    grad_press_ref[...] = glp_ref[:, rank:]
    piece = logits_ref.shape[0]
    place = lax.broadcasted_iota(jnp.int32, (piece, piece), 1)
    wanted = lax.broadcasted_iota(jnp.int32, (piece, piece), 0)
    values = jnp.where(place == wanted, logits_ref[:, :1], 0.0)
    logits_out_ref[...] = jnp.sum(values, axis=0, keepdims=True)


def per_device(n, nt, *args):
    bag_ids, touch_ids, elapsed, tables, accumulator, first, second, lift, press, head, labels = args
    towers, _, bags, total = bag_ids.shape
    rows, width = tables.shape[2:]
    fin, _, hid = first.shape
    outs = second.shape[2]
    rank = lift.shape[1]
    flat = towers * outs
    chips = n // 2
    own = total // n
    half = own * chips
    piece = own // nt
    block_hid = hid // n
    pair_flat = flat // chips
    lanes = towers * width
    vmem = pl.BlockSpec(memory_space=pltpu.VMEM)
    anys = pl.BlockSpec(memory_space=pl.ANY)
    sem = pltpu.SemaphoreType.DMA
    shape = jax.ShapeDtypeStruct
    between = pl.pallas_call(
        functools.partial(main_kernel, (n, nt)),
        out_shape=(
            shape((piece, rank), F32),
            shape((towers, width, rows), F32),
            shape((towers, width, rows), F32),
            shape((towers, width, hid), F32),
            shape((towers, block_hid, outs), F32),
            shape((pair_flat // 2, 2 * rank), F32),
        ),
        in_specs=[vmem] * 4 + [anys] * 4 + [vmem] * 2,
        out_specs=[anys] * 6,
        scratch_shapes=[
            pltpu.VMEM((towers, max(half, fin), hid), F32),
            pltpu.VMEM((towers, fin, hid), BF16),
            pltpu.VMEM((towers, fin, hid), BF16),
            pltpu.VMEM((towers, hid, outs), F32),
            pltpu.VMEM((towers, hid, outs), BF16),
            pltpu.VMEM((towers, hid, outs), BF16),
            pltpu.VMEM((flat, rank), F32),
            pltpu.VMEM((flat, rank), F32),
            pltpu.VMEM((2 * rank, flat), BF16),
            pltpu.VMEM((2 * rank, flat), BF16),
            pltpu.VMEM((total, 128), F32),
            pltpu.VMEM((towers, 2, half, rows), BF16),
            pltpu.VMEM((towers, width, rows), F32),
            pltpu.VMEM((2, half, lanes), F32),
            pltpu.VMEM((n, half, lanes), F32),
            pltpu.VMEM((chips, own, pair_flat), F32),
            pltpu.VMEM((chips, own, pair_flat), F32),
            pltpu.VMEM((nt, piece, 2 * rank), F32),
            pltpu.VMEM((nt, piece, 2 * rank), F32),
            pltpu.VMEM((nt, 1, rank), F32),
            pltpu.VMEM((nt, 1, rank), F32),
            pltpu.VMEM((chips, nt, piece, 2 * rank), F32),
            pltpu.VMEM((chips, nt, 1, rank), F32),
            pltpu.VMEM((half, hid), F32),
            pltpu.VMEM((towers, 2 * block_hid, half), BF16),
            pltpu.VMEM((towers, 2 * block_hid, half), BF16),
            pltpu.VMEM((towers, 2 * width, half), BF16),
            pltpu.VMEM((towers, 2 * width, half), BF16),
            pltpu.VMEM((towers, 2 * width, hid), F32),
            pltpu.VMEM((towers, width, hid), F32),
            pltpu.VMEM((towers, 2 * block_hid, outs), F32),
            pltpu.VMEM((towers, block_hid, outs), F32),
            pltpu.VMEM((towers, 2 * width, half), F32),
            pltpu.VMEM((towers, width, half), F32),
            pltpu.VMEM((pair_flat, 2 * rank), F32),
            pltpu.VMEM((pair_flat // 2, 2 * rank), F32),
            pltpu.VMEM((towers, width, rows), F32),
            pltpu.VMEM((piece, rank), F32),
            sem((2 * towers + 2,)),
            sem((3 + 3 * towers,)),
            sem((1,)),
            sem((1,)),
            sem((2, chips)),
            sem((chips, chips)),
            sem((2,)),
            sem((2, nt - 1)),
            sem((1,)),
            sem((chips - 1,)),
            sem((2,)),
            sem((2, chips - 1)),
            sem((2,)),
            sem((2, nt - 1)),
            sem((3 * towers + 1,)),
            sem((3 * towers + 1,)),
        ],
        compiler_params=pltpu.CompilerParams(
            collective_id=0, has_side_effects=True, vmem_limit_bytes=67043328
        ),
    )(
        bag_ids[:, 0],
        touch_ids,
        elapsed,
        jnp.transpose(tables[:, 0], (0, 2, 1)),
        first,
        second,
        lift,
        press,
        head[None, :],
        labels,
    )
    out = pl.pallas_call(
        final_kernel,
        out_shape=(
            shape((towers, width, rows), F32),
            shape((towers, 1, rows), F32),
            shape((width, towers, hid), F32),
            shape((block_hid, towers, outs), F32),
            shape((flat // n, rank), F32),
            shape((flat // n, rank), F32),
            shape((1, piece), F32),
        ),
        in_specs=[vmem] * 7,
        out_specs=[vmem] * 7,
    )(*between, accumulator)
    new_tables, new_acc, grad_first, grad_second, grad_lift, grad_press, logits = out
    return (
        jnp.transpose(new_tables, (0, 2, 1))[:, None],
        new_acc,
        grad_first,
        grad_second,
        grad_lift,
        grad_press,
        logits,
    )


def solution(mesh):
    placed = (
        P("tower", "member", None, None),
        P("tower", "member", None),
        P("tower", "member", None),
        P("tower", "member", None, None),
        P("tower", "member", None),
        P(None, "tower", None),
        P(None, "tower", None),
        P(),
        P(),
        P(),
        P("member", None),
    )
    return jax.shard_map(
        functools.partial(per_device, mesh.shape["member"], mesh.shape["tower"]),
        mesh=mesh,
        in_specs=placed,
        out_specs=(
            P("tower", "member", None, None),
            P("tower", "member", None),
            P("member", "tower", None),
            P("member", "tower", None),
            P(("tower", "member"), None),
            P(("tower", "member"), None),
            P("member", "tower"),
        ),
        check_vma=False,
    )
```

```python
import functools
import math

import jax
import jax.numpy as jnp
from jax import lax
from jax.experimental import pallas as pl
from jax.experimental.pallas import tpu as pltpu
from jax.sharding import PartitionSpec as P

MESH = pl.DeviceIdType.MESH
DECAY_RATE = 0.98
LEARN_RATE = 1.0
EPSILON = 1e-08
F32 = jnp.float32
BF16 = jnp.bfloat16
NN = (((1,), (0,)), ((), ()))
NT = (((1,), (1,)), ((), ()))


def split(x):
    hi = x.astype(BF16)
    return hi, (x - hi.astype(F32)).astype(BF16)


def dot1(a, b, dims=NN):
    return lax.dot_general(a, b, dims, preferred_element_type=F32)


def few3(a, b, dims=NN):
    (ah, al), (bh, bl) = a, b
    both = dot1(jnp.concatenate([ah, al], axis=0), bh, dims)
    m = ah.shape[0]
    return both[:m] + (both[m:] + dot1(ah, bl, dims))


def deep3(a, b, dims=NN):
    (ah, al), (bh, bl) = a, b
    return dot1(
        jnp.concatenate([ah, al, ah], axis=1),
        jnp.concatenate([bh, bh, bl], axis=dims[0][1][0]),
        dims,
    )


def sigmoid(x):
    return 1.0 / (1.0 + jnp.exp(-x))


def main_kernel(
    dims,
    bag_ref,
    touch_ref,
    elapsed_ref,
    tables_ref,
    first_hbm,
    second_hbm,
    lift_hbm,
    press_hbm,
    head_ref,
    label_ref,
    logits_out,
    decayed_out,
    gt_out,
    gf_out,
    gsec_out,
    glp_out,
    stage,
    w1h,
    w1l,
    w2f,
    w2h,
    w2l,
    lift,
    press,
    mixh,
    mixl,
    cols,
    counts_ref,
    decayed,
    pool,
    feats,
    tout_send,
    tout_recv,
    stats,
    rs_buf,
    line,
    line_buf,
    gath,
    errs,
    act,
    acth,
    actl,
    pth,
    ptl,
    gf,
    gf_in,
    gsec,
    gsec_in,
    gpool,
    gpool_in,
    glp,
    glp_in,
    gt,
    logits,
    load_sem,
    store_sem,
    crit_send,
    mate_send,
    ag_send,
    relay_send,
    ag_recv,
    rs_send,
    rs_recv,
    to_send,
    to_recv,
    gm_send,
    gm_recv,
    gt_send,
    gt_recv,
    back_send,
    back_recv,
):
    n, nt = dims
    me = lax.axis_index("member")
    tpos = lax.axis_index("tower")
    towers, bags, total = bag_ref.shape
    width, rows = tables_ref.shape[1:]
    touches = touch_ref.shape[2]
    hid, outs = w2h.shape[1:]
    fin = w1h.shape[1]
    rank = lift.shape[1]
    flat = towers * outs
    chips = n // 2
    own = total // n
    half = own * chips
    piece = own // nt
    chunk = min(256, half)
    tile = min(256, hid)
    pair_hid = 2 * (hid // n)
    block_hid = hid // n
    pair_flat = flat // chips
    chip, core = me // 2, lax.rem(me, 2)
    mate = me + 1 - 2 * core

    loads = []

    def load(source, target):
        loads.append(pltpu.make_async_copy(source, target, load_sem.at[len(loads)]))
        loads[-1].start()

    for t in range(towers):
        load(first_hbm.at[:, t, :], stage.at[t, :fin])
    for t in range(towers):
        load(second_hbm.at[:, t, :], w2f.at[t])
    load(lift_hbm.at[pl.ds(tpos * flat, flat)], lift)
    load(press_hbm.at[pl.ds(tpos * flat, flat)], press)

    barrier = pltpu.get_barrier_semaphore()
    for d in range(1, n):
        pl.semaphore_signal(
            barrier, inc=1, device_id={"member": lax.rem(me + d, n)}, device_id_type=MESH
        )
    for d in range(1, nt):
        pl.semaphore_signal(
            barrier, inc=1, device_id={"tower": lax.rem(tpos + d, nt)}, device_id_type=MESH
        )

    stores = []

    def store(source, target):
        stores.append(pltpu.make_async_copy(source, target, store_sem.at[len(stores)]))
        stores[-1].start()

    def slice_at(index):
        return pl.ds(pl.multiple_of(index * own, own), own)

    stack = [bag_ref[t].astype(F32) for t in range(towers)]
    stack.append(jnp.zeros((128 - towers * bags, total), F32))
    cols[...] = jnp.concatenate(stack, axis=0).T
    stack = []
    for t in range(towers):
        stack.append(touch_ref[t].astype(F32))
        stack.append(jnp.exp(elapsed_ref[t].astype(F32) * math.log(DECAY_RATE)))
    stack.append(jnp.zeros((128 - 2 * towers, touches), F32))
    owed = jnp.concatenate(stack, axis=0).T
    pairs = []
    place = lax.broadcasted_iota(jnp.int32, (touches, rows), 1).astype(F32)
    for t in range(towers):
        ids, rates = owed[:, 2 * t : 2 * t + 1], owed[:, 2 * t + 1 : 2 * t + 2]
        chosen = jnp.sum(jnp.where(place == ids, rates, 0.0), axis=0, keepdims=True)
        value = tables_ref[t] * jnp.where(chosen > 0.0, chosen, 1.0)
        decayed[t] = value
        pairs.append(jnp.concatenate(split(value), axis=0))
    out = jnp.where(chip < chips // 2, -1, 1)
    near_end = (chip == 1) | (chip == chips - 2)

    def own_copy(there, k, s, semaphore):
        at = slice_at(s)
        return pltpu.make_async_remote_copy(
            src_ref=pool.at[k, at],
            dst_ref=feats.at[me, at],
            send_sem=semaphore,
            recv_sem=ag_recv.at[chip, s],
            device_id={"member": 2 * there + k},
            device_id_type=MESH,
        )

    def mate_copy():
        return pltpu.make_async_remote_copy(
            src_ref=pool.at[1 - core],
            dst_ref=feats.at[me],
            send_sem=mate_send.at[0],
            recv_sem=ag_recv.at[chip, 0],
            device_id={"member": mate},
            device_id_type=MESH,
        )

    def pair_copy(source, s, semaphore):
        pair, at = pl.ds(2 * source, 2), slice_at(s)
        return pltpu.make_async_remote_copy(
            src_ref=feats.at[pair, at],
            dst_ref=feats.at[pair, at],
            send_sem=semaphore,
            recv_sem=ag_recv.at[source, s],
            device_id={"member": 2 * lax.rem(chip + out + chips, chips) + core},
            device_id_type=MESH,
        )

    def slice_from(there, sign, j):
        return lax.rem(there + chips + sign * j, chips)

    def whole_copies(there, semaphore):
        towards = jnp.where(there < chips // 2, -1, 1)
        return [
            own_copy(there, k, slice_from(there, towards, j), semaphore)
            for j in range(chips - 1, 0, -1)
            for k in range(2)
        ]

    def end_each(act_on):
        @pl.when(near_end)
        def _():
            act_on(chip + out, ag_send.at[0, 0])

    def inner_each(hops, act_on):
        for sign in (-1, 1):
            for i in hops:
                there = chip + sign * out * i

                @pl.when((there > 0) & (there < chips - 1))
                def _():
                    act_on(there, ag_send.at[(1 + sign) // 2, i])

    def start_all(there, semaphore):
        for copy in whole_copies(there, semaphore):
            copy.start()

    def own_arrives(i):
        pair_copy(lax.rem(chip + i, chips), chip, relay_send.at[0]).wait_recv()

    def relay(d, part):
        @pl.when(near_end)
        def _():
            for j in part:
                copy = pair_copy(chip - out * d, slice_from(chip, out, j), relay_send.at[d - 1])
                if j:
                    copy.wait_recv()
                copy.start()

    def rest_arrives(i):
        source = lax.rem(chip + i, chips)
        pair_copy(source, slice_from(chip, out, 1), relay_send.at[0]).wait_recv()

        @pl.when(jnp.logical_not(near_end) | (source == chip + out))
        def _():
            for j in range(2, chips):
                pair_copy(source, slice_from(chip, out, j), relay_send.at[0]).wait_recv()

    order = sorted(range(1, chips), key=lambda i: -min(i, chips - i))
    place = lax.broadcasted_iota(jnp.int32, (2 * own, rows), 1).astype(F32)

    def count(there):
        span = pl.ds(pl.multiple_of(there * 2 * own, 2 * own), 2 * own)
        found = []
        for t in range(towers):
            counts = jnp.zeros((2 * own, rows), F32)
            for b in range(bags):
                k = t * bags + b
                counts = counts + jnp.where(place == cols[span, k : k + 1], 1.0, 0.0)
            counts = counts.astype(BF16)
            for k in range(2):
                counts_ref[t, k, slice_at(there), :] = counts[k * own : (k + 1) * own]
            found.append(counts)
        return found

    mirrored = jnp.where(chip < chips // 2, chip, chips - 1 - chip)
    stops = [chips // 2 + i for i in range(chips // 2)]
    stops += [lax.rem(mirrored + i, chips // 2) for i in range(1, chips // 2 + 1)]
    stops = [jnp.where(chip < chips // 2, stop, chips - 1 - stop) for stop in stops]
    found = count(stops[0])
    for i, there in enumerate(stops):
        both = [dot1(counts, pairs[t], NT) for t, counts in enumerate(found)]
        if i + 1 < chips:
            found = count(stops[i + 1])
        pooled = jnp.concatenate([x[:, :width] + x[:, width:] for x in both], axis=1)
        for k in range(2):
            pool[k, slice_at(there), :] = pooled[k * own : (k + 1) * own]
        if i == 0:
            pl.semaphore_wait(barrier, n - 1 + nt - 1)
        if i + 1 < chips:
            for k in range(2):
                own_copy(there, k, there, crit_send.at[0]).start()

        @pl.when(near_end & (there != chip + out))
        def _():
            for k in range(2):
                own_copy(chip + out, k, there, ag_send.at[0, 0]).start()

    mate_copy().start()
    feats[me] = pool[core]

    for copy in loads[:towers]:
        copy.wait()
    for t in range(towers):

        @pl.loop(0, fin // 64)
        def _(i):
            span = pl.ds(pl.multiple_of(i * 64, 64), 64)
            w1h[t, span, :], w1l[t, span, :] = split(stage[t, span, :])

    inner_each([1], start_all)
    for copy in loads[towers:]:
        copy.wait()
    for t in range(towers):

        @pl.loop(0, hid // 128)
        def _(i):
            span = pl.ds(pl.multiple_of(i * 128, 128), 128)
            w2h[t, span, :], w2l[t, span, :] = split(w2f[t, span, :])

    head = head_ref[:, pl.ds(pl.multiple_of(tpos * flat, flat), flat)]
    mixh[...], mixl[...] = split(jnp.concatenate([lift[...].T * head, press[...].T], axis=0))
    store(decayed, decayed_out)

    mate_copy().wait_recv()
    for i in range(1, chips):
        own_arrives(i)
    inner_each(range(2, chips - 1), start_all)
    for d in range(1, chips - 1):
        relay(d, [0])
    flat_out = []
    for t in range(towers):
        part = slice(t * width, (t + 1) * width)
        x = jnp.concatenate([feats[b, slice_at(chip), part] for b in range(n)], axis=1)
        h = few3(split(x), (w1h[t], w1l[t]))
        flat_out.append(few3(split(h * sigmoid(h)), (w2h[t], w2l[t])))
    flat_out = jnp.concatenate(flat_out, axis=1)
    stats[...] = few3(split(flat_out), (mixh[...], mixl[...]), NT).reshape(nt, piece, 2 * rank)
    linear = jnp.sum(flat_out * head, axis=1, keepdims=True)
    seat = lax.broadcasted_iota(jnp.int32, (piece, rank), 1)
    wanted = lax.broadcasted_iota(jnp.int32, (piece, rank), 0)
    for k in range(nt):
        row = jnp.where(seat == wanted, linear[k * piece : (k + 1) * piece], 0.0)
        line[k] = jnp.sum(row, axis=0, keepdims=True)

    def tower_copies(d):
        other = lax.rem(tpos + d, nt)
        return [
            pltpu.make_async_remote_copy(
                src_ref=ref.at[other],
                dst_ref=buf.at[tpos],
                send_sem=rs_send.at[k],
                recv_sem=rs_recv.at[k, d - 1],
                device_id={"tower": other},
                device_id_type=MESH,
            )
            for k, (ref, buf) in enumerate(((line, line_buf), (stats, rs_buf)))
        ]

    for d in range(1, nt):
        for copy in tower_copies(d):
            copy.start()

    for c in range(chips):
        tout_send[c] = flat_out[:, c * pair_flat : (c + 1) * pair_flat]
    tout_recv[chip] = tout_send[chip]

    def tout_copy(i):
        there = lax.rem(chip + i, chips)
        return pltpu.make_async_remote_copy(
            src_ref=tout_send.at[there],
            dst_ref=tout_recv.at[chip],
            send_sem=to_send.at[0],
            recv_sem=to_recv.at[i - 1],
            device_id={"member": 2 * there + core},
            device_id_type=MESH,
        )

    def member_copies(i, there):
        return [
            pltpu.make_async_remote_copy(
                src_ref=ref.at[chip, tpos],
                dst_ref=ref.at[chip, tpos],
                send_sem=gm_send.at[k],
                recv_sem=gm_recv.at[k, i - 1],
                device_id={"member": 2 * there + core},
                device_id_type=MESH,
            )
            for k, ref in enumerate((errs, gath))
        ]

    def column_copies(d, source, count):
        where = pl.ds(source, count)
        return [
            pltpu.make_async_remote_copy(
                src_ref=ref.at[where, tpos],
                dst_ref=ref.at[where, tpos],
                send_sem=gt_send.at[k],
                recv_sem=gt_recv.at[k, d - 1],
                device_id={"tower": lax.rem(tpos + d, nt)},
                device_id_type=MESH,
            )
            for k, ref in enumerate((errs, gath))
        ]

    def column_start(source):
        for d in range(1, nt):
            for copy in column_copies(d, source, 1):
                copy.start()

    relay(1, range(chips - 1, 1, -1))
    beside = 1 - 2 * lax.rem(chip, 2)
    rest_arrives(beside + chips)
    per = 4
    together = per * width

    def hidden_group(t, c, g):
        part = slice(t * width, (t + 1) * width)
        span = slice(c * chunk, (c + 1) * chunk)
        x = jnp.concatenate([feats[per * g + k, span, part] for k in range(per)], axis=1)
        x = split(x)
        ins = pl.ds(pl.multiple_of(g * together, together), together)
        for k in range(hid // tile):
            lanes = slice(k * tile, (k + 1) * tile)
            yield lanes, deep3(x, (w1h[t, ins, lanes], w1l[t, ins, lanes]))

    near = chip // 2
    for t in range(towers):
        for c in range(half // chunk):
            span = slice(c * chunk, (c + 1) * chunk)
            for lanes, value in hidden_group(t, c, near):
                stage[t, span, lanes] = value

    for d in range(1, nt):
        for copy in tower_copies(d):
            copy.wait_recv()
    summed, linear = stats[tpos], line[tpos]
    for d in range(1, nt):
        summed = summed + rs_buf[lax.rem(tpos + d, nt)]
        linear = linear + line_buf[lax.rem(tpos + d, nt)]
    scaled, projected = summed[:, :rank], summed[:, rank:]
    linear = jnp.sum(jnp.where(seat == wanted, linear, 0.0), axis=1, keepdims=True)
    logit = jnp.sum(projected * scaled, axis=1, keepdims=True) + linear
    logit = jnp.broadcast_to(logit, (piece, rank))
    logits[...] = logit
    place = lax.broadcasted_iota(jnp.int32, (piece, own), 1)
    mine = lax.broadcasted_iota(jnp.int32, (piece, own), 0) + tpos * piece
    clicks = jnp.where(place == mine, label_ref[...].astype(F32), 0.0)
    error = sigmoid(logit) - jnp.sum(clicks, axis=1, keepdims=True)
    gath[chip, tpos, :, :rank] = error * projected
    gath[chip, tpos, :, rank:] = error * scaled
    errs[chip, tpos] = jnp.sum(jnp.where(seat == wanted, error, 0.0), axis=0, keepdims=True)
    for i in order:
        for copy in member_copies(i, lax.rem(chip + i, chips)):
            copy.start()
    column_start(chip)
    store(logits, logits_out)

    for d in range(2, chips - 1):
        relay(d, range(chips - 1, 1, -1))
    for source in sorted(range(chips), key=lambda c: -min(c, chips - 1 - c)):

        @pl.when(chip != source)
        def _():
            for copy in member_copies(lax.rem(chip + chips - source, chips), source):
                copy.wait_recv()
            column_start(source)

    for i in range(1, chips):
        pl.when(lax.rem(chip + i, chips) != chip + beside)(functools.partial(rest_arrives, i))

    start = pl.multiple_of(chip * pair_hid, pair_hid)
    groups = n // per
    for t in range(towers):
        part = slice(t * width, (t + 1) * width)
        for c in range(half // chunk):
            span = slice(c * chunk, (c + 1) * chunk)
            for i in range(1, groups):
                for lanes, value in hidden_group(t, c, lax.rem(near + i, groups)):
                    h = stage[t, span, lanes] + value
                    if i < groups - 1:
                        stage[t, span, lanes] = h
                    else:
                        sig = sigmoid(h)
                        a = h * sig
                        act[span, lanes] = a
                        stage[t, span, lanes] = sig + a * (1.0 - sig)
            both = jnp.concatenate([feats[2 * chip + k, span, part] for k in range(2)], axis=1)
            pth[t, :, span], ptl[t, :, span] = split(both.T)
            acth[t, :, span], actl[t, :, span] = split(act[span, pl.ds(start, pair_hid)].T)

    def sent(ref, semaphore):
        pltpu.make_async_remote_copy(
            src_ref=ref,
            dst_ref=ref,
            send_sem=semaphore,
            recv_sem=ag_recv.at[0, 0],
            device_id={"member": mate},
            device_id_type=MESH,
        ).wait_send()

    sent(pool.at[0], mate_send.at[0])
    for k, ref in enumerate((line, stats)):
        sent(ref.at[: nt - 1], rs_send.at[k])
    sent(feats.at[:2, : half - own], crit_send.at[0])
    def sent_all(there, semaphore):
        sent(pool.at[:, : half - own], semaphore)

    end_each(sent_all)
    inner_each(range(1, chips - 1), sent_all)

    @pl.when(near_end)
    def _():
        for d in range(1, chips - 1):
            sent(feats.at[:2, : half - own], relay_send.at[d - 1])

    for i in order:
        tout_copy(i).start()
    for d in range(1, nt):
        for copy in column_copies(d, 0, chips):
            copy.wait_recv()
    for k, ref in enumerate((errs, gath)):
        sent(ref.at[: chips - 1, 0], gm_send.at[k])
        sent(ref.at[:, : nt - 1], gt_send.at[k])

    def back_copy(slot, source, target):
        return pltpu.make_async_remote_copy(
            src_ref=source,
            dst_ref=target,
            send_sem=back_send.at[slot],
            recv_sem=back_recv.at[slot],
            device_id={"member": mate},
            device_id_type=MESH,
        )

    def rows_of(which, size):
        return pl.ds(pl.multiple_of(which * size, size), size)

    def back_copies(t):
        return [
            back_copy(3 * t, gpool.at[t, rows_of(1 - core, width)], gpool_in.at[t]),
            back_copy(3 * t + 1, gf.at[t, rows_of(1 - core, width)], gf_in.at[t]),
            back_copy(3 * t + 2, gsec.at[t, rows_of(1 - core, block_hid)], gsec_in.at[t]),
        ]

    def lift_copy():
        return back_copy(3 * towers, glp.at[rows_of(1 - core, pair_flat // 2)], glp_in)

    def put(ref, index, value, fresh):
        if fresh:
            ref[index] = value
        else:
            ref[index] += value

    errors = jnp.concatenate(
        [
            jnp.broadcast_to(errs[c, t], (piece, rank))
            for c in range(chips)
            for t in range(nt)
        ],
        axis=0,
    )
    seat = lax.broadcasted_iota(jnp.int32, (half, rank), 1)
    wanted = lax.rem(lax.broadcasted_iota(jnp.int32, (half, rank), 0), piece)
    errors = jnp.sum(jnp.where(seat == wanted, errors, 0.0), axis=1, keepdims=True)
    pair_rows = pl.ds(pl.multiple_of(chip * 2 * width, 2 * width), 2 * width)
    for t in range(towers):
        part = slice(t * outs, (t + 1) * outs)
        for c in range(half // chunk):
            span = slice(c * chunk, (c + 1) * chunk)
            here = slice(c * (chunk // own), (c + 1) * (chunk // own))
            block = gath[here].reshape(chunk, 2 * rank)
            go = split(
                errors[span] * head[:, part]
                + deep3(split(block), (mixh[:, part], mixl[:, part]))
            )
            grad_pooled = jnp.zeros((2 * width, chunk), F32)
            for k in range(hid // tile):
                lanes = slice(k * tile, (k + 1) * tile)
                grad_act = deep3(go, (w2h[t, lanes, :], w2l[t, lanes, :]), NT)
                grad_hidden = split(grad_act * stage[t, span, lanes])
                value = deep3((pth[t, :, span], ptl[t, :, span]), grad_hidden)
                put(gf, (t, slice(None), lanes), value, c == 0)
                first = (w1h[t, pair_rows, lanes], w1l[t, pair_rows, lanes])
                grad_pooled = grad_pooled + deep3(first, grad_hidden, NT)
            gpool[t, :, span] = grad_pooled
            put(gsec, (t,), deep3((acth[t, :, span], actl[t, :, span]), go), c == 0)
        for copy in back_copies(t):
            copy.start()

    for i in order:
        tout_copy(i).wait_recv()
    sent(tout_send.at[: chips - 1], to_send.at[0])
    outputs = jnp.concatenate([tout_recv[c] for c in range(chips)], axis=0)
    block = gath[...].reshape(half, 2 * rank)
    value = deep3(split(outputs.T), split(block))
    seat = lax.broadcasted_iota(jnp.int32, (pair_flat, flat), 1)
    wanted = lax.broadcasted_iota(jnp.int32, (pair_flat, flat), 0) + chip * pair_flat
    weights = jnp.sum(jnp.where(seat == wanted, head, 0.0), axis=1, keepdims=True)
    glp[:, :rank] = weights * value[:, :rank]
    glp[:, rank:] = value[:, rank:]
    lift_copy().start()

    for t in range(towers):
        from_mate = back_copies(t)
        mine = jnp.concatenate(split(gpool[t, rows_of(core, width), :]), axis=0)
        both = dot1(mine, counts_ref[t, core])
        from_mate[0].wait_recv()
        theirs = jnp.concatenate(split(gpool_in[t]), axis=0)
        both = both + dot1(theirs, counts_ref[t, 1 - core])
        gt[t] = both[:width] + both[width:]
        store(gt.at[t], gt_out.at[t])
        from_mate[1].wait_recv()
        gf_in[t] += gf[t, rows_of(core, width), :]
        store(gf_in.at[t], gf_out.at[t])
        from_mate[2].wait_recv()
        gsec_in[t] += gsec[t, rows_of(core, block_hid), :]
        store(gsec_in.at[t], gsec_out.at[t])
    lift_copy().wait_recv()
    glp_in[...] += glp[rows_of(core, pair_flat // 2), :]
    store(glp_in, glp_out)

    for t in range(towers):
        for copy in back_copies(t):
            copy.wait_send()
    lift_copy().wait_send()
    for copy in stores:
        copy.wait()


def final_kernel(
    logits_ref,
    decayed_ref,
    gt_ref,
    gf_ref,
    gsec_ref,
    glp_ref,
    acc_ref,
    new_tables_ref,
    new_acc_ref,
    grad_first_ref,
    grad_second_ref,
    grad_lift_ref,
    grad_press_ref,
    logits_out_ref,
):
    rank = logits_ref.shape[1]
    for t in range(gt_ref.shape[0]):
        grad_second_ref[:, t, :] = gsec_ref[t]
        grad_first_ref[:, t, :] = gf_ref[t]
        g = gt_ref[t]
        value = acc_ref[t] + jnp.mean(g * g, axis=0, keepdims=True)
        new_acc_ref[t] = value
        new_tables_ref[t] = decayed_ref[t] - LEARN_RATE * g / (jnp.sqrt(value) + EPSILON)
    grad_lift_ref[...] = glp_ref[:, :rank]
    grad_press_ref[...] = glp_ref[:, rank:]
    piece = logits_ref.shape[0]
    place = lax.broadcasted_iota(jnp.int32, (piece, piece), 1)
    wanted = lax.broadcasted_iota(jnp.int32, (piece, piece), 0)
    values = jnp.where(place == wanted, logits_ref[:, :1], 0.0)
    logits_out_ref[...] = jnp.sum(values, axis=0, keepdims=True)


def per_device(n, nt, *args):
    bag_ids, touch_ids, elapsed, tables, accumulator, first, second, lift, press, head, labels = args
    towers, _, bags, total = bag_ids.shape
    rows, width = tables.shape[2:]
    fin, _, hid = first.shape
    outs = second.shape[2]
    rank = lift.shape[1]
    flat = towers * outs
    chips = n // 2
    own = total // n
    half = own * chips
    piece = own // nt
    block_hid = hid // n
    pair_flat = flat // chips
    lanes = towers * width
    vmem = pl.BlockSpec(memory_space=pltpu.VMEM)
    anys = pl.BlockSpec(memory_space=pl.ANY)
    sem = pltpu.SemaphoreType.DMA
    shape = jax.ShapeDtypeStruct
    between = pl.pallas_call(
        functools.partial(main_kernel, (n, nt)),
        out_shape=(
            shape((piece, rank), F32),
            shape((towers, width, rows), F32),
            shape((towers, width, rows), F32),
            shape((towers, width, hid), F32),
            shape((towers, block_hid, outs), F32),
            shape((pair_flat // 2, 2 * rank), F32),
        ),
        in_specs=[vmem] * 4 + [anys] * 4 + [vmem] * 2,
        out_specs=[anys] * 6,
        scratch_shapes=[
            pltpu.VMEM((towers, max(half, fin), hid), F32),
            pltpu.VMEM((towers, fin, hid), BF16),
            pltpu.VMEM((towers, fin, hid), BF16),
            pltpu.VMEM((towers, hid, outs), F32),
            pltpu.VMEM((towers, hid, outs), BF16),
            pltpu.VMEM((towers, hid, outs), BF16),
            pltpu.VMEM((flat, rank), F32),
            pltpu.VMEM((flat, rank), F32),
            pltpu.VMEM((2 * rank, flat), BF16),
            pltpu.VMEM((2 * rank, flat), BF16),
            pltpu.VMEM((total, 128), F32),
            pltpu.VMEM((towers, 2, half, rows), BF16),
            pltpu.VMEM((towers, width, rows), F32),
            pltpu.VMEM((2, half, lanes), F32),
            pltpu.VMEM((n, half, lanes), F32),
            pltpu.VMEM((chips, own, pair_flat), F32),
            pltpu.VMEM((chips, own, pair_flat), F32),
            pltpu.VMEM((nt, piece, 2 * rank), F32),
            pltpu.VMEM((nt, piece, 2 * rank), F32),
            pltpu.VMEM((nt, 1, rank), F32),
            pltpu.VMEM((nt, 1, rank), F32),
            pltpu.VMEM((chips, nt, piece, 2 * rank), F32),
            pltpu.VMEM((chips, nt, 1, rank), F32),
            pltpu.VMEM((half, hid), F32),
            pltpu.VMEM((towers, 2 * block_hid, half), BF16),
            pltpu.VMEM((towers, 2 * block_hid, half), BF16),
            pltpu.VMEM((towers, 2 * width, half), BF16),
            pltpu.VMEM((towers, 2 * width, half), BF16),
            pltpu.VMEM((towers, 2 * width, hid), F32),
            pltpu.VMEM((towers, width, hid), F32),
            pltpu.VMEM((towers, 2 * block_hid, outs), F32),
            pltpu.VMEM((towers, block_hid, outs), F32),
            pltpu.VMEM((towers, 2 * width, half), F32),
            pltpu.VMEM((towers, width, half), F32),
            pltpu.VMEM((pair_flat, 2 * rank), F32),
            pltpu.VMEM((pair_flat // 2, 2 * rank), F32),
            pltpu.VMEM((towers, width, rows), F32),
            pltpu.VMEM((piece, rank), F32),
            sem((2 * towers + 2,)),
            sem((3 + 3 * towers,)),
            sem((1,)),
            sem((1,)),
            sem((2, chips - 1)),
            sem((chips - 2,)),
            sem((chips, chips)),
            sem((2,)),
            sem((2, nt - 1)),
            sem((1,)),
            sem((chips - 1,)),
            sem((2,)),
            sem((2, chips - 1)),
            sem((2,)),
            sem((2, nt - 1)),
            sem((3 * towers + 1,)),
            sem((3 * towers + 1,)),
        ],
        compiler_params=pltpu.CompilerParams(
            collective_id=0, has_side_effects=True, vmem_limit_bytes=67043328
        ),
    )(
        bag_ids[:, 0],
        touch_ids,
        elapsed,
        jnp.transpose(tables[:, 0], (0, 2, 1)),
        first,
        second,
        lift,
        press,
        head[None, :],
        labels,
    )
    out = pl.pallas_call(
        final_kernel,
        out_shape=(
            shape((towers, width, rows), F32),
            shape((towers, 1, rows), F32),
            shape((width, towers, hid), F32),
            shape((block_hid, towers, outs), F32),
            shape((flat // n, rank), F32),
            shape((flat // n, rank), F32),
            shape((1, piece), F32),
        ),
        in_specs=[vmem] * 7,
        out_specs=[vmem] * 7,
    )(*between, accumulator)
    new_tables, new_acc, grad_first, grad_second, grad_lift, grad_press, logits = out
    return (
        jnp.transpose(new_tables, (0, 2, 1))[:, None],
        new_acc,
        grad_first,
        grad_second,
        grad_lift,
        grad_press,
        logits,
    )


def solution(mesh):
    placed = (
        P("tower", "member", None, None),
        P("tower", "member", None),
        P("tower", "member", None),
        P("tower", "member", None, None),
        P("tower", "member", None),
        P(None, "tower", None),
        P(None, "tower", None),
        P(),
        P(),
        P(),
        P("member", None),
    )
    return jax.shard_map(
        functools.partial(per_device, mesh.shape["member"], mesh.shape["tower"]),
        mesh=mesh,
        in_specs=placed,
        out_specs=(
            P("tower", "member", None, None),
            P("tower", "member", None),
            P("member", "tower", None),
            P("member", "tower", None),
            P(("tower", "member"), None),
            P(("tower", "member"), None),
            P("member", "tower"),
        ),
        check_vma=False,
    )
```

```python
import functools
import math

import jax
import jax.numpy as jnp
from jax import lax
from jax.experimental import pallas as pl
from jax.experimental.pallas import tpu as pltpu
from jax.sharding import PartitionSpec as P

MESH = pl.DeviceIdType.MESH
DECAY_RATE = 0.98
LEARN_RATE = 1.0
EPSILON = 1e-08
F32 = jnp.float32
BF16 = jnp.bfloat16
NN = (((1,), (0,)), ((), ()))
NT = (((1,), (1,)), ((), ()))


def split(x):
    hi = x.astype(BF16)
    return hi, (x - hi.astype(F32)).astype(BF16)


def dot1(a, b, dims=NN):
    return lax.dot_general(a, b, dims, preferred_element_type=F32)


def few3(a, b, dims=NN):
    (ah, al), (bh, bl) = a, b
    both = dot1(jnp.concatenate([ah, al], axis=0), bh, dims)
    m = ah.shape[0]
    return both[:m] + (both[m:] + dot1(ah, bl, dims))


def deep3(a, b, dims=NN):
    (ah, al), (bh, bl) = a, b
    return dot1(
        jnp.concatenate([ah, al, ah], axis=1),
        jnp.concatenate([bh, bh, bl], axis=dims[0][1][0]),
        dims,
    )


def sigmoid(x):
    return 1.0 / (1.0 + jnp.exp(-x))


def main_kernel(
    dims,
    bag_ref,
    touch_ref,
    elapsed_ref,
    tables_ref,
    first_hbm,
    second_hbm,
    lift_hbm,
    press_hbm,
    head_ref,
    label_ref,
    logits_out,
    decayed_out,
    gt_out,
    gf_out,
    gsec_out,
    glp_out,
    stage,
    w1h,
    w1l,
    w2f,
    w2h,
    w2l,
    lift,
    press,
    mixh,
    mixl,
    cols,
    counts_ref,
    pool,
    feats,
    tout_send,
    tout_recv,
    stats,
    rs_buf,
    line,
    line_buf,
    gath,
    errs,
    act,
    acth,
    actl,
    pth,
    ptl,
    gf,
    gf_in,
    gsec,
    gsec_in,
    gpool,
    gpool_in,
    glp,
    glp_in,
    load_sem,
    crit_send,
    mate_send,
    ag_send,
    relay_send,
    ag_recv,
    rs_send,
    rs_recv,
    to_send,
    to_recv,
    gm_send,
    gm_recv,
    gt_send,
    gt_recv,
    back_send,
    back_recv,
):
    n, nt = dims
    me = lax.axis_index("member")
    tpos = lax.axis_index("tower")
    towers, bags, total = bag_ref.shape
    width, rows = tables_ref.shape[1:]
    touches = touch_ref.shape[2]
    hid, outs = w2h.shape[1:]
    fin = w1h.shape[1]
    rank = lift.shape[1]
    flat = towers * outs
    chips = n // 2
    own = total // n
    half = own * chips
    piece = own // nt
    chunk = min(256, half)
    tile = min(256, hid)
    pair_hid = 2 * (hid // n)
    block_hid = hid // n
    pair_flat = flat // chips
    chip, core = me // 2, lax.rem(me, 2)
    mate = me + 1 - 2 * core

    loads = []

    def load(source, target):
        loads.append(pltpu.make_async_copy(source, target, load_sem.at[len(loads)]))
        loads[-1].start()

    for t in range(towers):
        load(first_hbm.at[:, t, :], stage.at[t, :fin])
    for t in range(towers):
        load(second_hbm.at[:, t, :], w2f.at[t])
    load(lift_hbm.at[pl.ds(tpos * flat, flat)], lift)
    load(press_hbm.at[pl.ds(tpos * flat, flat)], press)

    barrier = pltpu.get_barrier_semaphore()
    for d in range(1, n):
        pl.semaphore_signal(
            barrier, inc=1, device_id={"member": lax.rem(me + d, n)}, device_id_type=MESH
        )
    for d in range(1, nt):
        pl.semaphore_signal(
            barrier, inc=1, device_id={"tower": lax.rem(tpos + d, nt)}, device_id_type=MESH
        )

    def slice_at(index):
        return pl.ds(pl.multiple_of(index * own, own), own)

    stack = [bag_ref[t].astype(F32) for t in range(towers)]
    stack.append(jnp.zeros((128 - towers * bags, total), F32))
    cols[...] = jnp.concatenate(stack, axis=0).T
    stack = []
    for t in range(towers):
        stack.append(touch_ref[t].astype(F32))
        stack.append(jnp.exp(elapsed_ref[t].astype(F32) * math.log(DECAY_RATE)))
    stack.append(jnp.zeros((128 - 2 * towers, touches), F32))
    owed = jnp.concatenate(stack, axis=0).T
    pairs = []
    place = lax.broadcasted_iota(jnp.int32, (touches, rows), 1).astype(F32)
    for t in range(towers):
        ids, rates = owed[:, 2 * t : 2 * t + 1], owed[:, 2 * t + 1 : 2 * t + 2]
        chosen = jnp.sum(jnp.where(place == ids, rates, 0.0), axis=0, keepdims=True)
        value = tables_ref[t] * jnp.where(chosen > 0.0, chosen, 1.0)
        decayed_out[t] = value
        pairs.append(jnp.concatenate(split(value), axis=0))
    out = jnp.where(chip < chips // 2, -1, 1)
    near_end = (chip == 1) | (chip == chips - 2)

    def own_copy(there, k, s, semaphore):
        at = slice_at(s)
        return pltpu.make_async_remote_copy(
            src_ref=pool.at[k, at],
            dst_ref=feats.at[me, at],
            send_sem=semaphore,
            recv_sem=ag_recv.at[chip, s],
            device_id={"member": 2 * there + k},
            device_id_type=MESH,
        )

    def mate_copy():
        return pltpu.make_async_remote_copy(
            src_ref=pool.at[1 - core],
            dst_ref=feats.at[me],
            send_sem=mate_send.at[0],
            recv_sem=ag_recv.at[chip, 0],
            device_id={"member": mate},
            device_id_type=MESH,
        )

    def pair_copy(source, s, semaphore):
        pair, at = pl.ds(2 * source, 2), slice_at(s)
        return pltpu.make_async_remote_copy(
            src_ref=feats.at[pair, at],
            dst_ref=feats.at[pair, at],
            send_sem=semaphore,
            recv_sem=ag_recv.at[source, s],
            device_id={"member": 2 * lax.rem(chip + out + chips, chips) + core},
            device_id_type=MESH,
        )

    def slice_from(there, sign, j):
        return lax.rem(there + chips + sign * j, chips)

    def whole_copies(there, semaphore):
        towards = jnp.where(there < chips // 2, -1, 1)
        return [
            own_copy(there, k, slice_from(there, towards, j), semaphore)
            for j in range(chips - 1, 0, -1)
            for k in range(2)
        ]

    def end_each(act_on):
        @pl.when(near_end)
        def _():
            act_on(chip + out, ag_send.at[0, 0])

    def inner_each(hops, act_on):
        for sign in (-1, 1):
            for i in hops:
                there = chip + sign * out * i

                @pl.when((there > 0) & (there < chips - 1))
                def _():
                    act_on(there, ag_send.at[(1 + sign) // 2, i])

    def start_all(there, semaphore):
        for copy in whole_copies(there, semaphore):
            copy.start()

    def own_arrives(i):
        pair_copy(lax.rem(chip + i, chips), chip, relay_send.at[0]).wait_recv()

    def relay(d, part):
        @pl.when(near_end)
        def _():
            for j in part:
                copy = pair_copy(chip - out * d, slice_from(chip, out, j), relay_send.at[d - 1])
                if j:
                    copy.wait_recv()
                copy.start()

    def rest_arrives(i):
        source = lax.rem(chip + i, chips)
        pair_copy(source, slice_from(chip, out, 1), relay_send.at[0]).wait_recv()

        @pl.when(jnp.logical_not(near_end) | (source == chip + out))
        def _():
            for j in range(2, chips):
                pair_copy(source, slice_from(chip, out, j), relay_send.at[0]).wait_recv()

    order = sorted(range(1, chips), key=lambda i: -min(i, chips - i))
    place = lax.broadcasted_iota(jnp.int32, (2 * own, rows), 1).astype(F32)

    def count(there):
        span = pl.ds(pl.multiple_of(there * 2 * own, 2 * own), 2 * own)
        found = []
        for t in range(towers):
            counts = jnp.zeros((2 * own, rows), F32)
            for b in range(bags):
                k = t * bags + b
                counts = counts + jnp.where(place == cols[span, k : k + 1], 1.0, 0.0)
            counts = counts.astype(BF16)
            for k in range(2):
                counts_ref[t, k, slice_at(there), :] = counts[k * own : (k + 1) * own]
            found.append(counts)
        return found

    mirrored = jnp.where(chip < chips // 2, chip, chips - 1 - chip)
    stops = [chips // 2 + i for i in range(chips // 2)]
    stops += [lax.rem(mirrored + i, chips // 2) for i in range(1, chips // 2 + 1)]
    stops = [jnp.where(chip < chips // 2, stop, chips - 1 - stop) for stop in stops]
    found = count(stops[0])
    for i, there in enumerate(stops):
        both = [dot1(counts, pairs[t], NT) for t, counts in enumerate(found)]
        if i + 1 < chips:
            found = count(stops[i + 1])
        pooled = jnp.concatenate([x[:, :width] + x[:, width:] for x in both], axis=1)
        for k in range(2):
            pool[k, slice_at(there), :] = pooled[k * own : (k + 1) * own]
        if i == 0:
            pl.semaphore_wait(barrier, n - 1 + nt - 1)
        if i + 1 < chips:
            for k in range(2):
                own_copy(there, k, there, crit_send.at[0]).start()

        @pl.when(near_end & (there != chip + out))
        def _():
            for k in range(2):
                own_copy(chip + out, k, there, ag_send.at[0, 0]).start()

    mate_copy().start()
    feats[me] = pool[core]

    for copy in loads[:towers]:
        copy.wait()
    for t in range(towers):

        @pl.loop(0, fin // 64)
        def _(i):
            span = pl.ds(pl.multiple_of(i * 64, 64), 64)
            w1h[t, span, :], w1l[t, span, :] = split(stage[t, span, :])

    inner_each([1], start_all)
    for copy in loads[towers:]:
        copy.wait()
    for t in range(towers):

        @pl.loop(0, hid // 128)
        def _(i):
            span = pl.ds(pl.multiple_of(i * 128, 128), 128)
            w2h[t, span, :], w2l[t, span, :] = split(w2f[t, span, :])

    head = head_ref[:, pl.ds(pl.multiple_of(tpos * flat, flat), flat)]
    mixh[...], mixl[...] = split(jnp.concatenate([lift[...].T * head, press[...].T], axis=0))

    mate_copy().wait_recv()
    for i in range(1, chips):
        own_arrives(i)
    inner_each(range(2, chips - 1), start_all)
    for d in range(1, chips - 1):
        relay(d, [0])
    flat_out = []
    for t in range(towers):
        part = slice(t * width, (t + 1) * width)
        x = jnp.concatenate([feats[b, slice_at(chip), part] for b in range(n)], axis=1)
        h = few3(split(x), (w1h[t], w1l[t]))
        flat_out.append(few3(split(h * sigmoid(h)), (w2h[t], w2l[t])))
    flat_out = jnp.concatenate(flat_out, axis=1)
    stats[...] = few3(split(flat_out), (mixh[...], mixl[...]), NT).reshape(nt, piece, 2 * rank)
    linear = jnp.sum(flat_out * head, axis=1, keepdims=True)
    seat = lax.broadcasted_iota(jnp.int32, (piece, rank), 1)
    wanted = lax.broadcasted_iota(jnp.int32, (piece, rank), 0)
    for k in range(nt):
        row = jnp.where(seat == wanted, linear[k * piece : (k + 1) * piece], 0.0)
        line[k] = jnp.sum(row, axis=0, keepdims=True)

    def tower_copies(d):
        other = lax.rem(tpos + d, nt)
        return [
            pltpu.make_async_remote_copy(
                src_ref=ref.at[other],
                dst_ref=buf.at[tpos],
                send_sem=rs_send.at[k],
                recv_sem=rs_recv.at[k, d - 1],
                device_id={"tower": other},
                device_id_type=MESH,
            )
            for k, (ref, buf) in enumerate(((line, line_buf), (stats, rs_buf)))
        ]

    for d in range(1, nt):
        for copy in tower_copies(d):
            copy.start()

    for c in range(chips):
        tout_send[c] = flat_out[:, c * pair_flat : (c + 1) * pair_flat]
    tout_recv[chip] = tout_send[chip]

    def tout_copy(i):
        there = lax.rem(chip + i, chips)
        return pltpu.make_async_remote_copy(
            src_ref=tout_send.at[there],
            dst_ref=tout_recv.at[chip],
            send_sem=to_send.at[0],
            recv_sem=to_recv.at[i - 1],
            device_id={"member": 2 * there + core},
            device_id_type=MESH,
        )

    def member_copies(i, there):
        return [
            pltpu.make_async_remote_copy(
                src_ref=ref.at[chip, tpos],
                dst_ref=ref.at[chip, tpos],
                send_sem=gm_send.at[k],
                recv_sem=gm_recv.at[k, i - 1],
                device_id={"member": 2 * there + core},
                device_id_type=MESH,
            )
            for k, ref in enumerate((errs, gath))
        ]

    def column_copies(d, source, count):
        where = pl.ds(source, count)
        return [
            pltpu.make_async_remote_copy(
                src_ref=ref.at[where, tpos],
                dst_ref=ref.at[where, tpos],
                send_sem=gt_send.at[k],
                recv_sem=gt_recv.at[k, d - 1],
                device_id={"tower": lax.rem(tpos + d, nt)},
                device_id_type=MESH,
            )
            for k, ref in enumerate((errs, gath))
        ]

    def column_start(source):
        for d in range(1, nt):
            for copy in column_copies(d, source, 1):
                copy.start()

    relay(1, range(chips - 1, 1, -1))
    beside = 1 - 2 * lax.rem(chip, 2)
    rest_arrives(beside + chips)
    per = 4
    together = per * width

    def hidden_group(t, c, g):
        part = slice(t * width, (t + 1) * width)
        span = slice(c * chunk, (c + 1) * chunk)
        x = jnp.concatenate([feats[per * g + k, span, part] for k in range(per)], axis=1)
        x = split(x)
        ins = pl.ds(pl.multiple_of(g * together, together), together)
        for k in range(hid // tile):
            lanes = slice(k * tile, (k + 1) * tile)
            yield lanes, deep3(x, (w1h[t, ins, lanes], w1l[t, ins, lanes]))

    near = chip // 2
    for t in range(towers):
        for c in range(half // chunk):
            span = slice(c * chunk, (c + 1) * chunk)
            for lanes, value in hidden_group(t, c, near):
                stage[t, span, lanes] = value

    for d in range(1, nt):
        for copy in tower_copies(d):
            copy.wait_recv()
    summed, linear = stats[tpos], line[tpos]
    for d in range(1, nt):
        summed = summed + rs_buf[lax.rem(tpos + d, nt)]
        linear = linear + line_buf[lax.rem(tpos + d, nt)]
    scaled, projected = summed[:, :rank], summed[:, rank:]
    linear = jnp.sum(jnp.where(seat == wanted, linear, 0.0), axis=1, keepdims=True)
    logit = jnp.sum(projected * scaled, axis=1, keepdims=True) + linear
    logit = jnp.broadcast_to(logit, (piece, rank))
    logits_out[...] = logit
    place = lax.broadcasted_iota(jnp.int32, (piece, own), 1)
    mine = lax.broadcasted_iota(jnp.int32, (piece, own), 0) + tpos * piece
    clicks = jnp.where(place == mine, label_ref[...].astype(F32), 0.0)
    error = sigmoid(logit) - jnp.sum(clicks, axis=1, keepdims=True)
    gath[chip, tpos, :, :rank] = error * projected
    gath[chip, tpos, :, rank:] = error * scaled
    errs[chip, tpos] = jnp.sum(jnp.where(seat == wanted, error, 0.0), axis=0, keepdims=True)
    for i in order:
        for copy in member_copies(i, lax.rem(chip + i, chips)):
            copy.start()
    column_start(chip)

    for d in range(2, chips - 1):
        relay(d, range(chips - 1, 1, -1))
    for source in sorted(range(chips), key=lambda c: -min(c, chips - 1 - c)):

        @pl.when(chip != source)
        def _():
            for copy in member_copies(lax.rem(chip + chips - source, chips), source):
                copy.wait_recv()
            column_start(source)

    for i in range(1, chips):
        pl.when(lax.rem(chip + i, chips) != chip + beside)(functools.partial(rest_arrives, i))

    start = pl.multiple_of(chip * pair_hid, pair_hid)
    groups = n // per
    for t in range(towers):
        part = slice(t * width, (t + 1) * width)
        for c in range(half // chunk):
            span = slice(c * chunk, (c + 1) * chunk)
            for i in range(1, groups):
                for lanes, value in hidden_group(t, c, lax.rem(near + i, groups)):
                    h = stage[t, span, lanes] + value
                    if i < groups - 1:
                        stage[t, span, lanes] = h
                    else:
                        sig = sigmoid(h)
                        a = h * sig
                        act[span, lanes] = a
                        stage[t, span, lanes] = sig + a * (1.0 - sig)
            both = jnp.concatenate([feats[2 * chip + k, span, part] for k in range(2)], axis=1)
            pth[t, :, span], ptl[t, :, span] = split(both.T)
            acth[t, :, span], actl[t, :, span] = split(act[span, pl.ds(start, pair_hid)].T)

    def sent(ref, semaphore):
        pltpu.make_async_remote_copy(
            src_ref=ref,
            dst_ref=ref,
            send_sem=semaphore,
            recv_sem=ag_recv.at[0, 0],
            device_id={"member": mate},
            device_id_type=MESH,
        ).wait_send()

    sent(pool.at[0], mate_send.at[0])
    for k, ref in enumerate((line, stats)):
        sent(ref.at[: nt - 1], rs_send.at[k])
    sent(feats.at[:2, : half - own], crit_send.at[0])
    def sent_all(there, semaphore):
        sent(pool.at[:, : half - own], semaphore)

    end_each(sent_all)
    inner_each(range(1, chips - 1), sent_all)

    @pl.when(near_end)
    def _():
        for d in range(1, chips - 1):
            sent(feats.at[:2, : half - own], relay_send.at[d - 1])

    for i in order:
        tout_copy(i).start()
    for d in range(1, nt):
        for copy in column_copies(d, 0, chips):
            copy.wait_recv()
    for k, ref in enumerate((errs, gath)):
        sent(ref.at[: chips - 1, 0], gm_send.at[k])
        sent(ref.at[:, : nt - 1], gt_send.at[k])

    def back_copy(slot, source, target):
        return pltpu.make_async_remote_copy(
            src_ref=source,
            dst_ref=target,
            send_sem=back_send.at[slot],
            recv_sem=back_recv.at[slot],
            device_id={"member": mate},
            device_id_type=MESH,
        )

    def rows_of(which, size):
        return pl.ds(pl.multiple_of(which * size, size), size)

    def back_copies(t):
        return [
            back_copy(3 * t, gpool.at[t, rows_of(1 - core, width)], gpool_in.at[t]),
            back_copy(3 * t + 1, gf.at[t, rows_of(1 - core, width)], gf_in.at[t]),
            back_copy(3 * t + 2, gsec.at[t, rows_of(1 - core, block_hid)], gsec_in.at[t]),
        ]

    def lift_copy():
        return back_copy(3 * towers, glp.at[rows_of(1 - core, pair_flat // 2)], glp_in)

    def put(ref, index, value, fresh):
        if fresh:
            ref[index] = value
        else:
            ref[index] += value

    errors = jnp.concatenate(
        [
            jnp.broadcast_to(errs[c, t], (piece, rank))
            for c in range(chips)
            for t in range(nt)
        ],
        axis=0,
    )
    seat = lax.broadcasted_iota(jnp.int32, (half, rank), 1)
    wanted = lax.rem(lax.broadcasted_iota(jnp.int32, (half, rank), 0), piece)
    errors = jnp.sum(jnp.where(seat == wanted, errors, 0.0), axis=1, keepdims=True)
    pair_rows = pl.ds(pl.multiple_of(chip * 2 * width, 2 * width), 2 * width)
    for t in range(towers):
        part = slice(t * outs, (t + 1) * outs)
        for c in range(half // chunk):
            span = slice(c * chunk, (c + 1) * chunk)
            here = slice(c * (chunk // own), (c + 1) * (chunk // own))
            block = gath[here].reshape(chunk, 2 * rank)
            go = split(
                errors[span] * head[:, part]
                + deep3(split(block), (mixh[:, part], mixl[:, part]))
            )
            grad_pooled = jnp.zeros((2 * width, chunk), F32)
            for k in range(hid // tile):
                lanes = slice(k * tile, (k + 1) * tile)
                grad_act = deep3(go, (w2h[t, lanes, :], w2l[t, lanes, :]), NT)
                grad_hidden = split(grad_act * stage[t, span, lanes])
                value = few3((pth[t, :, span], ptl[t, :, span]), grad_hidden)
                put(gf, (t, slice(None), lanes), value, c == 0)
                first = (w1h[t, pair_rows, lanes], w1l[t, pair_rows, lanes])
                grad_pooled = grad_pooled + few3(first, grad_hidden, NT)
            gpool[t, :, span] = grad_pooled
            put(gsec, (t,), deep3((acth[t, :, span], actl[t, :, span]), go), c == 0)
        for copy in back_copies(t):
            copy.start()

    for i in order:
        tout_copy(i).wait_recv()
    sent(tout_send.at[: chips - 1], to_send.at[0])
    outputs = jnp.concatenate([tout_recv[c] for c in range(chips)], axis=0)
    block = gath[...].reshape(half, 2 * rank)
    value = deep3(split(outputs.T), split(block))
    seat = lax.broadcasted_iota(jnp.int32, (pair_flat, flat), 1)
    wanted = lax.broadcasted_iota(jnp.int32, (pair_flat, flat), 0) + chip * pair_flat
    weights = jnp.sum(jnp.where(seat == wanted, head, 0.0), axis=1, keepdims=True)
    glp[:, :rank] = weights * value[:, :rank]
    glp[:, rank:] = value[:, rank:]
    lift_copy().start()

    for t in range(towers):
        from_mate = back_copies(t)
        mine = jnp.concatenate(split(gpool[t, rows_of(core, width), :]), axis=0)
        both = dot1(mine, counts_ref[t, core])
        from_mate[0].wait_recv()
        theirs = jnp.concatenate(split(gpool_in[t]), axis=0)
        both = both + dot1(theirs, counts_ref[t, 1 - core])
        gt_out[t] = both[:width] + both[width:]
        from_mate[1].wait_recv()
        gf_out[t] = gf_in[t] + gf[t, rows_of(core, width), :]
        from_mate[2].wait_recv()
        gsec_out[t] = gsec_in[t] + gsec[t, rows_of(core, block_hid), :]
    lift_copy().wait_recv()
    glp_out[...] = glp_in[...] + glp[rows_of(core, pair_flat // 2), :]

    for t in range(towers):
        for copy in back_copies(t):
            copy.wait_send()
    lift_copy().wait_send()


def final_kernel(
    logits_ref,
    decayed_ref,
    gt_ref,
    gf_ref,
    gsec_ref,
    glp_ref,
    acc_ref,
    new_tables_ref,
    new_acc_ref,
    grad_first_ref,
    grad_second_ref,
    grad_lift_ref,
    grad_press_ref,
    logits_out_ref,
):
    rank = logits_ref.shape[1]
    for t in range(gt_ref.shape[0]):
        grad_second_ref[:, t, :] = gsec_ref[t]
        grad_first_ref[:, t, :] = gf_ref[t]
        g = gt_ref[t]
        value = acc_ref[t] + jnp.mean(g * g, axis=0, keepdims=True)
        new_acc_ref[t] = value
        new_tables_ref[t] = decayed_ref[t] - LEARN_RATE * g / (jnp.sqrt(value) + EPSILON)
    grad_lift_ref[...] = glp_ref[:, :rank]
    grad_press_ref[...] = glp_ref[:, rank:]
    piece = logits_ref.shape[0]
    place = lax.broadcasted_iota(jnp.int32, (piece, piece), 1)
    wanted = lax.broadcasted_iota(jnp.int32, (piece, piece), 0)
    values = jnp.where(place == wanted, logits_ref[:, :1], 0.0)
    logits_out_ref[...] = jnp.sum(values, axis=0, keepdims=True)


def per_device(n, nt, *args):
    bag_ids, touch_ids, elapsed, tables, accumulator, first, second, lift, press, head, labels = args
    towers, _, bags, total = bag_ids.shape
    rows, width = tables.shape[2:]
    fin, _, hid = first.shape
    outs = second.shape[2]
    rank = lift.shape[1]
    flat = towers * outs
    chips = n // 2
    own = total // n
    half = own * chips
    piece = own // nt
    block_hid = hid // n
    pair_flat = flat // chips
    lanes = towers * width
    vmem = pl.BlockSpec(memory_space=pltpu.VMEM)
    anys = pl.BlockSpec(memory_space=pl.ANY)
    sem = pltpu.SemaphoreType.DMA
    shape = jax.ShapeDtypeStruct
    between = pl.pallas_call(
        functools.partial(main_kernel, (n, nt)),
        out_shape=(
            pltpu.VMEM((piece, rank), F32),
            pltpu.VMEM((towers, width, rows), F32),
            pltpu.VMEM((towers, width, rows), F32),
            pltpu.VMEM((towers, width, hid), F32),
            pltpu.VMEM((towers, block_hid, outs), F32),
            pltpu.VMEM((pair_flat // 2, 2 * rank), F32),
        ),
        in_specs=[vmem] * 4 + [anys] * 4 + [vmem] * 2,
        out_specs=[vmem] * 6,
        scratch_shapes=[
            pltpu.VMEM((towers, max(half, fin), hid), F32),
            pltpu.VMEM((towers, fin, hid), BF16),
            pltpu.VMEM((towers, fin, hid), BF16),
            pltpu.VMEM((towers, hid, outs), F32),
            pltpu.VMEM((towers, hid, outs), BF16),
            pltpu.VMEM((towers, hid, outs), BF16),
            pltpu.VMEM((flat, rank), F32),
            pltpu.VMEM((flat, rank), F32),
            pltpu.VMEM((2 * rank, flat), BF16),
            pltpu.VMEM((2 * rank, flat), BF16),
            pltpu.VMEM((total, 128), F32),
            pltpu.VMEM((towers, 2, half, rows), BF16),
            pltpu.VMEM((2, half, lanes), F32),
            pltpu.VMEM((n, half, lanes), F32),
            pltpu.VMEM((chips, own, pair_flat), F32),
            pltpu.VMEM((chips, own, pair_flat), F32),
            pltpu.VMEM((nt, piece, 2 * rank), F32),
            pltpu.VMEM((nt, piece, 2 * rank), F32),
            pltpu.VMEM((nt, 1, rank), F32),
            pltpu.VMEM((nt, 1, rank), F32),
            pltpu.VMEM((chips, nt, piece, 2 * rank), F32),
            pltpu.VMEM((chips, nt, 1, rank), F32),
            pltpu.VMEM((half, hid), F32),
            pltpu.VMEM((towers, 2 * block_hid, half), BF16),
            pltpu.VMEM((towers, 2 * block_hid, half), BF16),
            pltpu.VMEM((towers, 2 * width, half), BF16),
            pltpu.VMEM((towers, 2 * width, half), BF16),
            pltpu.VMEM((towers, 2 * width, hid), F32),
            pltpu.VMEM((towers, width, hid), F32),
            pltpu.VMEM((towers, 2 * block_hid, outs), F32),
            pltpu.VMEM((towers, block_hid, outs), F32),
            pltpu.VMEM((towers, 2 * width, half), F32),
            pltpu.VMEM((towers, width, half), F32),
            pltpu.VMEM((pair_flat, 2 * rank), F32),
            pltpu.VMEM((pair_flat // 2, 2 * rank), F32),
            sem((2 * towers + 2,)),
            sem((1,)),
            sem((1,)),
            sem((2, chips - 1)),
            sem((chips - 2,)),
            sem((chips, chips)),
            sem((2,)),
            sem((2, nt - 1)),
            sem((1,)),
            sem((chips - 1,)),
            sem((2,)),
            sem((2, chips - 1)),
            sem((2,)),
            sem((2, nt - 1)),
            sem((3 * towers + 1,)),
            sem((3 * towers + 1,)),
        ],
        compiler_params=pltpu.CompilerParams(
            collective_id=0, has_side_effects=True, vmem_limit_bytes=64 * 10**6
        ),
    )(
        bag_ids[:, 0],
        touch_ids,
        elapsed,
        jnp.transpose(tables[:, 0], (0, 2, 1)),
        first,
        second,
        lift,
        press,
        head[None, :],
        labels,
    )
    out = pl.pallas_call(
        final_kernel,
        out_shape=(
            shape((towers, width, rows), F32),
            shape((towers, 1, rows), F32),
            shape((width, towers, hid), F32),
            shape((block_hid, towers, outs), F32),
            shape((flat // n, rank), F32),
            shape((flat // n, rank), F32),
            shape((1, piece), F32),
        ),
        in_specs=[vmem] * 7,
        out_specs=[vmem] * 7,
        compiler_params=pltpu.CompilerParams(vmem_limit_bytes=8 * 2**20),
    )(*(pltpu.with_memory_space_constraint(x, pltpu.VMEM) for x in between), accumulator)
    new_tables, new_acc, grad_first, grad_second, grad_lift, grad_press, logits = out
    return (
        jnp.transpose(new_tables, (0, 2, 1))[:, None],
        new_acc,
        grad_first,
        grad_second,
        grad_lift,
        grad_press,
        logits,
    )


def solution(mesh):
    placed = (
        P("tower", "member", None, None),
        P("tower", "member", None),
        P("tower", "member", None),
        P("tower", "member", None, None),
        P("tower", "member", None),
        P(None, "tower", None),
        P(None, "tower", None),
        P(),
        P(),
        P(),
        P("member", None),
    )
    return jax.shard_map(
        functools.partial(per_device, mesh.shape["member"], mesh.shape["tower"]),
        mesh=mesh,
        in_specs=placed,
        out_specs=(
            P("tower", "member", None, None),
            P("tower", "member", None),
            P("member", "tower", None),
            P("member", "tower", None),
            P(("tower", "member"), None),
            P(("tower", "member"), None),
            P("member", "tower"),
        ),
        check_vma=False,
    )
```

```python
import functools
import math

import jax
import jax.numpy as jnp
from jax import lax
from jax.experimental import pallas as pl
from jax.experimental.pallas import tpu as pltpu
from jax.sharding import PartitionSpec as P

MESH = pl.DeviceIdType.MESH
DECAY_RATE = 0.98
LEARN_RATE = 1.0
EPSILON = 1e-08
F32 = jnp.float32
BF16 = jnp.bfloat16
NN = (((1,), (0,)), ((), ()))
NT = (((1,), (1,)), ((), ()))


def split(x):
    hi = x.astype(BF16)
    return hi, (x - hi.astype(F32)).astype(BF16)


def dot1(a, b, dims=NN):
    return lax.dot_general(a, b, dims, preferred_element_type=F32)


def few3(a, b, dims=NN):
    (ah, al), (bh, bl) = a, b
    both = dot1(jnp.concatenate([ah, al], axis=0), bh, dims)
    m = ah.shape[0]
    return both[:m] + (both[m:] + dot1(ah, bl, dims))


def deep3(a, b, dims=NN):
    (ah, al), (bh, bl) = a, b
    return dot1(
        jnp.concatenate([ah, al, ah], axis=1),
        jnp.concatenate([bh, bh, bl], axis=dims[0][1][0]),
        dims,
    )


def sigmoid(x):
    return 1.0 / (1.0 + jnp.exp(-x))


def main_kernel(
    dims,
    bag_ref,
    touch_ref,
    elapsed_ref,
    tables_ref,
    first_hbm,
    second_hbm,
    lift_hbm,
    press_hbm,
    head_ref,
    label_ref,
    logits_out,
    decayed_out,
    gt_out,
    gf_out,
    gsec_out,
    glp_out,
    stage,
    w1h,
    w1l,
    w2f,
    w2h,
    w2l,
    lift,
    press,
    mixh,
    mixl,
    cols,
    counts_ref,
    pool,
    feats,
    tout_send,
    tout_recv,
    stats,
    rs_buf,
    line,
    line_buf,
    gath,
    errs,
    act,
    acth,
    actl,
    ghh,
    ghl,
    pth,
    ptl,
    gf,
    gf_in,
    gsec,
    gsec_in,
    gpool,
    gpool_in,
    glp,
    glp_in,
    load_sem,
    crit_send,
    mate_send,
    ag_send,
    relay_send,
    ag_recv,
    rs_send,
    rs_recv,
    to_send,
    to_recv,
    gm_send,
    gm_recv,
    gt_send,
    gt_recv,
    back_send,
    back_recv,
):
    n, nt = dims
    me = lax.axis_index("member")
    tpos = lax.axis_index("tower")
    towers, bags, total = bag_ref.shape
    width, rows = tables_ref.shape[1:]
    touches = touch_ref.shape[2]
    hid, outs = w2h.shape[1:]
    fin = w1h.shape[1]
    rank = lift.shape[1]
    flat = towers * outs
    chips = n // 2
    own = total // n
    half = own * chips
    piece = own // nt
    chunk = min(256, half)
    tile = min(256, hid)
    pair_hid = 2 * (hid // n)
    block_hid = hid // n
    pair_flat = flat // chips
    chip, core = me // 2, lax.rem(me, 2)
    mate = me + 1 - 2 * core

    loads = []

    def load(source, target):
        loads.append(pltpu.make_async_copy(source, target, load_sem.at[len(loads)]))
        loads[-1].start()

    for t in range(towers):
        load(first_hbm.at[:, t, :], stage.at[t, :fin])
    for t in range(towers):
        load(second_hbm.at[:, t, :], w2f.at[t])
    load(lift_hbm.at[pl.ds(tpos * flat, flat)], lift)
    load(press_hbm.at[pl.ds(tpos * flat, flat)], press)

    barrier = pltpu.get_barrier_semaphore()
    for d in range(1, n):
        pl.semaphore_signal(
            barrier, inc=1, device_id={"member": lax.rem(me + d, n)}, device_id_type=MESH
        )
    for d in range(1, nt):
        pl.semaphore_signal(
            barrier, inc=1, device_id={"tower": lax.rem(tpos + d, nt)}, device_id_type=MESH
        )

    def slice_at(index):
        return pl.ds(pl.multiple_of(index * own, own), own)

    stack = [bag_ref[t].astype(F32) for t in range(towers)]
    stack.append(jnp.zeros((128 - towers * bags, total), F32))
    cols[...] = jnp.concatenate(stack, axis=0).T
    stack = []
    for t in range(towers):
        stack.append(touch_ref[t].astype(F32))
        stack.append(jnp.exp(elapsed_ref[t].astype(F32) * math.log(DECAY_RATE)))
    stack.append(jnp.zeros((128 - 2 * towers, touches), F32))
    owed = jnp.concatenate(stack, axis=0).T
    pairs = []
    place = lax.broadcasted_iota(jnp.int32, (touches, rows), 1).astype(F32)
    for t in range(towers):
        ids, rates = owed[:, 2 * t : 2 * t + 1], owed[:, 2 * t + 1 : 2 * t + 2]
        chosen = jnp.sum(jnp.where(place == ids, rates, 0.0), axis=0, keepdims=True)
        value = tables_ref[t] * jnp.where(chosen > 0.0, chosen, 1.0)
        decayed_out[t] = value
        pairs.append(jnp.concatenate(split(value), axis=0))
    out = jnp.where(chip < chips // 2, -1, 1)
    near_end = (chip == 1) | (chip == chips - 2)

    def own_copy(there, k, s, semaphore):
        at = slice_at(s)
        return pltpu.make_async_remote_copy(
            src_ref=pool.at[k, at],
            dst_ref=feats.at[me, at],
            send_sem=semaphore,
            recv_sem=ag_recv.at[chip, s],
            device_id={"member": 2 * there + k},
            device_id_type=MESH,
        )

    def mate_copy():
        return pltpu.make_async_remote_copy(
            src_ref=pool.at[1 - core],
            dst_ref=feats.at[me],
            send_sem=mate_send.at[0],
            recv_sem=ag_recv.at[chip, 0],
            device_id={"member": mate},
            device_id_type=MESH,
        )

    def pair_copy(source, s, semaphore):
        pair, at = pl.ds(2 * source, 2), slice_at(s)
        return pltpu.make_async_remote_copy(
            src_ref=feats.at[pair, at],
            dst_ref=feats.at[pair, at],
            send_sem=semaphore,
            recv_sem=ag_recv.at[source, s],
            device_id={"member": 2 * lax.rem(chip + out + chips, chips) + core},
            device_id_type=MESH,
        )

    def slice_from(there, sign, j):
        return lax.rem(there + chips + sign * j, chips)

    def whole_copies(there, semaphore):
        towards = jnp.where(there < chips // 2, -1, 1)
        return [
            own_copy(there, k, slice_from(there, towards, j), semaphore)
            for j in range(chips - 1, 0, -1)
            for k in range(2)
        ]

    def end_each(act_on):
        @pl.when(near_end)
        def _():
            act_on(chip + out, ag_send.at[0, 0])

    def inner_each(hops, act_on):
        for sign in (-1, 1):
            for i in hops:
                there = chip + sign * out * i

                @pl.when((there > 0) & (there < chips - 1))
                def _():
                    act_on(there, ag_send.at[(1 + sign) // 2, i])

    def start_all(there, semaphore):
        for copy in whole_copies(there, semaphore):
            copy.start()

    def own_arrives(i):
        pair_copy(lax.rem(chip + i, chips), chip, relay_send.at[0]).wait_recv()

    def relay(d, part):
        @pl.when(near_end)
        def _():
            for j in part:
                copy = pair_copy(chip - out * d, slice_from(chip, out, j), relay_send.at[d - 1])
                if j:
                    copy.wait_recv()
                copy.start()

    def rest_arrives(i):
        source = lax.rem(chip + i, chips)
        pair_copy(source, slice_from(chip, out, 1), relay_send.at[0]).wait_recv()

        @pl.when(jnp.logical_not(near_end) | (source == chip + out))
        def _():
            for j in range(2, chips):
                pair_copy(source, slice_from(chip, out, j), relay_send.at[0]).wait_recv()

    order = sorted(range(1, chips), key=lambda i: -min(i, chips - i))
    place = lax.broadcasted_iota(jnp.int32, (2 * own, rows), 1).astype(F32)

    def count(there):
        span = pl.ds(pl.multiple_of(there * 2 * own, 2 * own), 2 * own)
        found = []
        for t in range(towers):
            counts = jnp.zeros((2 * own, rows), F32)
            for b in range(bags):
                k = t * bags + b
                counts = counts + jnp.where(place == cols[span, k : k + 1], 1.0, 0.0)
            counts = counts.astype(BF16)
            for k in range(2):
                counts_ref[t, k, slice_at(there), :] = counts[k * own : (k + 1) * own]
            found.append(counts)
        return found

    mirrored = jnp.where(chip < chips // 2, chip, chips - 1 - chip)
    stops = [chips // 2 + i for i in range(chips // 2)]
    stops += [lax.rem(mirrored + i, chips // 2) for i in range(1, chips // 2 + 1)]
    stops = [jnp.where(chip < chips // 2, stop, chips - 1 - stop) for stop in stops]
    found = count(stops[0])
    for i, there in enumerate(stops):
        both = [dot1(counts, pairs[t], NT) for t, counts in enumerate(found)]
        if i + 1 < chips:
            found = count(stops[i + 1])
        pooled = jnp.concatenate([x[:, :width] + x[:, width:] for x in both], axis=1)
        for k in range(2):
            pool[k, slice_at(there), :] = pooled[k * own : (k + 1) * own]
        if i == 0:
            pl.semaphore_wait(barrier, n - 1 + nt - 1)
        if i + 1 < chips:
            for k in range(2):
                own_copy(there, k, there, crit_send.at[0]).start()

        @pl.when(near_end & (there != chip + out))
        def _():
            for k in range(2):
                own_copy(chip + out, k, there, ag_send.at[0, 0]).start()

    mate_copy().start()
    feats[me] = pool[core]

    for copy in loads[:towers]:
        copy.wait()
    for t in range(towers):

        @pl.loop(0, fin // 64)
        def _(i):
            span = pl.ds(pl.multiple_of(i * 64, 64), 64)
            w1h[t, span, :], w1l[t, span, :] = split(stage[t, span, :])

    inner_each([1], start_all)
    for copy in loads[towers:]:
        copy.wait()
    for t in range(towers):

        @pl.loop(0, hid // 128)
        def _(i):
            span = pl.ds(pl.multiple_of(i * 128, 128), 128)
            w2h[t, span, :], w2l[t, span, :] = split(w2f[t, span, :])

    head = head_ref[:, pl.ds(pl.multiple_of(tpos * flat, flat), flat)]
    mixh[...], mixl[...] = split(jnp.concatenate([lift[...].T * head, press[...].T], axis=0))

    mate_copy().wait_recv()
    for i in range(1, chips):
        own_arrives(i)
    inner_each(range(2, chips - 1), start_all)
    for d in range(1, chips - 1):
        relay(d, [0])
    flat_out = []
    for t in range(towers):
        part = slice(t * width, (t + 1) * width)
        x = jnp.concatenate([feats[b, slice_at(chip), part] for b in range(n)], axis=1)
        h = few3(split(x), (w1h[t], w1l[t]))
        flat_out.append(few3(split(h * sigmoid(h)), (w2h[t], w2l[t])))
    flat_out = jnp.concatenate(flat_out, axis=1)
    stats[...] = few3(split(flat_out), (mixh[...], mixl[...]), NT).reshape(nt, piece, 2 * rank)
    linear = jnp.sum(flat_out * head, axis=1, keepdims=True)
    seat = lax.broadcasted_iota(jnp.int32, (piece, rank), 1)
    wanted = lax.broadcasted_iota(jnp.int32, (piece, rank), 0)
    for k in range(nt):
        row = jnp.where(seat == wanted, linear[k * piece : (k + 1) * piece], 0.0)
        line[k] = jnp.sum(row, axis=0, keepdims=True)

    def tower_copies(d):
        other = lax.rem(tpos + d, nt)
        return [
            pltpu.make_async_remote_copy(
                src_ref=ref.at[other],
                dst_ref=buf.at[tpos],
                send_sem=rs_send.at[k],
                recv_sem=rs_recv.at[k, d - 1],
                device_id={"tower": other},
                device_id_type=MESH,
            )
            for k, (ref, buf) in enumerate(((line, line_buf), (stats, rs_buf)))
        ]

    for d in range(1, nt):
        for copy in tower_copies(d):
            copy.start()

    for c in range(chips):
        tout_send[c] = flat_out[:, c * pair_flat : (c + 1) * pair_flat]
    tout_recv[chip] = tout_send[chip]

    def tout_copy(i):
        there = lax.rem(chip + i, chips)
        return pltpu.make_async_remote_copy(
            src_ref=tout_send.at[there],
            dst_ref=tout_recv.at[chip],
            send_sem=to_send.at[0],
            recv_sem=to_recv.at[i - 1],
            device_id={"member": 2 * there + core},
            device_id_type=MESH,
        )

    def member_copies(i, there):
        return [
            pltpu.make_async_remote_copy(
                src_ref=ref.at[chip, tpos],
                dst_ref=ref.at[chip, tpos],
                send_sem=gm_send.at[k],
                recv_sem=gm_recv.at[k, i - 1],
                device_id={"member": 2 * there + core},
                device_id_type=MESH,
            )
            for k, ref in enumerate((errs, gath))
        ]

    def column_copies(d, source, count):
        where = pl.ds(source, count)
        return [
            pltpu.make_async_remote_copy(
                src_ref=ref.at[where, tpos],
                dst_ref=ref.at[where, tpos],
                send_sem=gt_send.at[k],
                recv_sem=gt_recv.at[k, d - 1],
                device_id={"tower": lax.rem(tpos + d, nt)},
                device_id_type=MESH,
            )
            for k, ref in enumerate((errs, gath))
        ]

    def column_start(source):
        for d in range(1, nt):
            for copy in column_copies(d, source, 1):
                copy.start()

    relay(1, range(chips - 1, 1, -1))
    beside = 1 - 2 * lax.rem(chip, 2)
    rest_arrives(beside + chips)
    per = 4
    together = per * width

    def hidden_group(t, c, g):
        part = slice(t * width, (t + 1) * width)
        span = slice(c * chunk, (c + 1) * chunk)
        x = jnp.concatenate([feats[per * g + k, span, part] for k in range(per)], axis=1)
        x = split(x)
        ins = pl.ds(pl.multiple_of(g * together, together), together)
        for k in range(hid // tile):
            lanes = slice(k * tile, (k + 1) * tile)
            yield lanes, deep3(x, (w1h[t, ins, lanes], w1l[t, ins, lanes]))

    near = chip // 2
    for t in range(towers):
        for c in range(half // chunk):
            span = slice(c * chunk, (c + 1) * chunk)
            for lanes, value in hidden_group(t, c, near):
                stage[t, span, lanes] = value

    for d in range(1, nt):
        for copy in tower_copies(d):
            copy.wait_recv()
    summed, linear = stats[tpos], line[tpos]
    for d in range(1, nt):
        summed = summed + rs_buf[lax.rem(tpos + d, nt)]
        linear = linear + line_buf[lax.rem(tpos + d, nt)]
    scaled, projected = summed[:, :rank], summed[:, rank:]
    linear = jnp.sum(jnp.where(seat == wanted, linear, 0.0), axis=1, keepdims=True)
    logit = jnp.sum(projected * scaled, axis=1, keepdims=True) + linear
    logit = jnp.broadcast_to(logit, (piece, rank))
    logits_out[...] = logit
    place = lax.broadcasted_iota(jnp.int32, (piece, own), 1)
    mine = lax.broadcasted_iota(jnp.int32, (piece, own), 0) + tpos * piece
    clicks = jnp.where(place == mine, label_ref[...].astype(F32), 0.0)
    error = sigmoid(logit) - jnp.sum(clicks, axis=1, keepdims=True)
    gath[chip, tpos, :, :rank] = error * projected
    gath[chip, tpos, :, rank:] = error * scaled
    errs[chip, tpos] = jnp.sum(jnp.where(seat == wanted, error, 0.0), axis=0, keepdims=True)
    for i in order:
        for copy in member_copies(i, lax.rem(chip + i, chips)):
            copy.start()
    column_start(chip)

    for d in range(2, chips - 1):
        relay(d, range(chips - 1, 1, -1))
    for source in sorted(range(chips), key=lambda c: -min(c, chips - 1 - c)):

        @pl.when(chip != source)
        def _():
            for copy in member_copies(lax.rem(chip + chips - source, chips), source):
                copy.wait_recv()
            column_start(source)

    for i in range(1, chips):
        pl.when(lax.rem(chip + i, chips) != chip + beside)(functools.partial(rest_arrives, i))

    start = pl.multiple_of(chip * pair_hid, pair_hid)
    groups = n // per
    for t in range(towers):
        part = slice(t * width, (t + 1) * width)
        for c in range(half // chunk):
            span = slice(c * chunk, (c + 1) * chunk)
            for i in range(1, groups):
                for lanes, value in hidden_group(t, c, lax.rem(near + i, groups)):
                    h = stage[t, span, lanes] + value
                    if i < groups - 1:
                        stage[t, span, lanes] = h
                    else:
                        sig = sigmoid(h)
                        a = h * sig
                        act[span, lanes] = a
                        stage[t, span, lanes] = sig + a * (1.0 - sig)
            both = jnp.concatenate([feats[2 * chip + k, span, part] for k in range(2)], axis=1)
            pth[t, :, span], ptl[t, :, span] = split(both.T)
            acth[t, :, span], actl[t, :, span] = split(act[span, pl.ds(start, pair_hid)].T)

    def sent(ref, semaphore):
        pltpu.make_async_remote_copy(
            src_ref=ref,
            dst_ref=ref,
            send_sem=semaphore,
            recv_sem=ag_recv.at[0, 0],
            device_id={"member": mate},
            device_id_type=MESH,
        ).wait_send()

    sent(pool.at[0], mate_send.at[0])
    for k, ref in enumerate((line, stats)):
        sent(ref.at[: nt - 1], rs_send.at[k])
    sent(feats.at[:2, : half - own], crit_send.at[0])
    def sent_all(there, semaphore):
        sent(pool.at[:, : half - own], semaphore)

    end_each(sent_all)
    inner_each(range(1, chips - 1), sent_all)

    @pl.when(near_end)
    def _():
        for d in range(1, chips - 1):
            sent(feats.at[:2, : half - own], relay_send.at[d - 1])

    for i in order:
        tout_copy(i).start()
    for d in range(1, nt):
        for copy in column_copies(d, 0, chips):
            copy.wait_recv()
    for k, ref in enumerate((errs, gath)):
        sent(ref.at[: chips - 1, 0], gm_send.at[k])
        sent(ref.at[:, : nt - 1], gt_send.at[k])

    def back_copy(slot, source, target):
        return pltpu.make_async_remote_copy(
            src_ref=source,
            dst_ref=target,
            send_sem=back_send.at[slot],
            recv_sem=back_recv.at[slot],
            device_id={"member": mate},
            device_id_type=MESH,
        )

    def rows_of(which, size):
        return pl.ds(pl.multiple_of(which * size, size), size)

    def back_copies(t):
        return [
            back_copy(3 * t, gpool.at[t, rows_of(1 - core, width)], gpool_in.at[t]),
            back_copy(3 * t + 1, gf.at[t, rows_of(1 - core, width)], gf_in.at[t]),
            back_copy(3 * t + 2, gsec.at[t, rows_of(1 - core, block_hid)], gsec_in.at[t]),
        ]

    def lift_copy():
        return back_copy(3 * towers, glp.at[rows_of(1 - core, pair_flat // 2)], glp_in)

    def put(ref, index, value, fresh):
        if fresh:
            ref[index] = value
        else:
            ref[index] += value

    errors = jnp.concatenate(
        [
            jnp.broadcast_to(errs[c, t], (piece, rank))
            for c in range(chips)
            for t in range(nt)
        ],
        axis=0,
    )
    seat = lax.broadcasted_iota(jnp.int32, (half, rank), 1)
    wanted = lax.rem(lax.broadcasted_iota(jnp.int32, (half, rank), 0), piece)
    errors = jnp.sum(jnp.where(seat == wanted, errors, 0.0), axis=1, keepdims=True)
    pair_rows = pl.ds(pl.multiple_of(chip * 2 * width, 2 * width), 2 * width)
    for t in range(towers):
        part = slice(t * outs, (t + 1) * outs)
        for c in range(half // chunk):
            span = slice(c * chunk, (c + 1) * chunk)
            here = slice(c * (chunk // own), (c + 1) * (chunk // own))
            block = gath[here].reshape(chunk, 2 * rank)
            go = split(
                errors[span] * head[:, part]
                + deep3(split(block), (mixh[:, part], mixl[:, part]))
            )
            for k in range(hid // tile):
                lanes = slice(k * tile, (k + 1) * tile)
                grad_act = deep3(go, (w2h[t, lanes, :], w2l[t, lanes, :]), NT)
                grad_hidden = split(grad_act * stage[t, span, lanes])
                ghh[:, lanes], ghl[:, lanes] = grad_hidden
            value = few3((pth[t, :, span], ptl[t, :, span]), (ghh[...], ghl[...]))
            put(gf, (t,), value, c == 0)
            first = (w1h[t, pair_rows, :], w1l[t, pair_rows, :])
            gpool[t, :, span] = few3(first, (ghh[...], ghl[...]), NT)
            put(gsec, (t,), deep3((acth[t, :, span], actl[t, :, span]), go), c == 0)
        for copy in back_copies(t):
            copy.start()

    for i in order:
        tout_copy(i).wait_recv()
    sent(tout_send.at[: chips - 1], to_send.at[0])
    outputs = jnp.concatenate([tout_recv[c] for c in range(chips)], axis=0)
    block = gath[...].reshape(half, 2 * rank)
    value = deep3(split(outputs.T), split(block))
    seat = lax.broadcasted_iota(jnp.int32, (pair_flat, flat), 1)
    wanted = lax.broadcasted_iota(jnp.int32, (pair_flat, flat), 0) + chip * pair_flat
    weights = jnp.sum(jnp.where(seat == wanted, head, 0.0), axis=1, keepdims=True)
    glp[:, :rank] = weights * value[:, :rank]
    glp[:, rank:] = value[:, rank:]
    lift_copy().start()

    for t in range(towers):
        from_mate = back_copies(t)
        mine = jnp.concatenate(split(gpool[t, rows_of(core, width), :]), axis=0)
        both = dot1(mine, counts_ref[t, core])
        from_mate[0].wait_recv()
        theirs = jnp.concatenate(split(gpool_in[t]), axis=0)
        both = both + dot1(theirs, counts_ref[t, 1 - core])
        gt_out[t] = both[:width] + both[width:]
        from_mate[1].wait_recv()
        gf_out[t] = gf_in[t] + gf[t, rows_of(core, width), :]
        from_mate[2].wait_recv()
        gsec_out[t] = gsec_in[t] + gsec[t, rows_of(core, block_hid), :]
    lift_copy().wait_recv()
    glp_out[...] = glp_in[...] + glp[rows_of(core, pair_flat // 2), :]

    for t in range(towers):
        for copy in back_copies(t):
            copy.wait_send()
    lift_copy().wait_send()


def final_kernel(
    logits_ref,
    decayed_ref,
    gt_ref,
    gf_ref,
    gsec_ref,
    glp_ref,
    acc_ref,
    new_tables_ref,
    new_acc_ref,
    grad_first_ref,
    grad_second_ref,
    grad_lift_ref,
    grad_press_ref,
    logits_out_ref,
):
    rank = logits_ref.shape[1]
    for t in range(gt_ref.shape[0]):
        grad_second_ref[:, t, :] = gsec_ref[t]
        grad_first_ref[:, t, :] = gf_ref[t]
        g = gt_ref[t]
        value = acc_ref[t] + jnp.mean(g * g, axis=0, keepdims=True)
        new_acc_ref[t] = value
        new_tables_ref[t] = decayed_ref[t] - LEARN_RATE * g / (jnp.sqrt(value) + EPSILON)
    grad_lift_ref[...] = glp_ref[:, :rank]
    grad_press_ref[...] = glp_ref[:, rank:]
    piece = logits_ref.shape[0]
    place = lax.broadcasted_iota(jnp.int32, (piece, piece), 1)
    wanted = lax.broadcasted_iota(jnp.int32, (piece, piece), 0)
    values = jnp.where(place == wanted, logits_ref[:, :1], 0.0)
    logits_out_ref[...] = jnp.sum(values, axis=0, keepdims=True)


def per_device(n, nt, *args):
    bag_ids, touch_ids, elapsed, tables, accumulator, first, second, lift, press, head, labels = args
    towers, _, bags, total = bag_ids.shape
    rows, width = tables.shape[2:]
    fin, _, hid = first.shape
    outs = second.shape[2]
    rank = lift.shape[1]
    flat = towers * outs
    chips = n // 2
    own = total // n
    half = own * chips
    piece = own // nt
    block_hid = hid // n
    pair_flat = flat // chips
    lanes = towers * width
    vmem = pl.BlockSpec(memory_space=pltpu.VMEM)
    anys = pl.BlockSpec(memory_space=pl.ANY)
    sem = pltpu.SemaphoreType.DMA
    shape = jax.ShapeDtypeStruct
    between = pl.pallas_call(
        functools.partial(main_kernel, (n, nt)),
        out_shape=(
            pltpu.VMEM((piece, rank), F32),
            pltpu.VMEM((towers, width, rows), F32),
            pltpu.VMEM((towers, width, rows), F32),
            pltpu.VMEM((towers, width, hid), F32),
            pltpu.VMEM((towers, block_hid, outs), F32),
            pltpu.VMEM((pair_flat // 2, 2 * rank), F32),
        ),
        in_specs=[vmem] * 4 + [anys] * 4 + [vmem] * 2,
        out_specs=[vmem] * 6,
        scratch_shapes=[
            pltpu.VMEM((towers, max(half, fin), hid), F32),
            pltpu.VMEM((towers, fin, hid), BF16),
            pltpu.VMEM((towers, fin, hid), BF16),
            pltpu.VMEM((towers, hid, outs), F32),
            pltpu.VMEM((towers, hid, outs), BF16),
            pltpu.VMEM((towers, hid, outs), BF16),
            pltpu.VMEM((flat, rank), F32),
            pltpu.VMEM((flat, rank), F32),
            pltpu.VMEM((2 * rank, flat), BF16),
            pltpu.VMEM((2 * rank, flat), BF16),
            pltpu.VMEM((total, 128), F32),
            pltpu.VMEM((towers, 2, half, rows), BF16),
            pltpu.VMEM((2, half, lanes), F32),
            pltpu.VMEM((n, half, lanes), F32),
            pltpu.VMEM((chips, own, pair_flat), F32),
            pltpu.VMEM((chips, own, pair_flat), F32),
            pltpu.VMEM((nt, piece, 2 * rank), F32),
            pltpu.VMEM((nt, piece, 2 * rank), F32),
            pltpu.VMEM((nt, 1, rank), F32),
            pltpu.VMEM((nt, 1, rank), F32),
            pltpu.VMEM((chips, nt, piece, 2 * rank), F32),
            pltpu.VMEM((chips, nt, 1, rank), F32),
            pltpu.VMEM((half, hid), F32),
            pltpu.VMEM((towers, 2 * block_hid, half), BF16),
            pltpu.VMEM((towers, 2 * block_hid, half), BF16),
            pltpu.VMEM((min(256, half), hid), BF16),
            pltpu.VMEM((min(256, half), hid), BF16),
            pltpu.VMEM((towers, 2 * width, half), BF16),
            pltpu.VMEM((towers, 2 * width, half), BF16),
            pltpu.VMEM((towers, 2 * width, hid), F32),
            pltpu.VMEM((towers, width, hid), F32),
            pltpu.VMEM((towers, 2 * block_hid, outs), F32),
            pltpu.VMEM((towers, block_hid, outs), F32),
            pltpu.VMEM((towers, 2 * width, half), F32),
            pltpu.VMEM((towers, width, half), F32),
            pltpu.VMEM((pair_flat, 2 * rank), F32),
            pltpu.VMEM((pair_flat // 2, 2 * rank), F32),
            sem((2 * towers + 2,)),
            sem((1,)),
            sem((1,)),
            sem((2, chips - 1)),
            sem((chips - 2,)),
            sem((chips, chips)),
            sem((2,)),
            sem((2, nt - 1)),
            sem((1,)),
            sem((chips - 1,)),
            sem((2,)),
            sem((2, chips - 1)),
            sem((2,)),
            sem((2, nt - 1)),
            sem((3 * towers + 1,)),
            sem((3 * towers + 1,)),
        ],
        compiler_params=pltpu.CompilerParams(
            collective_id=0, has_side_effects=True, vmem_limit_bytes=64 * 10**6
        ),
    )(
        bag_ids[:, 0],
        touch_ids,
        elapsed,
        jnp.transpose(tables[:, 0], (0, 2, 1)),
        first,
        second,
        lift,
        press,
        head[None, :],
        labels,
    )
    out = pl.pallas_call(
        final_kernel,
        out_shape=(
            shape((towers, width, rows), F32),
            shape((towers, 1, rows), F32),
            shape((width, towers, hid), F32),
            shape((block_hid, towers, outs), F32),
            shape((flat // n, rank), F32),
            shape((flat // n, rank), F32),
            shape((1, piece), F32),
        ),
        in_specs=[vmem] * 7,
        out_specs=[vmem] * 7,
        compiler_params=pltpu.CompilerParams(vmem_limit_bytes=8 * 2**20),
    )(*(pltpu.with_memory_space_constraint(x, pltpu.VMEM) for x in between), accumulator)
    new_tables, new_acc, grad_first, grad_second, grad_lift, grad_press, logits = out
    return (
        jnp.transpose(new_tables, (0, 2, 1))[:, None],
        new_acc,
        grad_first,
        grad_second,
        grad_lift,
        grad_press,
        logits,
    )


def solution(mesh):
    placed = (
        P("tower", "member", None, None),
        P("tower", "member", None),
        P("tower", "member", None),
        P("tower", "member", None, None),
        P("tower", "member", None),
        P(None, "tower", None),
        P(None, "tower", None),
        P(),
        P(),
        P(),
        P("member", None),
    )
    return jax.shard_map(
        functools.partial(per_device, mesh.shape["member"], mesh.shape["tower"]),
        mesh=mesh,
        in_specs=placed,
        out_specs=(
            P("tower", "member", None, None),
            P("tower", "member", None),
            P("member", "tower", None),
            P("member", "tower", None),
            P(("tower", "member"), None),
            P(("tower", "member"), None),
            P("member", "tower"),
        ),
        check_vma=False,
    )
```
